32 devices in a mesh: dp: 16 (over z, y, core), mp: 2 (over x).
Axes of the slice: x: 2, y: 2, z: 4, core: 2. Of those that a mesh axis runs over, the one named last changes fastest.
Arguments:
- tokens: bfloat16 [32768, 1280], P(('dp', 'mp')), may hold values from -6 to 6
- norm_gains: float32 [2, 1280], replicated, may hold values from 0.5 to 1.5
- attn_in: bfloat16 [3, 1280, 1280], P(None, None, 'mp'), may hold values from -0.15625 to 0.15625
- attn_out: bfloat16 [1280, 1280], P('mp'), may hold values from -0.5 to 0.5
- mlp_in: bfloat16 [2, 1280, 5120], P(None, None, 'mp'), may hold values from -0.15625 to 0.15625
- mlp_out: bfloat16 [5120, 1280], P('mp'), may hold values from -0.078125 to 0.078125
- lengths: int32 [16, 48], P('dp'), may hold values from 1 to 1024, 2048 in all within a row
- out_grad: bfloat16 [32768, 1280], P(('dp', 'mp')), may hold values from -6 to 6
Outputs:
- output: bfloat16 [32768, 1280], P(('dp', 'mp'))
- grad_tokens: bfloat16 [32768, 1280], P(('dp', 'mp'))
- grad_gains: float32 [2, 1280], P(None, ('dp', 'mp'))
- grad_attn_in: float32 [3, 1280, 1280], P(None, 'dp', 'mp')
- grad_attn_out: float32 [1280, 1280], P('mp', 'dp')
- grad_mlp_in: float32 [2, 1280, 5120], P(None, 'dp', 'mp')
- grad_mlp_out: float32 [5120, 1280], P('mp', 'dp')
The draws below stay inside these ranges and needn't reach their ends.
Inputs may be any that keep to these rules, and one draw needn't show every extreme that they name: `lengths`: each row lists the patch counts of the 48 series packed in order into one bucket; a row sums to 2048 and its largest entry is exactly 1024.
All inputs are finite; a program needn't handle non-finite values.
Results may differ from the reference program's by a relative error of at most 0.023.
Values may be sent and summed in bfloat16 or wider, within the bound.
No kernel may reach another device: no remote copies, remote signals or barrier semaphores. Data moves between devices by JAX's collectives and lax.ppermute only.
A program may use at most 320 MiB of HBM per device.

```python
import math
import jax
import jax.numpy as jnp
import numpy as np
from jax import lax

MODEL_DIM = 1280
HEAD_COUNT = 16
HEAD_DIM = 80
HIDDEN_SIZE = 5120
BUCKET = 2048
LONGEST = 1024
SERIES = 48
QUERY_ROWS = 512
TOKENS = 32768
N_DP = 16


def steps_of(key, shape, split, low, top_value):
    gain = 1.0
    for axis_at, blocks in split:
        steps = jax.random.uniform(jax.random.fold_in(jax.random.fold_in(key, 6), axis_at), (blocks,), jnp.float32, low / len(split), top_value / len(split))
        gain = gain * jnp.repeat(jnp.exp(steps), shape[axis_at] // blocks).reshape((-1,) + (1,) * (len(shape) - 1 - axis_at))
    return gain


def length_profile(number_of, total, limit, skew):
    weights = [(1 << 20) // math.isqrt(grade ** skew) + 1 for grade in range(2, number_of + 1)]
    rest, given = total - limit - (number_of - 1), [1] * (number_of - 1)
    while rest > 0:
        free = [i for i in range(number_of - 1) if given[i] < limit]
        mass, left = sum([weights[i] for i in free]), rest
        for i in free:
            extra = min(limit - given[i], max(1, left * weights[i] // mass), rest)
            given[i] = given[i] + extra
            rest = rest - extra
    return np.array([limit] + given)


def ragged(key, number_of, total, reach, slope):
    if number_of == 2:
        one = jax.random.randint(key, (), max(1, total - reach), min(reach, total - 1) + 1)
        return jnp.stack([one, total - one])
    tallies = jnp.asarray(length_profile(number_of, total, reach, slope), jnp.int32)
    pairs = (number_of - 1) // 2
    donor, taker = tallies[1:1 + 2 * pairs:2], tallies[2:2 + 2 * pairs:2]
    margin = jnp.minimum(donor - 1, reach - taker)
    shifted = jax.random.randint(jax.random.fold_in(key, 1), (pairs,), 0, 1 << 20) % (margin + 1)
    tallies = tallies.at[1:1 + 2 * pairs:2].set(donor - shifted).at[2:2 + 2 * pairs:2].set(taker + shifted)
    return tallies[jax.random.permutation(jax.random.fold_in(key, 2), number_of)]


def centred(key, dims, width, most, pieces=(), held_as=jnp.bfloat16):
    drawn = width * jax.random.normal(key, dims, jnp.float32)
    if pieces:
        drawn = drawn * steps_of(key, dims, pieces, -0.22, 0.18)
    return jnp.clip(drawn, -most, most).astype(held_as)


def setup_inputs(seed: int = 0) -> dict:
    key_list = jax.random.split(jax.random.key(seed), 9)
    return {
        "tokens": centred(key_list[0], (TOKENS, MODEL_DIM), 1.0, 6.0, ((0, 32),)),
        "norm_gains": jnp.clip(1.0 + 0.1 * jax.random.normal(key_list[1], (2, MODEL_DIM), jnp.float32), 0.5, 1.5),
        "attn_in": centred(key_list[2], (3, MODEL_DIM, HEAD_COUNT * HEAD_DIM), MODEL_DIM ** -0.5, 0.15625, ((2, 2),)),
        "attn_out": centred(key_list[3], (HEAD_COUNT * HEAD_DIM, MODEL_DIM), (HEAD_COUNT * HEAD_DIM // 8) ** -0.5, 0.5, ((0, 2),)),
        "mlp_in": centred(key_list[4], (2, MODEL_DIM, HIDDEN_SIZE), MODEL_DIM ** -0.5, 0.15625, ((2, 2),)),
        "mlp_out": centred(key_list[5], (HIDDEN_SIZE, MODEL_DIM), HIDDEN_SIZE ** -0.5, 0.078125, ((0, 2),)),
        "lengths": jax.vmap(lambda own: ragged(own, SERIES, BUCKET, LONGEST, 2))(jax.random.split(key_list[6], N_DP)).reshape((N_DP, SERIES)).astype(jnp.int32),
        "out_grad": centred(key_list[7], (TOKENS, MODEL_DIM), 1.0, 6.0, ((0, 32),)),
    }


@jax.custom_vjp
def low(v):
    return lax.optimization_barrier(v.astype(jnp.bfloat16)).astype(jnp.float32)

@jax.custom_vjp
def low_back(v):
    return v

def low_keep(v):
    return (low(v), None)

def low_pass(kept, grad):
    return (grad,)

def back_keep(v):
    return (v, None)

def back_low(kept, grad):
    return (low(grad),)
low.defvjp(low_keep, low_pass)
low_back.defvjp(back_keep, back_low)
EPSILON = 1e-06
NEGATIVE = -1e+30
HIGHEST = lax.Precision.HIGHEST

def layout(lengths_row):
    series_ends = jnp.cumsum(lengths_row, dtype=jnp.int32)
    places = jnp.arange(BUCKET, dtype=jnp.int32)
    before = series_ends[None, :] <= places[:, None]
    segment = lax.optimization_barrier(jnp.sum(before.astype(jnp.int32), axis=1, dtype=jnp.int32))
    starts = lax.optimization_barrier(jnp.sum(jnp.where(before, lengths_row[None, :], 0), axis=1, dtype=jnp.int32))
    return (segment, places, places - starts)

def turning(position):
    half_dim = HEAD_DIM // 2
    frequency = 10000.0 ** (-(jnp.arange(half_dim, dtype=jnp.float32) * 2.0 / HEAD_DIM))
    angles = position.astype(jnp.float32)[:, None] * frequency[None, :]
    return (jnp.cos(angles)[:, None, :], jnp.sin(angles)[:, None, :])

def rotate(values, cos_part, sine_part):
    half_dim = values.shape[-1] // 2
    first_half = values[..., :half_dim]
    second_half = values[..., half_dim:]
    return jnp.concatenate([first_half * cos_part - second_half * sine_part, second_half * cos_part + first_half * sine_part], axis=-1)

def rms_scaled(values, gain_row):
    inverse = lax.rsqrt(lax.optimization_barrier(jnp.mean(values * values, axis=-1, keepdims=True)) + EPSILON)
    return values * inverse * gain_row

def layer_forward(inputs, norm_gains, attn_in, attn_out, mlp_in, mlp_out, segment, places, cos_part, sine_part):
    normed_one = low(rms_scaled(inputs, norm_gains[0]))
    projected = low_back(jnp.einsum('nd,jdc->jnc', normed_one, attn_in, precision=HIGHEST))
    shaped = projected.reshape(3, BUCKET, HEAD_COUNT, HEAD_DIM)
    queries = low(rotate(shaped[0], cos_part, sine_part))
    keys_rot = low(rotate(shaped[1], cos_part, sine_part))
    value_rows = low(shaped[2])
    scaling = HEAD_DIM ** (-0.5)

    def attend_block(block_index):
        first_row = block_index * QUERY_ROWS
        query_block = lax.dynamic_slice_in_dim(queries, first_row, QUERY_ROWS, 0)
        seg_block = lax.dynamic_slice_in_dim(segment, first_row, QUERY_ROWS, 0)
        place_block = lax.dynamic_slice_in_dim(places, first_row, QUERY_ROWS, 0)
        allowed = (seg_block[:, None] == segment[None, :]) & (places[None, :] <= place_block[:, None])
        scores = low_back(jnp.einsum('qhd,khd->hqk', query_block, keys_rot, precision=HIGHEST) * scaling)
        scores = jnp.where(allowed[None], scores, NEGATIVE)
        weights = low(jax.nn.softmax(scores, axis=-1))
        return low(low_back(jnp.einsum('hqk,khd->qhd', weights, value_rows, precision=HIGHEST)))
    mixed_heads = lax.map(jax.checkpoint(attend_block), jnp.arange(BUCKET // QUERY_ROWS, dtype=jnp.int32))
    attended = mixed_heads.reshape(BUCKET, HEAD_COUNT * HEAD_DIM)
    middle = inputs + low_back(jnp.dot(attended, attn_out, precision=HIGHEST))
    normed_two = low(rms_scaled(middle, norm_gains[1]))
    gate_up = low_back(jnp.einsum('nd,jdf->jnf', normed_two, mlp_in, precision=HIGHEST))
    activated = low(jax.nn.silu(gate_up[0]) * gate_up[1])
    return middle + jnp.dot(activated, mlp_out, precision=HIGHEST)

def reference(tokens, norm_gains, attn_in, attn_out, mlp_in, mlp_out, lengths, out_grad):
    params = (norm_gains.astype(jnp.float32), attn_in.astype(jnp.float32), attn_out.astype(jnp.float32), mlp_in.astype(jnp.float32), mlp_out.astype(jnp.float32))
    inputs = tokens.astype(jnp.float32).reshape(N_DP, BUCKET, MODEL_DIM)
    cotangent = out_grad.astype(jnp.float32).reshape(N_DP, BUCKET, MODEL_DIM)

    def per_bucket(totals, bucket_item):
        bucket_in, bucket_cot, lengths_row = bucket_item
        segment, places, position = layout(lengths_row)
        cos_part, sine_part = turning(position)

        def forward(values, *weights):
            return layer_forward(values, *weights, segment, places, cos_part, sine_part)
        result, pullback = jax.vjp(forward, bucket_in, *params)
        gradients = pullback(bucket_cot)
        totals = tuple((running + fresh for running, fresh in zip(totals, gradients[1:])))
        return (totals, (result.astype(jnp.bfloat16), gradients[0].astype(jnp.bfloat16)))
    starting = tuple((jnp.zeros(param.shape, jnp.float32) for param in params))
    totals, (outputs, input_grads) = lax.scan(per_bucket, starting, (inputs, cotangent, lengths))
    return (outputs.reshape(TOKENS, MODEL_DIM), input_grads.reshape(TOKENS, MODEL_DIM), totals[0], totals[1], totals[2], totals[3], totals[4])
```

```python
import jax, jax.numpy as jnp, functools
from jax import lax
from jax.experimental import pallas as pl
from jax.experimental.pallas import tpu as pltpu
from jax.sharding import PartitionSpec as P

BLK = 256
LANES = 128
LOG2E = 1.4426950408889634
NEG = -1e30
bf16 = jnp.bfloat16
f32 = jnp.float32
NT = (((1,), (1,)), ((), ()))
NN = (((1,), (0,)), ((), ()))


def dot(a, b, dims=NN):
    return lax.dot_general(a, b, dims, preferred_element_type=f32)


def allowed_mask(j, i, start_row, blk):
    kpos = j * blk + lax.broadcasted_iota(jnp.int32, (blk, blk), 0)
    qpos = i * blk + lax.broadcasted_iota(jnp.int32, (blk, blk), 1)
    return (kpos >= start_row) & (kpos <= qpos)


def attn_fwd_kernel(first_ref, q_ref, k_ref, v_ref, start_ref, o_ref, lse_ref, vt_ref, acc_ref, m_ref, l_ref, *, blk, hd, scale):
    heads = k_ref.shape[0]
    nk = k_ref.shape[1] // blk
    base = first_ref[nk]
    i = base + pl.program_id(0)

    @pl.when(pl.program_id(0) == 0)
    def _():
        def body(h, c):
            for t in range(nk):
                vt_ref[h, :, t * blk : (t + 1) * blk] = v_ref[h, t * blk : (t + 1) * blk, :].T
            return c
        lax.fori_loop(0, heads, body, 0)

    acc_ref[...] = jnp.zeros_like(acc_ref)
    m_ref[...] = jnp.full_like(m_ref, NEG)
    l_ref[...] = jnp.zeros_like(l_ref)
    c2 = scale * LOG2E

    def step(j, carry):
        mask = allowed_mask(j, i, start_ref[0], blk)
        rows = pl.ds(pl.multiple_of(j * blk, blk), blk)
        for h in range(heads):
            s = dot(k_ref[h, rows, :], q_ref[h], NT)
            s = jnp.where(mask, s * c2, NEG)
            m_old = m_ref[h : h + 1]
            m_new = jnp.maximum(m_old, jnp.max(s, axis=0, keepdims=True))
            alpha = jnp.exp2(m_old - m_new)
            p = jnp.exp2(s - m_new)
            l_ref[h : h + 1] = alpha * l_ref[h : h + 1] + jnp.sum(p, axis=0, keepdims=True)
            m_ref[h : h + 1] = m_new
            part = slice(h * hd, (h + 1) * hd)
            acc_ref[part, :] = alpha * acc_ref[part, :] + dot(vt_ref[h, :hd, rows], p.astype(bf16))
        return carry

    step(i, 0)
    lax.fori_loop(first_ref[i], i, step, 0)
    for h in range(heads):
        part = slice(h * hd, (h + 1) * hd)
        acc_ref[part, :] = acc_ref[part, :] / l_ref[h : h + 1]
    o_ref[...] = acc_ref[...].T.astype(bf16)
    lse_ref[...] = m_ref[...] + jnp.log2(l_ref[...])


def attention_forward(first, base, q3, k3, v3, start_row, hd, scale, nq, blk=BLK):
    heads, rows, lanes = k3.shape
    table = jnp.concatenate([first, jnp.reshape(base, (1,))]).astype(jnp.int32)
    nk = rows // blk
    return pl.pallas_call(
        functools.partial(attn_fwd_kernel, blk=blk, hd=hd, scale=scale),
        grid_spec=pltpu.PrefetchScalarGridSpec(
            num_scalar_prefetch=1,
            grid=(nq,),
            in_specs=[
                pl.BlockSpec((heads, blk, lanes), lambda i, t: (0, i + t[nk], 0)),
                pl.BlockSpec((heads, rows, lanes), lambda i, t: (0, 0, 0), pipeline_mode=pl.Buffered(1)),
                pl.BlockSpec((heads, rows, lanes), lambda i, t: (0, 0, 0), pipeline_mode=pl.Buffered(1)),
                pl.BlockSpec((1, 1, blk), lambda i, t: (i + t[nk], 0, 0)),
            ],
            out_specs=[
                pl.BlockSpec((blk, heads * hd), lambda i, t: (i, 0)),
                pl.BlockSpec((heads, blk), lambda i, t: (0, i)),
            ],
            scratch_shapes=[
                pltpu.VMEM((heads, lanes, rows), bf16),
                pltpu.VMEM((heads * hd, blk), f32),
                pltpu.VMEM((heads, blk), f32),
                pltpu.VMEM((heads, blk), f32),
            ],
        ),
        out_shape=[
            jax.ShapeDtypeStruct((nq * blk, heads * hd), bf16),
            jax.ShapeDtypeStruct((heads, nq * blk), f32),
        ],
        compiler_params=pltpu.CompilerParams(vmem_limit_bytes=56 << 20),
        name="attention_forward",
    )(table, q3, k3, v3, start_row)


def attn_bwd_kernel(first_ref, order_ref, q_ref, k_ref, v_ref, start_ref, lse_ref, o_ref, do_ref, cos_ref, sin_ref, cost_ref, sint_ref,
                    g_ref, kt_ref, do3_ref, dk_ref, dv_ref, dqt_ref, d_ref, *, blk, hd, scale):
    heads, rows, lanes = k_ref.shape
    nk = rows // blk
    half = hd // 2
    at_step = pl.program_id(0)
    i = order_ref[at_step]

    @pl.when(at_step == 0)
    def _():
        def body(h, c):
            for t in range(nk):
                kt_ref[h, :, t * blk : (t + 1) * blk] = k_ref[h, t * blk : (t + 1) * blk, :].T
            return c
        lax.fori_loop(0, heads, body, 0)
        dk_ref[...] = jnp.zeros_like(dk_ref)
        dv_ref[...] = jnp.zeros_like(dv_ref)
        do3_ref[...] = jnp.zeros_like(do3_ref)

    for h in range(heads):
        do3_ref[h, :, :hd] = do_ref[:, h * hd : (h + 1) * hd]
    prod = do_ref[...].astype(f32) * o_ref[...].astype(f32)
    high = prod.astype(bf16)
    low = (prod - high.astype(f32)).astype(bf16)
    pad_heads = d_ref.shape[0]
    owner = lax.broadcasted_iota(jnp.int32, (pad_heads, heads * hd), 1) // hd
    pick = (owner == lax.broadcasted_iota(jnp.int32, (pad_heads, heads * hd), 0)).astype(f32).astype(bf16)
    d_ref[...] = dot(pick, high, NT) + dot(pick, low, NT)
    dqt_ref[...] = jnp.zeros_like(dqt_ref)
    c2 = scale * LOG2E

    def step(j, carry):
        mask = allowed_mask(j, i, start_ref[0], blk)
        at = pl.ds(pl.multiple_of(j * blk, blk), blk)
        for h in range(heads):
            k = k_ref[h, at, :]
            q = q_ref[h]
            do = do3_ref[h]
            s = dot(k, q, NT)
            p = jnp.where(mask, jnp.exp2(s * c2 - lse_ref[h : h + 1]), 0.0)
            dp = dot(v_ref[h, at, :], do, NT)
            ds = (p * (dp - d_ref[h : h + 1])).astype(bf16)
            dv_ref[h, at, :] += dot(p.astype(bf16), do)
            dk_ref[h, at, :] += dot(ds, q)
            part = slice(h * hd, (h + 1) * hd)
            dqt_ref[part, :] += dot(kt_ref[h, :hd, at], ds)
        return carry

    lax.fori_loop(first_ref[i], i + 1, step, 0)
    ct = cost_ref[...]
    st = sint_ref[...]
    for h in range(heads):
        a = dqt_ref[h * hd : h * hd + half, :] * scale
        b = dqt_ref[h * hd + half : (h + 1) * hd, :] * scale
        dqt_ref[h * hd : h * hd + half, :] = a * ct + b * st
        dqt_ref[h * hd + half : (h + 1) * hd, :] = b * ct - a * st
    g_ref[0, pl.ds(pl.multiple_of(i * blk, blk), blk), :] = dqt_ref[...].T.astype(bf16)

    @pl.when(at_step == nk - 1)
    def _():
        def fin(t, c):
            at = pl.ds(pl.multiple_of(t * blk, blk), blk)
            cos, sin = cos_ref[at, :], sin_ref[at, :]
            lane = lax.broadcasted_iota(jnp.int32, (blk, lanes), 1)
            for h in range(heads):
                x = dk_ref[h, at, :] * scale
                other = jnp.where(lane < half, pltpu.roll(x, lanes - half, 1), -pltpu.roll(x, half, 1))
                g_ref[1, at, h * hd : (h + 1) * hd] = (x * cos + other * sin).astype(bf16)[:, :hd]
                g_ref[2, at, h * hd : (h + 1) * hd] = dv_ref[h, at, :].astype(bf16)[:, :hd]
            return c
        lax.fori_loop(0, nk, fin, 0)


def attention_backward(first, order, q3, k3, v3, start_row, lse, attended, grad_att, cos, sin, cost, sint, hd, scale, blk=BLK):
    heads, rows, lanes = k3.shape
    nk = rows // blk
    pad_heads = max(8, heads)
    half = hd // 2
    whole = lambda shape: pl.BlockSpec(shape, lambda i, t, o: (0,) * len(shape), pipeline_mode=pl.Buffered(1))
    return pl.pallas_call(
        functools.partial(attn_bwd_kernel, blk=blk, hd=hd, scale=scale),
        grid_spec=pltpu.PrefetchScalarGridSpec(
            num_scalar_prefetch=2,
            grid=(nk,),
            in_specs=[
                pl.BlockSpec((heads, blk, lanes), lambda i, t, o: (0, o[i], 0)),
                whole((heads, rows, lanes)),
                whole((heads, rows, lanes)),
                pl.BlockSpec((1, 1, blk), lambda i, t, o: (o[i], 0, 0)),
                pl.BlockSpec((heads, blk), lambda i, t, o: (0, i)),
                pl.BlockSpec((blk, heads * hd), lambda i, t, o: (i, 0)),
                pl.BlockSpec((blk, heads * hd), lambda i, t, o: (i, 0)),
                whole((rows, lanes)),
                whole((rows, lanes)),
                pl.BlockSpec((half, blk), lambda i, t, o: (0, o[i])),
                pl.BlockSpec((half, blk), lambda i, t, o: (0, o[i])),
            ],
            out_specs=pl.BlockSpec((3, rows, heads * hd), lambda i, t, o: (0, 0, 0), pipeline_mode=pl.Buffered(1)),
            scratch_shapes=[
                pltpu.VMEM((heads, lanes, rows), bf16),
                pltpu.VMEM((heads, blk, lanes), bf16),
                pltpu.VMEM((heads, rows, lanes), f32),
                pltpu.VMEM((heads, rows, lanes), f32),
                pltpu.VMEM((heads * hd, blk), f32),
                pltpu.VMEM((pad_heads, blk), f32),
            ],
        ),
        out_shape=jax.ShapeDtypeStruct((3, rows, heads * hd), bf16),
        compiler_params=pltpu.CompilerParams(vmem_limit_bytes=60 << 20),
        name="attention_backward",
    )(first, order, q3, k3, v3, start_row, lse, attended, grad_att, cos, sin, cost, sint)


def mlp_kernel(x_ref, og_ref, wg_ref, wu_ref, wo_ref, out_ref, gn_ref, gw_ref, xt_ref, ogt_ref, act_ref, gg_ref, gu_ref, *, rc, cc, turned):
    rows, dim = x_ref.shape
    hb = wg_ref.shape[1]
    forward_wo, backward_wo = (NT, NN) if turned else (NN, NT)

    @pl.when(pl.program_id(0) == 0)
    def _():
        def turn(t, c):
            at = pl.ds(pl.multiple_of(t * cc, cc), cc)
            for r in range(0, rows, cc):
                xt_ref[at, r : r + cc] = x_ref[r : r + cc, at].T
                ogt_ref[at, r : r + cc] = og_ref[r : r + cc, at].T
            return c
        lax.fori_loop(0, dim // cc, turn, 0)
        out_ref[...] = jnp.zeros_like(out_ref)
        gn_ref[...] = jnp.zeros_like(gn_ref)

    def by_rows(r, c):
        at = pl.ds(pl.multiple_of(r * rc, rc), rc)
        x = x_ref[at, :]
        g = dot(x, wg_ref[...])
        u = dot(x, wu_ref[...])
        ga = dot(og_ref[at, :], wo_ref[...], backward_wo)
        s = 1.0 / (1.0 + jnp.exp(-g))
        silu = g * s
        act = (silu * u).astype(bf16)
        gg = (ga * u * (s * (1.0 + g * (1.0 - s)))).astype(bf16)
        gu = (ga * silu).astype(bf16)
        act_ref[at, :] = act
        gg_ref[at, :] = gg
        gu_ref[at, :] = gu
        out_ref[at, :] += dot(act, wo_ref[...], forward_wo)
        gn_ref[at, :] += dot(gg, wg_ref[...], NT) + dot(gu, wu_ref[...], NT)
        return c

    lax.fori_loop(0, rows // rc, by_rows, 0)

    def by_columns(t, c):
        at = pl.ds(pl.multiple_of(t * cc, cc), cc)
        xt = xt_ref[at, :]
        gw_ref[at, 0:hb] = dot(xt, gg_ref[...]).astype(bf16)
        gw_ref[at, hb : 2 * hb] = dot(xt, gu_ref[...]).astype(bf16)
        gw_ref[at, 2 * hb :] = dot(ogt_ref[at, :], act_ref[...]).astype(bf16)
        return c

    lax.fori_loop(0, dim // cc, by_columns, 0)


def block_of(size, most):
    return next(b for b in (most, 512, 256, 128) if b <= most and size % b == 0)


def mlp(x, og, weights, hidden, turned, hb=512, rc=512, cc=256):
    rows, dim = x.shape
    hb = block_of(hidden, hb)
    nh = hidden // hb
    rc = block_of(rows, rc)
    whole = lambda shape: pl.BlockSpec(shape, lambda h: (0,) * len(shape), pipeline_mode=pl.Buffered(1))
    arrays = [w[0] for w in weights]
    specs = [w[1](hb, nh) for w in weights]
    return pl.pallas_call(
        functools.partial(mlp_kernel, rc=rc, cc=cc, turned=turned),
        grid=(nh,),
        in_specs=[whole((rows, dim)), whole((rows, dim))] + specs,
        out_specs=[whole((rows, dim)), whole((rows, dim)), pl.BlockSpec((dim, 3 * hb), lambda h: (0, h))],
        scratch_shapes=[
            pltpu.VMEM((dim, rows), bf16), pltpu.VMEM((dim, rows), bf16),
            pltpu.VMEM((rows, hb), bf16), pltpu.VMEM((rows, hb), bf16), pltpu.VMEM((rows, hb), bf16),
        ],
        out_shape=[
            jax.ShapeDtypeStruct((rows, dim), f32),
            jax.ShapeDtypeStruct((rows, dim), f32),
            jax.ShapeDtypeStruct((dim, 3 * hidden), bf16),
        ],
        compiler_params=pltpu.CompilerParams(vmem_limit_bytes=60 << 20),
        name="feed_forward",
    )(x, og, *arrays)


def local_weights(mlp_in, mlp_out):
    dim = mlp_in.shape[1]
    return (
        (mlp_in, lambda hb, nh: pl.BlockSpec((None, dim, hb), lambda h: (0, 0, h))),
        (mlp_in, lambda hb, nh: pl.BlockSpec((None, dim, hb), lambda h: (1, 0, h))),
        (mlp_out, lambda hb, nh: pl.BlockSpec((hb, dim), lambda h: (h, 0))),
    )


def turned_weights(w):
    dim = w.shape[0]
    return tuple((w, lambda hb, nh, part=part: pl.BlockSpec((dim, hb), lambda h: (0, part * nh + h))) for part in range(3))

EPSILON = 1e-06
HEAD_DIM = 80


def layout(lengths_row, bucket_rows):
    series_ends = jnp.cumsum(lengths_row, dtype=jnp.int32)
    places = jnp.arange(bucket_rows, dtype=jnp.int32)
    before = series_ends[None, :] <= places[:, None]
    starts = jnp.sum(jnp.where(before, lengths_row[None, :], 0), axis=1, dtype=jnp.int32)
    return places, starts


def turning(position, hd):
    half = hd // 2
    frequency = 10000.0 ** (-(jnp.arange(half, dtype=f32) * 2.0 / hd))
    place = position.astype(f32)
    turned = frequency[:, None] * place[None, :]
    wide = jnp.concatenate([frequency, frequency, jnp.zeros((LANES - hd,), f32)])
    angles = place[:, None] * wide[None, :]
    return jnp.cos(angles), jnp.sin(angles), jnp.cos(turned), jnp.sin(turned)


def qkv_kernel(base_ref, x_ref, gain_ref, w_ref, cos_ref, sin_ref, *refs, hd):
    n_ref, q_ref, k_ref, v_ref = refs[-4:]
    heads, rows, lanes = q_ref.shape
    half = hd // 2
    x = x_ref[...].astype(f32)
    inverse = lax.rsqrt(jnp.mean(x * x, axis=-1, keepdims=True) + EPSILON)
    normed = (x * inverse * gain_ref[...]).astype(bf16)
    n_ref[...] = normed
    cos, sin = cos_ref[...], sin_ref[...]
    lane = lax.broadcasted_iota(jnp.int32, (rows, lanes), 1)
    pad = jnp.zeros((rows, lanes - hd), f32)
    for j, out in enumerate((q_ref, k_ref, v_ref)):
        y = dot(normed, w_ref[j])
        for h in range(heads):
            part = jnp.concatenate([y[:, h * hd : (h + 1) * hd], pad], axis=1)
            if j < 2:
                other = jnp.where(lane < half, -pltpu.roll(part, lanes - half, 1), pltpu.roll(part, half, 1))
                part = part * cos + other * sin
                part = jnp.where(lane < hd, part, 0.0)
            out[h] = part.astype(bf16)


def project(x, base, bucket_rows, gain_row, attn_in, cos, sin, hd, before=None, blk=BLK):
    rows, dim = x.shape
    cols = attn_in.shape[2]
    heads = cols // hd
    at = lambda i, b: (b[0] + i, 0)
    at_heads = lambda i, b: (0, b[0] + i, 0)
    extra = () if before is None else tuple(before)
    return pl.pallas_call(
        functools.partial(qkv_kernel, hd=hd),
        grid_spec=pltpu.PrefetchScalarGridSpec(
            num_scalar_prefetch=1,
            grid=(rows // blk,),
            in_specs=[
                pl.BlockSpec((blk, dim), lambda i, b: (i, 0)),
                pl.BlockSpec((1, dim), lambda i, b: (0, 0)),
                pl.BlockSpec(attn_in.shape, lambda i, b: (0, 0, 0), pipeline_mode=pl.Buffered(1)),
                pl.BlockSpec((blk, LANES), at),
                pl.BlockSpec((blk, LANES), at),
            ]
            + [pl.BlockSpec(memory_space=pl.ANY)] * len(extra),
            out_specs=[pl.BlockSpec((blk, dim), at)] + [pl.BlockSpec((heads, blk, LANES), at_heads)] * 3,
        ),
        out_shape=[jax.ShapeDtypeStruct((bucket_rows, dim), bf16)]
        + [jax.ShapeDtypeStruct((heads, bucket_rows, LANES), bf16)] * 3,
        input_output_aliases={6 + n: n for n in range(len(extra))},
        compiler_params=pltpu.CompilerParams(vmem_limit_bytes=48 << 20),
        name="project",
    )(jnp.reshape(base, (1,)).astype(jnp.int32), x, gain_row[None, :], attn_in, cos, sin, *extra)


def unproject_kernel(base_ref, g_ref, w_ref, out_ref):
    total = dot(g_ref[0], w_ref[0], NT) + dot(g_ref[1], w_ref[1], NT) + dot(g_ref[2], w_ref[2], NT)
    out_ref[...] = total.astype(out_ref.dtype)


def unproject(grad_qkv, base, rows, attn_in, dtype, blk=BLK):
    cols = grad_qkv.shape[2]
    dim = attn_in.shape[1]
    return pl.pallas_call(
        unproject_kernel,
        grid_spec=pltpu.PrefetchScalarGridSpec(
            num_scalar_prefetch=1,
            grid=(rows // blk,),
            in_specs=[
                pl.BlockSpec((3, blk, cols), lambda i, b: (0, b[0] + i, 0)),
                pl.BlockSpec(attn_in.shape, lambda i, b: (0, 0, 0), pipeline_mode=pl.Buffered(1)),
            ],
            out_specs=pl.BlockSpec((blk, dim), lambda i, b: (i, 0)),
        ),
        out_shape=jax.ShapeDtypeStruct((rows, dim), dtype),
        compiler_params=pltpu.CompilerParams(vmem_limit_bytes=48 << 20),
        name="unproject",
    )(jnp.reshape(base, (1,)).astype(jnp.int32), grad_qkv, attn_in)


def inverse_rms(values):
    return lax.rsqrt(jnp.mean(values * values, axis=-1, keepdims=True) + EPSILON)


def norm_input_part(values, gain_row, grad_normed):
    inverse = inverse_rms(values)
    weighted = grad_normed * gain_row
    inner = jnp.mean(weighted * values, axis=-1, keepdims=True)
    return weighted * inverse - values * (inverse * inverse * inverse) * inner


def dims(a, b, contract):
    return lax.dot_general(a, b, (contract, ((), ())), preferred_element_type=f32)


def per_device(tokens, norm_gains, attn_in, attn_out, mlp_in, mlp_out, lengths, out_grad):
    n_mp = lax.axis_size("mp")
    n_dp = lax.axis_size("dp")
    me = lax.axis_index("mp")
    group = lax.axis_index("dp")
    rows, dim = tokens.shape
    bucket = rows * n_mp
    hd = HEAD_DIM
    cols = attn_out.shape[0]
    hidden = mlp_out.shape[0]
    share = dim // n_dp
    scale = hd**-0.5
    pair = n_mp == 2
    swap = ((0, 1), (1, 0))
    places, starts = layout(lengths[0], bucket)
    cos, sin, cost, sint = turning(places - starts, hd)
    first = starts[::BLK] // BLK
    start_row = starts.reshape(bucket // BLK, 1, BLK)
    blocks = bucket // BLK
    own_blocks = rows // BLK

    def mine(array, axis, size):
        return lax.dynamic_slice_in_dim(array, group * size, size, axis)

    if pair:
        other_x = lax.ppermute(tokens, "mp", swap)
        piece = jnp.concatenate(
            [mine(mlp_in[0], 0, share), mine(mlp_in[1], 0, share), mine(mlp_out, 1, share).T, mine(attn_out, 1, share).T], axis=1
        )
        other_w = lax.all_gather(lax.ppermute(piece, "mp", swap), "dp", axis=0, tiled=True)
        other_attn_out = other_w[:, 3 * hidden :]
        own_at, other_at = me * own_blocks, (1 - me) * own_blocks
        half_done = project(tokens, own_at, bucket, norm_gains[0], attn_in, cos, sin, hd)
        normed_one, q3, k3, v3 = project(other_x, other_at, bucket, norm_gains[0], attn_in, cos, sin, hd, half_done)
        att_send, lse_other = attention_forward(first, other_at, q3, k3, v3, start_row, hd, scale, own_blocks)
        att_got = lax.ppermute(att_send, "mp", swap)
        att_own, lse_own = attention_forward(first, own_at, q3, k3, v3, start_row, hd, scale, own_blocks)
        branch = dot(att_own, attn_out) + dims(att_got, other_attn_out, ((1,), (1,)))
    else:
        normed_one, q3, k3, v3 = project(
            lax.all_gather(tokens, "mp", axis=0, tiled=True), 0, bucket, norm_gains[0], attn_in, cos, sin, hd
        )
        att_all, lse_all = attention_forward(first, 0, q3, k3, v3, start_row, hd, scale, blocks)
        att_rows = lax.all_to_all(att_all, "mp", 0, 1, tiled=True)
        all_attn_out = lax.all_gather(attn_out, "mp", axis=0, tiled=True)
        branch = dot(att_rows, all_attn_out)
    middle = tokens.astype(f32) + branch
    normed_two = (middle * inverse_rms(middle) * norm_gains[1]).astype(bf16)
    if pair:
        out_a, gn_a, gw_own = mlp(normed_two, out_grad, local_weights(mlp_in, mlp_out), hidden, False)
        out_b, gn_b, gw_other = mlp(normed_two, out_grad, turned_weights(other_w), hidden, True)
        output = (middle + (out_a + out_b)).astype(bf16)
        grad_normed_two = gn_a + gn_b
    else:
        all_in = lax.all_gather(mlp_in, "mp", axis=2, tiled=True)
        all_out = lax.all_gather(mlp_out, "mp", axis=0, tiled=True)
        out_a, gn_a, gw_all = mlp(normed_two, out_grad, local_weights(all_in, all_out), hidden * n_mp, False)
        output = (middle + out_a).astype(bf16)
        grad_normed_two = gn_a
    grad_middle = out_grad.astype(f32) + norm_input_part(middle, norm_gains[1], grad_normed_two)
    branch_grad = grad_middle.astype(bf16)

    def scatter(array):
        return lax.psum_scatter(array, "dp", scatter_dimension=0, tiled=True)

    if pair:
        do_send = dims(branch_grad, other_attn_out, ((1,), (0,))).astype(bf16)
        do_got = lax.ppermute(do_send, "mp", swap)
        do_own = dims(branch_grad, attn_out, ((1,), (1,))).astype(bf16)
        grad_heads = jnp.concatenate([do_own, do_got], axis=0)
        att_all = jnp.concatenate([att_own, att_send], axis=0)
        lse_all = jnp.concatenate([lse_own, lse_other], axis=1)
        count = jnp.arange(own_blocks, dtype=jnp.int32)
        order = jnp.concatenate([own_at + count, other_at + count])
    else:
        do_rows = dims(branch_grad, all_attn_out, ((1,), (1,))).astype(bf16)
        grad_heads = lax.all_to_all(do_rows, "mp", 1, 0, tiled=True)
        order = jnp.arange(blocks, dtype=jnp.int32)
    grad_qkv = attention_backward(
        first, order, q3, k3, v3, start_row, lse_all, att_all, grad_heads, cos, sin, cost, sint, hd, scale
    )
    if pair:
        gn_send = unproject(grad_qkv, other_at, rows, attn_in, bf16)
        gn_got = lax.ppermute(gn_send, "mp", swap)
        grad_normed_one = unproject(grad_qkv, own_at, rows, attn_in, f32) + gn_got.astype(f32)
    else:
        grad_normed_one = lax.psum_scatter(
            unproject(grad_qkv, 0, bucket, attn_in, bf16), "mp", scatter_dimension=0, tiled=True
        ).astype(f32)
    inputs = tokens.astype(f32)
    grad_tokens = (grad_middle + norm_input_part(inputs, norm_gains[0], grad_normed_one)).astype(bf16)
    gw_attn_in = jnp.concatenate(
        [dims(normed_one, grad_qkv[j], ((0,), (0,))).astype(bf16) for j in range(3)], axis=1
    )
    if pair:
        other_sum = jnp.concatenate(
            [scatter(gw_other), scatter(dims(branch_grad, att_got, ((0,), (0,))).astype(bf16))], axis=1
        )
        from_pair = lax.ppermute(other_sum, "mp", swap).astype(f32)
        sum_mlp = scatter(gw_own).astype(f32) + from_pair[:, : 3 * hidden]
        sum_attn_out = scatter(dims(branch_grad, att_own, ((0,), (0,))).astype(bf16)).astype(f32) + from_pair[:, 3 * hidden :]
        hb = block_of(hidden, 512)
        parts = sum_mlp.reshape(share, hidden // hb, 3, hb).transpose(2, 0, 1, 3).reshape(3, share, hidden)
    else:
        hb = block_of(hidden * n_mp, 512)
        sum_mlp = scatter(gw_all).reshape(share, hidden * n_mp // hb, 3, hb).transpose(2, 0, 1, 3).reshape(3, share, hidden * n_mp)
        parts = lax.psum_scatter(sum_mlp, "mp", scatter_dimension=2, tiled=True).astype(f32)
        sum_attn_out = lax.psum_scatter(
            scatter(dims(branch_grad, att_rows, ((0,), (0,))).astype(bf16)), "mp", scatter_dimension=1, tiled=True
        ).astype(f32)
    sum_attn_in = scatter(gw_attn_in).astype(f32).reshape(share, 3, cols).transpose(1, 0, 2)
    gain_one = jnp.sum(mine(attn_in, 1, share).astype(f32) * sum_attn_in, axis=(0, 2))
    gain_two = jnp.sum(mine(mlp_in, 1, share).astype(f32) * parts[:2], axis=(0, 2))
    gains = jnp.stack([gain_one, gain_two]) / mine(norm_gains, 1, share)
    gains = lax.psum_scatter(gains, "mp", scatter_dimension=1, tiled=True)
    return (output, grad_tokens, gains, sum_attn_in, sum_attn_out.T, parts[:2], parts[2].T)


def solution(mesh):
    placed = (
        P(("dp", "mp"), None),
        P(),
        P(None, None, "mp"),
        P("mp", None),
        P(None, None, "mp"),
        P("mp", None),
        P("dp", None),
        P(("dp", "mp"), None),
    )
    return jax.shard_map(
        per_device,
        mesh=mesh,
        in_specs=placed,
        out_specs=(
            P(("dp", "mp"), None),
            P(("dp", "mp"), None),
            P(None, ("dp", "mp")),
            P(None, "dp", "mp"),
            P("mp", "dp"),
            P(None, "dp", "mp"),
            P("mp", "dp"),
        ),
        check_vma=False,
    )
```

```python
import functools

import jax
import jax.numpy as jnp
from jax import lax
from jax.experimental import pallas as pl
from jax.experimental.pallas import tpu as pltpu
from jax.sharding import PartitionSpec as P

BLK = 256
LANES = 128
HEAD_DIM = 80
EPSILON = 1e-06
LOG2E = 1.4426950408889634
NEG = -1e30
bf16 = jnp.bfloat16
f32 = jnp.float32
NT = (((1,), (1,)), ((), ()))
NN = (((1,), (0,)), ((), ()))
ONE = dict(pipeline_mode=pl.Buffered(1))


def dot(a, b, contract=NN):
    return lax.dot_general(a, b, contract, preferred_element_type=f32)


COST = pl.CostEstimate(flops=40_000_000_000, bytes_accessed=20_000_000, transcendentals=0)
ANY = pl.BlockSpec(memory_space=pl.ANY)


def params(mib):
    return pltpu.CompilerParams(vmem_limit_bytes=mib << 20)


def block_of(size, most):
    return next(b for b in (most, 1024, 512, 256, 128) if b <= most and size % b == 0)


def scalar(value):
    return jnp.reshape(value, (1,)).astype(jnp.int32)


def layout(lengths_row, bucket_rows):
    series_ends = jnp.cumsum(lengths_row, dtype=jnp.int32)
    places = jnp.arange(bucket_rows, dtype=jnp.int32)
    before = series_ends[None, :] <= places[:, None]
    starts = jnp.sum(jnp.where(before, lengths_row[None, :], 0), axis=1, dtype=jnp.int32)
    return places, starts


def turning(position, hd):
    half = hd // 2
    frequency = 10000.0 ** (-(jnp.arange(half, dtype=f32) * 2.0 / hd))
    place = position.astype(f32)
    turned = frequency[:, None] * place[None, :]
    wide = jnp.concatenate([frequency, frequency, jnp.zeros((LANES - hd,), f32)])
    angles = place[:, None] * wide[None, :]
    return jnp.cos(angles), jnp.sin(angles), jnp.cos(turned), jnp.sin(turned)


def project_kernel(base_ref, x_ref, gain_ref, w_ref, cos_ref, sin_ref, *refs, hd):
    n_ref, q_ref, k_ref, v_ref, kt_ref, vt_ref = refs[-6:]
    heads, rows, lanes = q_ref.shape
    half = hd // 2
    x = x_ref[...].astype(f32)
    inverse = lax.rsqrt(jnp.mean(x * x, axis=-1, keepdims=True) + EPSILON)
    normed = (x * inverse * gain_ref[...]).astype(bf16)
    n_ref[...] = normed
    cos, sin = cos_ref[...], sin_ref[...]
    lane = lax.broadcasted_iota(jnp.int32, (rows, lanes), 1)
    pad = jnp.zeros((rows, lanes - hd), f32)
    for j, out in enumerate((q_ref, k_ref, v_ref)):
        y = dot(normed, w_ref[j])
        for h in range(heads):
            part = jnp.concatenate([y[:, h * hd : (h + 1) * hd], pad], axis=1)
            if j < 2:
                other = jnp.where(lane < half, -pltpu.roll(part, lanes - half, 1), pltpu.roll(part, half, 1))
                part = part * cos + other * sin
                part = jnp.where(lane < hd, part, 0.0)
            part = part.astype(bf16)
            out[h] = part
            if j == 1:
                kt_ref[h] = part.T
            if j == 2:
                vt_ref[h] = part.T


def project(x, base, bucket_rows, gain_row, attn_in, cos, sin, hd, before=None, wait=(), blk=BLK):
    rows, dim = x.shape
    heads = attn_in.shape[2] // hd
    at = lambda i, b: (b[0] + i, 0)
    at_heads = lambda i, b: (0, b[0] + i, 0)
    at_turned = lambda i, b: (0, 0, b[0] + i)
    extra = () if before is None else tuple(before)
    return pl.pallas_call(
        functools.partial(project_kernel, hd=hd),
        grid_spec=pltpu.PrefetchScalarGridSpec(
            num_scalar_prefetch=1,
            grid=(rows // blk,),
            in_specs=[
                pl.BlockSpec((blk, dim), lambda i, b: (i, 0)),
                pl.BlockSpec((1, dim), lambda i, b: (0, 0)),
                pl.BlockSpec(attn_in.shape, lambda i, b: (0, 0, 0), **ONE),
                pl.BlockSpec((blk, LANES), at),
                pl.BlockSpec((blk, LANES), at),
            ]
            + [ANY] * (len(extra) + len(wait)),
            out_specs=[pl.BlockSpec((blk, dim), at)]
            + [pl.BlockSpec((heads, blk, LANES), at_heads)] * 3
            + [pl.BlockSpec((heads, LANES, blk), at_turned)] * 2,
        ),
        out_shape=[jax.ShapeDtypeStruct((bucket_rows, dim), bf16)]
        + [jax.ShapeDtypeStruct((heads, bucket_rows, LANES), bf16)] * 3
        + [jax.ShapeDtypeStruct((heads, LANES, bucket_rows), bf16)] * 2,
        input_output_aliases={6 + n: n for n in range(len(extra))},
        compiler_params=params(56),
        cost_estimate=COST,
        name="project",
    )(scalar(base), x, gain_row[None, :], attn_in, cos, sin, *extra, *wait)


def allowed_mask(j, i, start_row, blk):
    kpos = j * blk + lax.broadcasted_iota(jnp.int32, (blk, blk), 0)
    qpos = i * blk + lax.broadcasted_iota(jnp.int32, (blk, blk), 1)
    return (kpos >= start_row) & (kpos <= qpos)


def attention_forward_kernel(first_ref, q_ref, k_ref, vt_ref, start_ref, *refs, base, blk, hd, scale):
    o_ref, lse_ref, acc_ref, m_ref, l_ref = refs[-5:]
    heads = k_ref.shape[0]
    i = base + pl.program_id(0)
    acc_ref[...] = jnp.zeros_like(acc_ref)
    m_ref[...] = jnp.full_like(m_ref, NEG)
    l_ref[...] = jnp.zeros_like(l_ref)
    c2 = scale * LOG2E

    def step(j, carry):
        mask = allowed_mask(j, i, start_ref[0], blk)
        rows = pl.ds(pl.multiple_of(j * blk, blk), blk)
        for h in range(heads):
            s = dot(k_ref[h, rows, :], q_ref[h], NT)
            s = jnp.where(mask, s * c2, NEG)
            m_old = m_ref[h : h + 1]
            m_new = jnp.maximum(m_old, jnp.max(s, axis=0, keepdims=True))
            alpha = jnp.exp2(m_old - m_new)
            p = jnp.exp2(s - m_new)
            l_ref[h : h + 1] = alpha * l_ref[h : h + 1] + jnp.sum(p, axis=0, keepdims=True)
            m_ref[h : h + 1] = m_new
            part = slice(h * hd, (h + 1) * hd)
            acc_ref[part, :] = alpha * acc_ref[part, :] + dot(vt_ref[h, :hd, rows], p.astype(bf16))
        return carry

    step(i, 0)
    lax.fori_loop(first_ref[i], i, step, 0)
    for h in range(heads):
        part = slice(h * hd, (h + 1) * hd)
        acc_ref[part, :] = acc_ref[part, :] / l_ref[h : h + 1]
    o_ref[...] = acc_ref[...].T.astype(bf16)
    lse_ref[...] = m_ref[...] + jnp.log2(l_ref[...])


def attention_forward(first, low, high, q3, k3, vt, start_row, hd, scale, wait=(), blk=BLK):
    heads, rows, lanes = k3.shape
    base, count = low // blk, (high - low) // blk
    return pl.pallas_call(
        functools.partial(attention_forward_kernel, base=base, blk=blk, hd=hd, scale=scale),
        grid_spec=pltpu.PrefetchScalarGridSpec(
            num_scalar_prefetch=1,
            grid=(count,),
            in_specs=[
                pl.BlockSpec((heads, blk, lanes), lambda i, t: (0, i + base, 0)),
                pl.BlockSpec((heads, high, lanes), lambda i, t: (0, 0, 0), **ONE),
                pl.BlockSpec((heads, lanes, high), lambda i, t: (0, 0, 0), **ONE),
                pl.BlockSpec((1, 1, blk), lambda i, t: (i + base, 0, 0)),
            ]
            + [ANY] * len(wait),
            out_specs=[
                pl.BlockSpec((blk, heads * hd), lambda i, t: (i, 0)),
                pl.BlockSpec((heads, blk), lambda i, t: (0, i)),
            ],
            scratch_shapes=[
                pltpu.VMEM((heads * hd, blk), f32),
                pltpu.VMEM((heads, blk), f32),
                pltpu.VMEM((heads, blk), f32),
            ],
        ),
        out_shape=[
            jax.ShapeDtypeStruct((count * blk, heads * hd), bf16),
            jax.ShapeDtypeStruct((heads, count * blk), f32),
        ],
        compiler_params=params(56),
        cost_estimate=COST,
        name="attention_forward",
    )(first, q3, k3, vt, start_row, *wait)


def attention_backward_kernel(
    first_ref, q_ref, k_ref, v_ref, kt_ref, start_ref, lse_ref, o_ref, do_ref, cos_ref, sin_ref, cost_ref, sint_ref, w_ref, *refs,
    base, count, blk, hd, scale, carried, waits,
):
    carry_in, refs = (refs[:2], refs[2:]) if carried else ((), refs)
    refs = refs[waits:]
    g_ref, wide_ref, narrow_ref, refs = *refs[:3], refs[3:]
    carry_out, refs = (refs[:2], refs[2:]) if base else ((), refs)
    do3_ref, dk_ref, dv_ref, dqt_ref, d_ref = refs
    heads, rows, lanes = k_ref.shape
    half = hd // 2
    step_at = pl.program_id(0)
    i = base + count - 1 - step_at

    @pl.when(step_at == 0)
    def _():
        do3_ref[...] = jnp.zeros_like(do3_ref)
        if carried:
            dk_ref[...] = carry_in[0][...]
            dv_ref[...] = carry_in[1][...]
        else:
            dk_ref[...] = jnp.zeros_like(dk_ref)
            dv_ref[...] = jnp.zeros_like(dv_ref)

    for h in range(heads):
        do3_ref[h, :, :hd] = do_ref[:, h * hd : (h + 1) * hd]
    prod = do_ref[...].astype(f32) * o_ref[...].astype(f32)
    high = prod.astype(bf16)
    low = (prod - high.astype(f32)).astype(bf16)
    pad_heads = d_ref.shape[0]
    owner = lax.broadcasted_iota(jnp.int32, (pad_heads, heads * hd), 1) // hd
    pick = (owner == lax.broadcasted_iota(jnp.int32, (pad_heads, heads * hd), 0)).astype(f32).astype(bf16)
    d_ref[...] = dot(pick, high, NT) + dot(pick, low, NT)
    dqt_ref[...] = jnp.zeros_like(dqt_ref)
    c2 = scale * LOG2E

    def step(j, carry):
        mask = allowed_mask(j, i, start_ref[0], blk)
        at = pl.ds(pl.multiple_of(j * blk, blk), blk)
        for h in range(heads):
            q = q_ref[h]
            do = do3_ref[h]
            s = dot(k_ref[h, at, :], q, NT)
            p = jnp.where(mask, jnp.exp2(s * c2 - lse_ref[h : h + 1]), 0.0)
            dp = dot(v_ref[h, at, :], do, NT)
            ds = (p * (dp - d_ref[h : h + 1])).astype(bf16)
            dv_ref[h, at, :] += dot(p.astype(bf16), do)
            dk_ref[h, at, :] += dot(ds, q)
            part = slice(h * hd, (h + 1) * hd)
            dqt_ref[part, :] += dot(kt_ref[h, :hd, at], ds)
        return carry

    lax.fori_loop(first_ref[i], i + 1, step, 0)
    ct = cost_ref[...]
    st = sint_ref[...]
    for h in range(heads):
        a = dqt_ref[h * hd : h * hd + half, :] * scale
        b = dqt_ref[h * hd + half : (h + 1) * hd, :] * scale
        dqt_ref[h * hd : h * hd + half, :] = a * ct + b * st
        dqt_ref[h * hd + half : (h + 1) * hd, :] = b * ct - a * st
    g_ref[0] = dqt_ref[...].T.astype(bf16)
    at = pl.ds(pl.multiple_of(i * blk, blk), blk)
    cos, sin = cos_ref[...], sin_ref[...]
    lane = lax.broadcasted_iota(jnp.int32, (blk, lanes), 1)
    for h in range(heads):
        x = dk_ref[h, at, :] * scale
        other = jnp.where(lane < half, pltpu.roll(x, lanes - half, 1), -pltpu.roll(x, half, 1))
        g_ref[1, :, h * hd : (h + 1) * hd] = (x * cos + other * sin).astype(bf16)[:, :hd]
        g_ref[2, :, h * hd : (h + 1) * hd] = dv_ref[h, at, :].astype(bf16)[:, :hd]
    total = dot(g_ref[0], w_ref[0], NT) + dot(g_ref[1], w_ref[1], NT) + dot(g_ref[2], w_ref[2], NT)
    wide_ref[...] = total
    narrow_ref[...] = total.astype(bf16)
    if base:

        @pl.when(step_at == count - 1)
        def _():
            carry_out[0][...] = dk_ref[:, : base * blk, :]
            carry_out[1][...] = dv_ref[:, : base * blk, :]


def attention_backward(first, low, high, q3, k3, v3, kt, start_row, lse, attended, grad_att, tables, attn_in, hd, scale, carry, wait=(), blk=BLK):
    heads, rows, lanes = k3.shape
    base, count = low // blk, (high - low) // blk
    cos, sin, cost, sint = tables
    pad_heads = max(8, heads)
    half = hd // 2
    here = lambda i: count - 1 - i
    there = lambda i: base + count - 1 - i
    carried = carry is not None
    before = jax.ShapeDtypeStruct((heads, low, lanes), f32)
    return pl.pallas_call(
        functools.partial(attention_backward_kernel, base=base, count=count, blk=blk, hd=hd, scale=scale, carried=carried, waits=len(wait)),
        grid_spec=pltpu.PrefetchScalarGridSpec(
            num_scalar_prefetch=1,
            grid=(count,),
            in_specs=[
                pl.BlockSpec((heads, blk, lanes), lambda i, t: (0, there(i), 0)),
                pl.BlockSpec((heads, high, lanes), lambda i, t: (0, 0, 0), **ONE),
                pl.BlockSpec((heads, high, lanes), lambda i, t: (0, 0, 0), **ONE),
                pl.BlockSpec((heads, lanes, high), lambda i, t: (0, 0, 0), **ONE),
                pl.BlockSpec((1, 1, blk), lambda i, t: (there(i), 0, 0)),
                pl.BlockSpec((heads, blk), lambda i, t: (0, here(i))),
                pl.BlockSpec((blk, heads * hd), lambda i, t: (here(i), 0)),
                pl.BlockSpec((blk, heads * hd), lambda i, t: (here(i), 0)),
                pl.BlockSpec((blk, lanes), lambda i, t: (there(i), 0)),
                pl.BlockSpec((blk, lanes), lambda i, t: (there(i), 0)),
                pl.BlockSpec((half, blk), lambda i, t: (0, there(i))),
                pl.BlockSpec((half, blk), lambda i, t: (0, there(i))),
                pl.BlockSpec(attn_in.shape, lambda i, t: (0, 0, 0), **ONE),
            ]
            + [pl.BlockSpec((heads, high, lanes), lambda i, t: (0, 0, 0), **ONE)] * (2 if carried else 0)
            + [ANY] * len(wait),
            out_specs=[pl.BlockSpec((3, blk, heads * hd), lambda i, t: (0, here(i), 0))]
            + [pl.BlockSpec((blk, attn_in.shape[1]), lambda i, t: (here(i), 0))] * 2
            + [pl.BlockSpec((heads, low, lanes), lambda i, t: (0, 0, 0), **ONE)] * (2 if base else 0),
            scratch_shapes=[
                pltpu.VMEM((heads, blk, lanes), bf16),
                pltpu.VMEM((heads, high, lanes), f32),
                pltpu.VMEM((heads, high, lanes), f32),
                pltpu.VMEM((heads * hd, blk), f32),
                pltpu.VMEM((pad_heads, blk), f32),
            ],
        ),
        out_shape=[
            jax.ShapeDtypeStruct((3, count * blk, heads * hd), bf16),
            jax.ShapeDtypeStruct((count * blk, attn_in.shape[1]), f32),
            jax.ShapeDtypeStruct((count * blk, attn_in.shape[1]), bf16),
        ]
        + [before] * (2 if base else 0),
        compiler_params=params(60),
        cost_estimate=COST,
        name="attention_backward",
    )(first, q3, k3, v3, kt, start_row, lse, attended, grad_att, cos, sin, cost, sint, attn_in, *(carry if carried else ()), *wait)


def mix_kernel(me_ref, own_ref, other_ref, gain_ref, *refs, base, own_blocks, parts, pieces, per):
    attended, refs = refs[: parts * pieces], refs[parts * pieces :]
    weights = refs[:parts]
    middle_ref, normed_ref = refs[-2:]
    i = pl.program_id(0)
    mine = (base + i) // own_blocks == me_ref[0]
    x = jnp.where(mine, own_ref[...].astype(f32), other_ref[...].astype(f32))
    for n in range(parts):
        a = attended[n * pieces][...]
        for k in range(1, pieces):
            a = jnp.where(i // per == k, attended[n * pieces + k][...], a)
        x = x + dot(a, weights[n][...])
    middle_ref[...] = x
    inverse = lax.rsqrt(jnp.mean(x * x, axis=-1, keepdims=True) + EPSILON)
    normed_ref[...] = (x * inverse * gain_ref[...]).astype(bf16)


def mix(me, low, bucket_rows, own_x, other_x, gain_row, attended, weights, before=None, wait=(), blk=BLK):
    own_rows, dim = own_x.shape
    own_blocks = own_rows // blk
    parts, pieces = len(attended), len(attended[0])
    per = attended[0][0].shape[0] // blk
    base, count = low // blk, pieces * per
    extra = () if before is None else tuple(before)
    at_x = lambda i, m: ((base + i) % own_blocks, 0)
    at = lambda i, m: (base + i, 0)
    return pl.pallas_call(
        functools.partial(mix_kernel, base=base, own_blocks=own_blocks, parts=parts, pieces=pieces, per=per),
        grid_spec=pltpu.PrefetchScalarGridSpec(
            num_scalar_prefetch=1,
            grid=(count,),
            in_specs=[
                pl.BlockSpec((blk, dim), at_x),
                pl.BlockSpec((blk, dim), at_x),
                pl.BlockSpec((1, dim), lambda i, m: (0, 0)),
            ]
            + [
                pl.BlockSpec((blk, a.shape[1]), lambda i, m, k=k: (jnp.clip(i - k * per, 0, per - 1), 0))
                for part in attended
                for k, a in enumerate(part)
            ]
            + [pl.BlockSpec(w.shape, lambda i, m: (0, 0), **ONE) for w in weights]
            + [ANY] * (len(extra) + len(wait)),
            out_specs=[pl.BlockSpec((blk, dim), at)] * 2,
        ),
        out_shape=[jax.ShapeDtypeStruct((bucket_rows, dim), f32), jax.ShapeDtypeStruct((bucket_rows, dim), bf16)],
        input_output_aliases={4 + parts * (pieces + 1) + n: n for n in range(len(extra))},
        compiler_params=params(48),
        name="mix",
    )(scalar(me), own_x, other_x, gain_row[None, :], *[a for part in attended for a in part], *weights, *extra, *wait)


def ff_forward_kernel(base_ref, x_ref, wg_ref, wu_ref, wo_ref, *refs, rc):
    out_ref, g_ref, u_ref, act_ref, acc_ref = refs[-5:]
    rows = x_ref.shape[0]

    @pl.when(pl.program_id(0) == 0)
    def _():
        acc_ref[...] = jnp.zeros_like(acc_ref)

    def by_rows(r, c):
        at = pl.ds(pl.multiple_of(r * rc, rc), rc)
        x = x_ref[at, :]
        g = dot(x, wg_ref[...])
        u = dot(x, wu_ref[...])
        g_ref[at, :] = g
        u_ref[at, :] = u
        act = (g * (1.0 / (1.0 + jnp.exp(-g))) * u).astype(bf16)
        act_ref[at, :] = act
        acc_ref[at, :] += dot(act, wo_ref[...])
        return c

    lax.fori_loop(0, rows // rc, by_rows, 0)

    @pl.when(pl.program_id(0) == pl.num_programs(0) - 1)
    def _():
        out_ref[...] = acc_ref[...].astype(out_ref.dtype)


def ff_forward(x, base, rows, mlp_in, mlp_out, dtype, wait=(), hb=512, rc=512):
    dim = x.shape[1]
    hidden = mlp_out.shape[0]
    hb = block_of(hidden, hb)
    rc = block_of(rows, rc)
    return pl.pallas_call(
        functools.partial(ff_forward_kernel, rc=rc),
        grid_spec=pltpu.PrefetchScalarGridSpec(
            num_scalar_prefetch=1,
            grid=(hidden // hb,),
            in_specs=[
                pl.BlockSpec((rows, dim), lambda h, b: (b[0], 0), **ONE),
                pl.BlockSpec((None, dim, hb), lambda h, b: (0, 0, h)),
                pl.BlockSpec((None, dim, hb), lambda h, b: (1, 0, h)),
                pl.BlockSpec((hb, dim), lambda h, b: (h, 0)),
            ]
            + [ANY] * len(wait),
            out_specs=[pl.BlockSpec((rows, dim), lambda h, b: (0, 0), **ONE)] + [pl.BlockSpec((rows, hb), lambda h, b: (0, h))] * 3,
            scratch_shapes=[pltpu.VMEM((rows, dim), f32)],
        ),
        out_shape=[jax.ShapeDtypeStruct((rows, dim), dtype)]
        + [jax.ShapeDtypeStruct((rows, hidden), f32)] * 2
        + [jax.ShapeDtypeStruct((rows, hidden), bf16)],
        compiler_params=params(60),
        cost_estimate=COST,
        name="ff_forward",
    )(scalar(base), x, mlp_in, mlp_in, mlp_out, *wait)


def ff_backward_kernel(og_ref, g_ref, u_ref, wg_ref, wu_ref, wo_ref, *refs, rc):
    gn_ref, gg_ref, gu_ref, acc_ref = refs[-4:]
    rows = og_ref.shape[0]

    @pl.when(pl.program_id(0) == 0)
    def _():
        acc_ref[...] = jnp.zeros_like(acc_ref)

    def by_rows(r, c):
        at = pl.ds(pl.multiple_of(r * rc, rc), rc)
        ga = dot(og_ref[at, :], wo_ref[...], NT)
        g = g_ref[at, :]
        s = 1.0 / (1.0 + jnp.exp(-g))
        silu = g * s
        gg = (ga * u_ref[at, :] * (s * (1.0 + g * (1.0 - s)))).astype(bf16)
        gu = (ga * silu).astype(bf16)
        gg_ref[at, :] = gg
        gu_ref[at, :] = gu
        acc_ref[at, :] += dot(gg, wg_ref[...], NT) + dot(gu, wu_ref[...], NT)
        return c

    lax.fori_loop(0, rows // rc, by_rows, 0)

    @pl.when(pl.program_id(0) == pl.num_programs(0) - 1)
    def _():
        gn_ref[...] = acc_ref[...].astype(gn_ref.dtype)


def ff_backward(og, g, u, mlp_in, mlp_out, dtype, wait=(), hb=512, rc=512):
    rows, dim = og.shape
    hidden = mlp_out.shape[0]
    hb = block_of(hidden, hb)
    rc = block_of(rows, rc)
    return pl.pallas_call(
        functools.partial(ff_backward_kernel, rc=rc),
        grid=(hidden // hb,),
        in_specs=[
            pl.BlockSpec((rows, dim), lambda h: (0, 0), **ONE),
            pl.BlockSpec((rows, hb), lambda h: (0, h)),
            pl.BlockSpec((rows, hb), lambda h: (0, h)),
            pl.BlockSpec((None, dim, hb), lambda h: (0, 0, h)),
            pl.BlockSpec((None, dim, hb), lambda h: (1, 0, h)),
            pl.BlockSpec((hb, dim), lambda h: (h, 0)),
        ]
        + [ANY] * len(wait),
        out_specs=[pl.BlockSpec((rows, dim), lambda h: (0, 0), **ONE)] + [pl.BlockSpec((rows, hb), lambda h: (0, h))] * 2,
        scratch_shapes=[pltpu.VMEM((rows, dim), f32)],
        out_shape=[jax.ShapeDtypeStruct((rows, dim), dtype)] + [jax.ShapeDtypeStruct((rows, hidden), bf16)] * 2,
        compiler_params=params(60),
        cost_estimate=COST,
        name="ff_backward",
    )(og, g, u, mlp_in, mlp_in, mlp_out, *wait)


def weights_kernel(base_ref, *refs, pieces, kinds, waits, cc):
    lhs, refs = refs[:pieces], refs[pieces:]
    rhs, refs = refs[: pieces * kinds], refs[pieces * kinds + waits :]
    out_ref, turned = refs[0], refs[1:]
    dim = lhs[0].shape[1]
    wide = out_ref.shape[1] // kinds

    @pl.when(pl.program_id(0) == 0)
    def _():
        for x_ref, t_ref in zip(lhs, turned):
            for k in range(0, x_ref.shape[0], 256):
                def turn(t, c, k=k, x_ref=x_ref, t_ref=t_ref):
                    at = pl.ds(pl.multiple_of(t * 256, 256), 256)
                    t_ref[at, k : k + 256] = x_ref[k : k + 256, at].T
                    return c
                lax.fori_loop(0, dim // 256, turn, 0)

    def by_columns(t, c):
        at = pl.ds(pl.multiple_of(t * cc, cc), cc)
        for kind in range(kinds):
            total = None
            for n, t_ref in enumerate(turned):
                part = dot(t_ref[at, :], rhs[n * kinds + kind][...])
                total = part if total is None else total + part
            out_ref[at, kind * wide : (kind + 1) * wide] = total.astype(bf16)
        return c

    lax.fori_loop(0, dim // cc, by_columns, 0)


def weight_gradient(base, lhs, lhs_maps, rows, rhs, hb, wait=(), cc=640):
    dim = lhs[0].shape[1]
    kinds = len(rhs[0])
    columns = rhs[0][0].shape[1]
    return pl.pallas_call(
        functools.partial(weights_kernel, pieces=len(lhs), kinds=kinds, waits=len(wait), cc=cc),
        grid_spec=pltpu.PrefetchScalarGridSpec(
            num_scalar_prefetch=1,
            grid=(columns // hb,),
            in_specs=[pl.BlockSpec((rows, dim), lambda h, b, m=m: (m(b), 0), **ONE) for m in lhs_maps]
            + [pl.BlockSpec((rows, hb), lambda h, b: (0, h)) for group in rhs for _ in group]
            + [ANY] * len(wait),
            out_specs=pl.BlockSpec((dim, kinds * hb), lambda h, b: (0, h)),
            scratch_shapes=[pltpu.VMEM((dim, rows), bf16) for _ in lhs],
        ),
        out_shape=jax.ShapeDtypeStruct((dim, kinds * columns), bf16),
        compiler_params=params(60),
        cost_estimate=COST,
        name="weight_gradient",
    )(scalar(base), *lhs, *[r for group in rhs for r in group], *wait)


def attn_weights_kernel(n_ref, *refs, lows, cc):
    parts, out_ref, turned = refs[: len(lows)], refs[-2], refs[-1]
    rows, dim = n_ref.shape

    @pl.when(pl.program_id(0) == 0)
    def _():
        for k in range(0, rows, 256):
            def turn(t, c, k=k):
                at = pl.ds(pl.multiple_of(t * 256, 256), 256)
                turned[at, k : k + 256] = n_ref[k : k + 256, at].T
                return c
            lax.fori_loop(0, dim // 256, turn, 0)

    def by_columns(t, c):
        at = pl.ds(pl.multiple_of(t * cc, cc), cc)
        total = None
        for low, g_ref in zip(lows, parts):
            part = dot(turned[at, low : low + g_ref.shape[0]], g_ref[...])
            total = part if total is None else total + part
        out_ref[at, :] = total.astype(bf16)
        return c

    lax.fori_loop(0, dim // cc, by_columns, 0)


def attn_weight_gradient(normed_one, lows, grad_qkv, wait=(), cc=640):
    rows, dim = normed_one.shape
    cols = grad_qkv[0].shape[2]
    return pl.pallas_call(
        functools.partial(attn_weights_kernel, lows=lows, cc=cc),
        grid=(3,),
        in_specs=[pl.BlockSpec((rows, dim), lambda j: (0, 0), **ONE)]
        + [pl.BlockSpec((None, g.shape[1], cols), lambda j: (j, 0, 0)) for g in grad_qkv]
        + [ANY] * len(wait),
        out_specs=pl.BlockSpec((dim, cols), lambda j: (0, j)) if cols % LANES == 0 else pl.BlockSpec((None, dim, cols), lambda j: (j, 0, 0)),
        scratch_shapes=[pltpu.VMEM((dim, rows), bf16)],
        out_shape=jax.ShapeDtypeStruct((dim, 3 * cols) if cols % LANES == 0 else (3, dim, cols), bf16),
        compiler_params=params(56),
        cost_estimate=COST,
        name="attn_weight_gradient",
    )(normed_one, *grad_qkv, *wait)


def norm_input_part(z, gain, e):
    inverse = lax.rsqrt(jnp.mean(z * z, axis=-1, keepdims=True) + EPSILON)
    weighted = e * gain
    inner = jnp.mean(weighted * z, axis=-1, keepdims=True)
    return weighted * inverse - z * (inverse * inverse * inverse) * inner


def chosen(i, refs, per):
    value = refs[0][...]
    for k in range(1, len(refs)):
        value = jnp.where(i // per == k, refs[k][...], value)
    return value


def in_turn(count, per, blk, wide):
    return [pl.BlockSpec((blk, wide), lambda i, m, k=k: (jnp.clip(i - k * per, 0, per - 1), 0)) for k in range(count)]


def middle_backward_kernel(me_ref, og_ref, z_ref, own_ref, gain_ref, *refs, pieces, per, parts):
    got, refs = refs[:pieces], refs[pieces:]
    weights, refs = refs[:parts], refs[-2 - parts :]
    i = pl.program_id(0)
    e = own_ref[...]
    if pieces:
        e = e + chosen(i, got, per).astype(f32)
    grad = og_ref[...].astype(f32) + norm_input_part(z_ref[...], gain_ref[...], e)
    refs[0][...] = grad
    branch = grad.astype(bf16)
    refs[1][...] = branch
    for w, out in zip(weights, refs[2:]):
        out[...] = dot(branch, w[...], NT).astype(bf16)


def middle_backward(me, out_grad, middle, gn_own, got_gn, gain_row, weights, wait=(), blk=BLK):
    rows, dim = out_grad.shape
    pieces = len(got_gn)
    per = got_gn[0].shape[0] // blk if pieces else 1
    own_blocks = rows // blk
    at = lambda i, m: (i, 0)
    return pl.pallas_call(
        functools.partial(middle_backward_kernel, pieces=pieces, per=per, parts=len(weights)),
        grid_spec=pltpu.PrefetchScalarGridSpec(
            num_scalar_prefetch=1,
            grid=(own_blocks,),
            in_specs=[
                pl.BlockSpec((blk, dim), at),
                pl.BlockSpec((blk, dim), lambda i, m: (m[0] * own_blocks + i, 0)),
                pl.BlockSpec((blk, dim), at),
                pl.BlockSpec((1, dim), lambda i, m: (0, 0)),
            ]
            + in_turn(pieces, per, blk, dim)
            + [pl.BlockSpec(w.shape, lambda i, m: (0, 0), **ONE) for w in weights]
            + [ANY] * len(wait),
            out_specs=[pl.BlockSpec((blk, dim), at)] * 2 + [pl.BlockSpec((blk, w.shape[0]), at) for w in weights],
        ),
        out_shape=[jax.ShapeDtypeStruct((rows, dim), f32), jax.ShapeDtypeStruct((rows, dim), bf16)]
        + [jax.ShapeDtypeStruct((rows, w.shape[0]), bf16) for w in weights],
        compiler_params=params(48),
        cost_estimate=COST,
        name="middle_backward",
    )(scalar(me), out_grad, middle, gn_own, gain_row[None, :], *got_gn, *weights, *wait)


def tokens_backward_kernel(me_ref, x_ref, grad_ref, gain_ref, *refs, sides):
    i = pl.program_id(0)
    out_ref, refs = refs[-1], refs[:-1]
    e = None
    for n, ((count, each), (more, every)) in enumerate(sides):
        own, got, refs = refs[:count], refs[count : count + more], refs[count + more :]
        here = chosen(i, own, each) + chosen(i, got, every).astype(f32)
        e = here if e is None else jnp.where(me_ref[0] == n, here, e)
    out_ref[...] = (grad_ref[...] + norm_input_part(x_ref[...].astype(f32), gain_ref[...], e)).astype(bf16)


def tokens_backward(me, tokens, grad_middle, gain_row, sides, blk=BLK):
    rows, dim = tokens.shape
    at = lambda i, m: (i, 0)
    shape = tuple(tuple((len(part), part[0].shape[0] // blk) for part in side) for side in sides)
    specs = [spec for side in shape for part in side for spec in in_turn(*part, blk, dim)]
    return pl.pallas_call(
        functools.partial(tokens_backward_kernel, sides=shape),
        grid_spec=pltpu.PrefetchScalarGridSpec(
            num_scalar_prefetch=1,
            grid=(rows // blk,),
            in_specs=[pl.BlockSpec((blk, dim), at), pl.BlockSpec((blk, dim), at), pl.BlockSpec((1, dim), lambda i, m: (0, 0))] + specs,
            out_specs=pl.BlockSpec((blk, dim), at),
        ),
        out_shape=jax.ShapeDtypeStruct((rows, dim), bf16),
        compiler_params=params(48),
        cost_estimate=COST,
        name="tokens_backward",
    )(scalar(me), tokens, grad_middle, gain_row[None, :], *[a for own, got in sides for a in (*own, *got)])


def contract(a, b, dims):
    return lax.dot_general(a, b, (dims, ((), ())), preferred_element_type=f32)


def after(value, *others):
    return lax.optimization_barrier((value, *others))[0]


SWAP = ((0, 1), (1, 0))


def halving_start(array, group, n_dp):
    rows = array.shape[0] // n_dp
    shaped = array.reshape((n_dp // 2, 2, rows) + array.shape[1:])
    return halving_split(0, shaped, None, group)


def halving_split(bit, kept, got, group):
    side = (group >> bit) & 1
    def pick(at):
        part = lax.dynamic_index_in_dim(kept, at, 1, False)
        if got is None:
            return part
        return (part.astype(f32) + lax.dynamic_index_in_dim(got, at, 1, False).astype(f32)).astype(bf16)
    return bit, pick(1 - side), pick(side)


def halving_step(state, group, n_dp, behind):
    bit, send, keep = state
    got = lax.ppermute(send, "dp", [(n, n ^ (1 << bit)) for n in range(n_dp)])
    keep, behind = lax.optimization_barrier((keep, behind))
    if keep.shape[0] == 1:
        return (bit + 1, keep, got), behind
    split = lambda a: a.reshape((a.shape[0] // 2, 2) + a.shape[1:])
    return halving_split(bit + 1, split(keep), split(got), group), behind


def halving_end(state):
    _, keep, got = state
    return (keep.astype(f32) + got.astype(f32))[0]


def per_device(tokens, norm_gains, attn_in, attn_out, mlp_in, mlp_out, lengths, out_grad):
    n_mp = lax.axis_size("mp")
    n_dp = lax.axis_size("dp")
    me = lax.axis_index("mp")
    group = lax.axis_index("dp")
    rows, dim = tokens.shape
    bucket = rows * n_mp
    hd = HEAD_DIM
    cols = attn_out.shape[0]
    hidden = mlp_out.shape[0]
    share = dim // n_dp
    scale = hd**-0.5
    pair = n_mp == 2
    hb = block_of(hidden, 512)
    places, starts = layout(lengths[0], bucket)
    tables = turning(places - starts, hd)
    cos, sin = tables[:2]
    first = starts[::BLK] // BLK
    start_row = starts.reshape(bucket // BLK, 1, BLK)
    own_blocks = rows // BLK

    def mine(array, axis, size):
        return lax.dynamic_slice_in_dim(array, group * size, size, axis)

    def swap(array):
        return lax.ppermute(array, "mp", SWAP)

    def scatter(array):
        return lax.psum_scatter(array, "dp", scatter_dimension=0, tiled=True)

    if pair:
        piece = swap(mine(attn_out, 0, cols // n_dp))
        other_attn_out = lax.all_gather(piece, "dp", axis=0, tiled=True)
        other_x = swap(tokens)
        half_done = project(tokens, me * own_blocks, bucket, norm_gains[0], attn_in, cos, sin, hd, wait=(piece,))
        normed_one, q3, k3, v3, kt, vt = project(
            other_x, (1 - me) * own_blocks, bucket, norm_gains[0], attn_in, cos, sin, hd, half_done
        )
        chunk = rows // 2
        att, lse, att_got = [], [], []
        for n, low in enumerate(range(0, bucket, chunk)):
            wait = tuple(att_got[n - 2 : n - 1]) if n > 1 else ()
            if n == 1:
                wait = (other_attn_out,)
            a, l = attention_forward(first, low, low + chunk, q3, k3, vt, start_row, hd, scale, tuple(att[-1:]) + wait)
            att.append(a)
            lse.append(l)
            att_got.append(swap(a))
        grad_tied, att_got[2], att_got[3] = lax.optimization_barrier((out_grad, att_got[2], att_got[3]))
        mix_rows = lambda low, these, before: mix(
            me, low, bucket, tokens, other_x, norm_gains[1], (att[these], att_got[these]), (attn_out, other_attn_out), before
        )
        middle_all, normed_two = mix_rows(3 * chunk, slice(3, 4), mix_rows(0, slice(0, 3), None))
        other = 1 - me
        got_grad = [swap(grad_tied[low : low + chunk]) for low in (0, chunk)]
        out_b, g_b, u_b, act_b = ff_forward(normed_two, other, rows, mlp_in, mlp_out, bf16)
        out_a, g_a, u_a, act_a = ff_forward(normed_two, me, rows, mlp_in, mlp_out, f32, wait=(act_b, got_grad[0]))
        other_grad = jnp.concatenate(got_grad)
        gw_out = weight_gradient(
            0, (other_grad, out_grad), (lambda b: 0, lambda b: 0), rows, ((act_b,), (act_a,)), hb, wait=(out_a,)
        )
        sum_out = scatter(gw_out)
        gn_b, gg_b, gu_b = ff_backward(other_grad, g_b, u_b, mlp_in, mlp_out, bf16, wait=(gw_out,))
        got_gn = [swap(gn_b[low : low + chunk]) for low in (0, chunk)]
        gn_a, gg_a, gu_a = ff_backward(out_grad, g_a, u_a, mlp_in, mlp_out, f32, wait=(gn_b,))
        gate_up = (normed_two, normed_two), (lambda b: 1 - b[0], lambda b: b[0]), rows
        gw_gate = weight_gradient(me, *gate_up, ((gg_b,), (gg_a,)), hb, wait=(gn_a, got_gn[0]))
        sum_gate = scatter(gw_gate)
        grad_middle, branch_grad, do_own, do_send = middle_backward(
            me, out_grad, middle_all, gn_a, got_gn, norm_gains[1], (attn_out, other_attn_out), wait=(gw_gate,)
        )
    else:
        all_x = lax.all_gather(tokens, "mp", axis=0, tiled=True)
        normed_one, q3, k3, v3, kt, vt = project(all_x, 0, bucket, norm_gains[0], attn_in, cos, sin, hd)
        att_all, lse_all = attention_forward(first, 0, bucket, q3, k3, vt, start_row, hd, scale)
        every_head = lax.all_gather(att_all, "mp", axis=1, tiled=True)
        every_out = lax.all_gather(attn_out, "mp", axis=0, tiled=True)
        middle_all, normed_two = mix(0, 0, bucket, all_x, all_x, norm_gains[1], ((every_head,),), (every_out,))
        all_grad = lax.all_gather(out_grad, "mp", axis=0, tiled=True)
        out_b, g_b, u_b, act_b = ff_forward(normed_two, 0, bucket, mlp_in, mlp_out, bf16)
        gn_b, gg_b, gu_b = ff_backward(all_grad, g_b, u_b, mlp_in, mlp_out, bf16)
        gw_out = weight_gradient(0, (all_grad,), (lambda b: 0,), bucket, ((act_b,),), hb)
        sum_out = scatter(gw_out)
        sum_gate = scatter(weight_gradient(0, (normed_two,), (lambda b: 0,), bucket, ((gg_b,),), hb))
        sum_up = scatter(weight_gradient(0, (normed_two,), (lambda b: 0,), bucket, ((gu_b,),), hb))
        grad_normed_two = lax.psum_scatter(gn_b, "mp", scatter_dimension=0, tiled=True).astype(f32)
        grad_middle, branch_grad = middle_backward(me, out_grad, middle_all, grad_normed_two, (), norm_gains[1], ())
        middle = lax.dynamic_slice_in_dim(middle_all, me * rows, rows, 0)
        output = (middle + lax.psum_scatter(out_b, "mp", scatter_dimension=0, tiled=True).astype(f32)).astype(bf16)
    if pair:
        do_got = swap(do_send)
        gw_up = weight_gradient(me, *gate_up, ((gu_b,), (gu_a,)), hb, wait=(do_send,))
        out_b, gw_up = lax.optimization_barrier((out_b, gw_up))
        att_own = jnp.where(me == 0, jnp.concatenate(att[:2]), jnp.concatenate(att[2:]))
        att_other = jnp.where(me == 0, jnp.concatenate(att_got[:2]), jnp.concatenate(att_got[2:]))
        gw_attn_out = jnp.concatenate(
            [contract(branch_grad, a, ((0,), (0,))).astype(bf16) for a in (att_own, att_other)], axis=1
        )
        up = halving_start(gw_up, group, n_dp)
        up, gw_attn_out = halving_step(up, group, n_dp, gw_attn_out)
        sum_attn_out = scatter(gw_attn_out)
        got_out = [swap(out_b[low : low + chunk]) for low in (0, chunk)]
        do_low = jnp.where(me == 0, do_own, do_got)
        do_high = jnp.where(me == 0, do_got, do_own)
        grad_att = {0: do_low[:chunk], chunk: do_low[chunk:], rows: do_high}
        lse_of = {0: lse[0], chunk: lse[1], rows: jnp.concatenate(lse[2:], axis=1)}
        att_of = {0: att[0], chunk: att[1], rows: jnp.concatenate(att[2:], axis=0)}
        carry, grad_qkv, own_part, got_part = None, {}, {}, {}
        for low, high in ((rows, bucket), (chunk, rows), (0, chunk)):
            wait = {rows: (sum_out,), chunk: (sum_gate, got_out[0]), 0: (got_out[1],) + tuple(got_part.get(rows, ())[:1])}[low]
            made = attention_backward(
                first, low, high, q3, k3, v3, kt, start_row, lse_of[low], att_of[low], grad_att[low], tables, attn_in, hd, scale,
                carry, wait + (up[1],),
            )
            own_part[low], send, carry = made[1], made[2], made[3:]
            up, grad_qkv[low] = halving_step(up, group, n_dp, made[0])
            path = ((0, 1),) if low == rows else ((1, 0),)
            got_part[low] = [lax.ppermute(send[n : n + chunk], "mp", path) for n in range(0, high - low, chunk)]
        grad_tokens = tokens_backward(
            me,
            tokens,
            grad_middle,
            norm_gains[0],
            (([own_part[0], own_part[chunk]], got_part[0] + got_part[chunk]), ([own_part[rows]], got_part[rows])),
        )
        lows = (0, chunk, rows)
        gw_attn_in = attn_weight_gradient(normed_one, lows, [grad_qkv[low] for low in lows], wait=(sum_attn_out, got_part[rows][1], got_part[chunk][0]))
        sum_up = halving_end(up)
    else:
        all_branch = lax.all_gather(branch_grad, "mp", axis=0, tiled=True)
        grad_heads = contract(all_branch, attn_out, ((1,), (1,))).astype(bf16)
        gw_attn_out = contract(all_branch, att_all, ((0,), (0,))).astype(bf16)
        made = attention_backward(
            first, 0, bucket, q3, k3, v3, kt, start_row, lse_all, att_all, grad_heads, tables, attn_in, hd, scale, None
        )
        grad_qkv, grad_normed_one = made[0], lax.psum_scatter(made[2], "mp", scatter_dimension=0, tiled=True)
        nothing = jnp.zeros((rows, dim), f32)
        grad_tokens = tokens_backward(0, tokens, grad_middle, norm_gains[0], (((nothing,), (grad_normed_one,)),))
        gw_attn_in = attn_weight_gradient(normed_one, (0,), [grad_qkv])
        if gw_attn_in.ndim == 3:
            gw_attn_in = gw_attn_in.transpose(1, 0, 2).reshape(dim, 3 * cols)
    if pair:
        middle = lax.dynamic_slice_in_dim(middle_all, me * rows, rows, 0)
        output = (middle + (out_a + jnp.concatenate(got_out).astype(f32))).astype(bf16)
    sum_in = jnp.stack([sum_gate.astype(f32), sum_up.astype(f32)])
    sum_out = sum_out.astype(f32)
    if not pair:
        sum_attn_out = scatter(gw_attn_out)
    sum_attn_out = sum_attn_out.astype(f32)
    if pair:
        sum_attn_out = sum_attn_out[:, :cols] + swap(sum_attn_out[:, cols:].astype(bf16)).astype(f32)
    sum_attn_in = scatter(gw_attn_in).astype(f32).reshape(share, 3, cols).transpose(1, 0, 2)
    gain_one = jnp.sum(mine(attn_in, 1, share).astype(f32) * sum_attn_in, axis=(0, 2))
    gain_two = jnp.sum(mine(mlp_in, 1, share).astype(f32) * sum_in, axis=(0, 2))
    gains = jnp.stack([gain_one, gain_two]) / mine(norm_gains, 1, share)
    if pair:
        halves = gains.reshape(2, 2, share // 2)
        gains = lax.dynamic_index_in_dim(halves, me, 1, False) + swap(lax.dynamic_index_in_dim(halves, 1 - me, 1, False))
    else:
        gains = lax.psum_scatter(gains, "mp", scatter_dimension=1, tiled=True)
    return (output, grad_tokens, gains, sum_attn_in, sum_attn_out.T, sum_in, sum_out.T)


def solution(mesh):
    placed = (
        P(("dp", "mp"), None),
        P(),
        P(None, None, "mp"),
        P("mp", None),
        P(None, None, "mp"),
        P("mp", None),
        P("dp", None),
        P(("dp", "mp"), None),
    )
    return jax.shard_map(
        per_device,
        mesh=mesh,
        in_specs=placed,
        out_specs=(
            P(("dp", "mp"), None),
            P(("dp", "mp"), None),
            P(None, ("dp", "mp")),
            P(None, "dp", "mp"),
            P("mp", "dp"),
            P(None, "dp", "mp"),
            P("mp", "dp"),
        ),
        check_vma=False,
    )
```

```python
import functools

import jax
import jax.numpy as jnp
from jax import lax
from jax.experimental import pallas as pl
from jax.experimental.pallas import tpu as pltpu
from jax.sharding import PartitionSpec as P

BLK = 256
LANES = 128
HEAD_DIM = 80
EPSILON = 1e-06
LOG2E = 1.4426950408889634
NEG = -1e30
bf16 = jnp.bfloat16
f32 = jnp.float32
NT = (((1,), (1,)), ((), ()))
NN = (((1,), (0,)), ((), ()))
ONE = dict(pipeline_mode=pl.Buffered(1))


def dot(a, b, contract=NN):
    return lax.dot_general(a, b, contract, preferred_element_type=f32)


COST = pl.CostEstimate(flops=40_000_000_000, bytes_accessed=20_000_000, transcendentals=0)
ANY = pl.BlockSpec(memory_space=pl.ANY)


def params(mib):
    return pltpu.CompilerParams(vmem_limit_bytes=mib << 20)


def block_of(size, most):
    return next(b for b in (most, 1024, 512, 256, 128) if b <= most and size % b == 0)


def scalar(value):
    return jnp.reshape(value, (1,)).astype(jnp.int32)


def chosen(i, refs, per):
    value = refs[0][...]
    for k in range(1, len(refs)):
        value = jnp.where(i // per == k, refs[k][...], value)
    return value


def in_turn(count, per, blk, wide):
    return [pl.BlockSpec((blk, wide), lambda i, m, k=k: (jnp.clip(i - k * per, 0, per - 1), 0)) for k in range(count)]


def layout(lengths_row, bucket_rows):
    series_ends = jnp.cumsum(lengths_row, dtype=jnp.int32)
    places = jnp.arange(bucket_rows, dtype=jnp.int32)
    before = series_ends[None, :] <= places[:, None]
    starts = jnp.sum(jnp.where(before, lengths_row[None, :], 0), axis=1, dtype=jnp.int32)
    return places, starts


def turning(position, hd):
    half = hd // 2
    frequency = 10000.0 ** (-(jnp.arange(half, dtype=f32) * 2.0 / hd))
    place = position.astype(f32)
    turned = frequency[:, None] * place[None, :]
    wide = jnp.concatenate([frequency, frequency, jnp.zeros((LANES - hd,), f32)])
    angles = place[:, None] * wide[None, :]
    return jnp.cos(angles), jnp.sin(angles), jnp.cos(turned), jnp.sin(turned)


def project_kernel(base_ref, x_ref, gain_ref, w_ref, cos_ref, sin_ref, *refs, hd):
    n_ref, q_ref, k_ref, v_ref, kt_ref, vt_ref = refs[-6:]
    heads, rows, lanes = q_ref.shape
    half = hd // 2
    x = x_ref[...].astype(f32)
    inverse = lax.rsqrt(jnp.mean(x * x, axis=-1, keepdims=True) + EPSILON)
    normed = (x * inverse * gain_ref[...]).astype(bf16)
    n_ref[...] = normed
    cos, sin = cos_ref[...], sin_ref[...]
    lane = lax.broadcasted_iota(jnp.int32, (rows, lanes), 1)
    pad = jnp.zeros((rows, lanes - hd), f32)
    for j, out in enumerate((q_ref, k_ref, v_ref)):
        y = dot(normed, w_ref[j])
        for h in range(heads):
            part = jnp.concatenate([y[:, h * hd : (h + 1) * hd], pad], axis=1)
            if j < 2:
                other = jnp.where(lane < half, -pltpu.roll(part, lanes - half, 1), pltpu.roll(part, half, 1))
                part = part * cos + other * sin
                part = jnp.where(lane < hd, part, 0.0)
            part = part.astype(bf16)
            out[h] = part
            if j == 1:
                kt_ref[h] = part.T
            if j == 2:
                vt_ref[h] = part.T


def project(x, base, bucket_rows, gain_row, attn_in, cos, sin, hd, before=None, wait=(), blk=BLK):
    rows, dim = x.shape
    heads = attn_in.shape[2] // hd
    at = lambda i, b: (b[0] + i, 0)
    at_heads = lambda i, b: (0, b[0] + i, 0)
    at_turned = lambda i, b: (0, 0, b[0] + i)
    extra = () if before is None else tuple(before)
    return pl.pallas_call(
        functools.partial(project_kernel, hd=hd),
        grid_spec=pltpu.PrefetchScalarGridSpec(
            num_scalar_prefetch=1,
            grid=(rows // blk,),
            in_specs=[
                pl.BlockSpec((blk, dim), lambda i, b: (i, 0)),
                pl.BlockSpec((1, dim), lambda i, b: (0, 0)),
                pl.BlockSpec(attn_in.shape, lambda i, b: (0, 0, 0), **ONE),
                pl.BlockSpec((blk, LANES), at),
                pl.BlockSpec((blk, LANES), at),
            ]
            + [ANY] * (len(extra) + len(wait)),
            out_specs=[pl.BlockSpec((blk, dim), at)]
            + [pl.BlockSpec((heads, blk, LANES), at_heads)] * 3
            + [pl.BlockSpec((heads, LANES, blk), at_turned)] * 2,
        ),
        out_shape=[jax.ShapeDtypeStruct((bucket_rows, dim), bf16)]
        + [jax.ShapeDtypeStruct((heads, bucket_rows, LANES), bf16)] * 3
        + [jax.ShapeDtypeStruct((heads, LANES, bucket_rows), bf16)] * 2,
        input_output_aliases={6 + n: n for n in range(len(extra))},
        compiler_params=params(56),
        cost_estimate=COST,
        name="project",
    )(scalar(base), x, gain_row[None, :], attn_in, cos, sin, *extra, *wait)


def allowed_mask(j, i, start_row, blk):
    kpos = j * blk + lax.broadcasted_iota(jnp.int32, (blk, blk), 0)
    qpos = i * blk + lax.broadcasted_iota(jnp.int32, (blk, blk), 1)
    return (kpos >= start_row) & (kpos <= qpos)


def attention_forward_kernel(first_ref, q_ref, k_ref, vt_ref, start_ref, *refs, base, blk, hd, scale):
    o_ref, lse_ref, acc_ref, m_ref, l_ref = refs[-5:]
    heads = k_ref.shape[0]
    i = base + pl.program_id(0)
    acc_ref[...] = jnp.zeros_like(acc_ref)
    m_ref[...] = jnp.full_like(m_ref, NEG)
    l_ref[...] = jnp.zeros_like(l_ref)
    c2 = scale * LOG2E

    def step(j, carry):
        mask = allowed_mask(j, i, start_ref[0], blk)
        rows = pl.ds(pl.multiple_of(j * blk, blk), blk)
        for h in range(heads):
            s = dot(k_ref[h, rows, :], q_ref[h], NT)
            s = jnp.where(mask, s * c2, NEG)
            m_old = m_ref[h : h + 1]
            m_new = jnp.maximum(m_old, jnp.max(s, axis=0, keepdims=True))
            alpha = jnp.exp2(m_old - m_new)
            p = jnp.exp2(s - m_new)
            l_ref[h : h + 1] = alpha * l_ref[h : h + 1] + jnp.sum(p, axis=0, keepdims=True)
            m_ref[h : h + 1] = m_new
            part = slice(h * hd, (h + 1) * hd)
            acc_ref[part, :] = alpha * acc_ref[part, :] + dot(vt_ref[h, :hd, rows], p.astype(bf16))
        return carry

    step(i, 0)
    lax.fori_loop(first_ref[i], i, step, 0)
    for h in range(heads):
        part = slice(h * hd, (h + 1) * hd)
        acc_ref[part, :] = acc_ref[part, :] / l_ref[h : h + 1]
    o_ref[...] = acc_ref[...].T.astype(bf16)
    lse_ref[...] = m_ref[...] + jnp.log2(l_ref[...])


def attention_forward(first, low, high, q3, k3, vt, start_row, hd, scale, wait=(), blk=BLK):
    heads, rows, lanes = k3.shape
    base, count = low // blk, (high - low) // blk
    return pl.pallas_call(
        functools.partial(attention_forward_kernel, base=base, blk=blk, hd=hd, scale=scale),
        grid_spec=pltpu.PrefetchScalarGridSpec(
            num_scalar_prefetch=1,
            grid=(count,),
            in_specs=[
                pl.BlockSpec((heads, blk, lanes), lambda i, t: (0, i + base, 0)),
                pl.BlockSpec((heads, high, lanes), lambda i, t: (0, 0, 0), **ONE),
                pl.BlockSpec((heads, lanes, high), lambda i, t: (0, 0, 0), **ONE),
                pl.BlockSpec((1, 1, blk), lambda i, t: (i + base, 0, 0)),
            ]
            + [ANY] * len(wait),
            out_specs=[
                pl.BlockSpec((blk, heads * hd), lambda i, t: (i, 0)),
                pl.BlockSpec((heads, blk), lambda i, t: (0, i)),
            ],
            scratch_shapes=[
                pltpu.VMEM((heads * hd, blk), f32),
                pltpu.VMEM((heads, blk), f32),
                pltpu.VMEM((heads, blk), f32),
            ],
        ),
        out_shape=[
            jax.ShapeDtypeStruct((count * blk, heads * hd), bf16),
            jax.ShapeDtypeStruct((heads, count * blk), f32),
        ],
        compiler_params=params(56),
        cost_estimate=COST,
        name="attention_forward",
    )(first, q3, k3, vt, start_row, *wait)


def attention_backward_kernel(
    first_ref, q_ref, k_ref, v_ref, kt_ref, start_ref, lse_ref, o_ref, do_ref, cos_ref, sin_ref, cost_ref, sint_ref, w_ref, *refs,
    base, count, blk, hd, scale, carried, waits, outs,
):
    carry_in, refs = (refs[:2], refs[2:]) if carried else ((), refs)
    refs = refs[waits:]
    g_ref, wide_ref, narrow, refs = *refs[:2], refs[2 : 2 + outs], refs[2 + outs :]
    carry_out, refs = (refs[:2], refs[2:]) if base else ((), refs)
    do3_ref, dk_ref, dv_ref, dqt_ref, d_ref = refs
    heads, rows, lanes = k_ref.shape
    half = hd // 2
    step_at = pl.program_id(0)
    i = base + count - 1 - step_at

    @pl.when(step_at == 0)
    def _():
        do3_ref[...] = jnp.zeros_like(do3_ref)
        if carried:
            dk_ref[...] = carry_in[0][...]
            dv_ref[...] = carry_in[1][...]
        else:
            dk_ref[...] = jnp.zeros_like(dk_ref)
            dv_ref[...] = jnp.zeros_like(dv_ref)

    for h in range(heads):
        do3_ref[h, :, :hd] = do_ref[:, h * hd : (h + 1) * hd]
    prod = do_ref[...].astype(f32) * o_ref[...].astype(f32)
    high = prod.astype(bf16)
    low = (prod - high.astype(f32)).astype(bf16)
    pad_heads = d_ref.shape[0]
    owner = lax.broadcasted_iota(jnp.int32, (pad_heads, heads * hd), 1) // hd
    pick = (owner == lax.broadcasted_iota(jnp.int32, (pad_heads, heads * hd), 0)).astype(f32).astype(bf16)
    d_ref[...] = dot(pick, high, NT) + dot(pick, low, NT)
    dqt_ref[...] = jnp.zeros_like(dqt_ref)
    c2 = scale * LOG2E

    def step(j, carry):
        mask = allowed_mask(j, i, start_ref[0], blk)
        at = pl.ds(pl.multiple_of(j * blk, blk), blk)
        for h in range(heads):
            q = q_ref[h]
            do = do3_ref[h]
            s = dot(k_ref[h, at, :], q, NT)
            p = jnp.where(mask, jnp.exp2(s * c2 - lse_ref[h : h + 1]), 0.0)
            dp = dot(v_ref[h, at, :], do, NT)
            ds = (p * (dp - d_ref[h : h + 1])).astype(bf16)
            dv_ref[h, at, :] += dot(p.astype(bf16), do)
            dk_ref[h, at, :] += dot(ds, q)
            part = slice(h * hd, (h + 1) * hd)
            dqt_ref[part, :] += dot(kt_ref[h, :hd, at], ds)
        return carry

    lax.fori_loop(first_ref[i], i + 1, step, 0)
    ct = cost_ref[...]
    st = sint_ref[...]
    for h in range(heads):
        a = dqt_ref[h * hd : h * hd + half, :] * scale
        b = dqt_ref[h * hd + half : (h + 1) * hd, :] * scale
        dqt_ref[h * hd : h * hd + half, :] = a * ct + b * st
        dqt_ref[h * hd + half : (h + 1) * hd, :] = b * ct - a * st
    g_ref[0] = dqt_ref[...].T.astype(bf16)
    at = pl.ds(pl.multiple_of(i * blk, blk), blk)
    cos, sin = cos_ref[...], sin_ref[...]
    lane = lax.broadcasted_iota(jnp.int32, (blk, lanes), 1)
    for h in range(heads):
        x = dk_ref[h, at, :] * scale
        other = jnp.where(lane < half, pltpu.roll(x, lanes - half, 1), -pltpu.roll(x, half, 1))
        g_ref[1, :, h * hd : (h + 1) * hd] = (x * cos + other * sin).astype(bf16)[:, :hd]
        g_ref[2, :, h * hd : (h + 1) * hd] = dv_ref[h, at, :].astype(bf16)[:, :hd]
    total = dot(g_ref[0], w_ref[0], NT) + dot(g_ref[1], w_ref[1], NT) + dot(g_ref[2], w_ref[2], NT)
    wide_ref[...] = total
    for n in range(outs):

        @pl.when((i - base) // (count // outs) == n)
        def _():
            narrow[n][...] = total.astype(bf16)
    if base:

        @pl.when(step_at == count - 1)
        def _():
            carry_out[0][...] = dk_ref[:, : base * blk, :]
            carry_out[1][...] = dv_ref[:, : base * blk, :]


def attention_backward(first, low, high, q3, k3, v3, kt, start_row, lse, attended, grad_att, tables, attn_in, hd, scale, carry, outs=1, wait=(), blk=BLK):
    heads, rows, lanes = k3.shape
    base, count = low // blk, (high - low) // blk
    cos, sin, cost, sint = tables
    pad_heads = max(8, heads)
    half = hd // 2
    here = lambda i: count - 1 - i
    there = lambda i: base + count - 1 - i
    carried = carry is not None
    before = jax.ShapeDtypeStruct((heads, low, lanes), f32)
    return pl.pallas_call(
        functools.partial(attention_backward_kernel, base=base, count=count, blk=blk, hd=hd, scale=scale, carried=carried, waits=len(wait), outs=outs),
        grid_spec=pltpu.PrefetchScalarGridSpec(
            num_scalar_prefetch=1,
            grid=(count,),
            in_specs=[
                pl.BlockSpec((heads, blk, lanes), lambda i, t: (0, there(i), 0)),
                pl.BlockSpec((heads, high, lanes), lambda i, t: (0, 0, 0), **ONE),
                pl.BlockSpec((heads, high, lanes), lambda i, t: (0, 0, 0), **ONE),
                pl.BlockSpec((heads, lanes, high), lambda i, t: (0, 0, 0), **ONE),
                pl.BlockSpec((1, 1, blk), lambda i, t: (there(i), 0, 0)),
                pl.BlockSpec((heads, blk), lambda i, t: (0, here(i))),
                pl.BlockSpec((blk, heads * hd), lambda i, t: (here(i), 0)),
                pl.BlockSpec((blk, heads * hd), lambda i, t: (here(i), 0)),
                pl.BlockSpec((blk, lanes), lambda i, t: (there(i), 0)),
                pl.BlockSpec((blk, lanes), lambda i, t: (there(i), 0)),
                pl.BlockSpec((half, blk), lambda i, t: (0, there(i))),
                pl.BlockSpec((half, blk), lambda i, t: (0, there(i))),
                pl.BlockSpec(attn_in.shape, lambda i, t: (0, 0, 0), **ONE),
            ]
            + [pl.BlockSpec((heads, high, lanes), lambda i, t: (0, 0, 0), **ONE)] * (2 if carried else 0)
            + [ANY] * len(wait),
            out_specs=[pl.BlockSpec((3, blk, heads * hd), lambda i, t: (0, here(i), 0))]
            + [pl.BlockSpec((blk, attn_in.shape[1]), lambda i, t: (here(i), 0))]
            + [
                pl.BlockSpec((blk, attn_in.shape[1]), lambda i, t, k=k, n=count // outs: (jnp.clip(here(i) - k * n, 0, n - 1), 0))
                for k in range(outs)
            ]
            + [pl.BlockSpec((heads, low, lanes), lambda i, t: (0, 0, 0), **ONE)] * (2 if base else 0),
            scratch_shapes=[
                pltpu.VMEM((heads, blk, lanes), bf16),
                pltpu.VMEM((heads, high, lanes), f32),
                pltpu.VMEM((heads, high, lanes), f32),
                pltpu.VMEM((heads * hd, blk), f32),
                pltpu.VMEM((pad_heads, blk), f32),
            ],
        ),
        out_shape=[
            jax.ShapeDtypeStruct((3, count * blk, heads * hd), bf16),
            jax.ShapeDtypeStruct((count * blk, attn_in.shape[1]), f32),
        ]
        + [jax.ShapeDtypeStruct((count * blk // outs, attn_in.shape[1]), bf16)] * outs
        + [before] * (2 if base else 0),
        compiler_params=params(60),
        cost_estimate=COST,
        name="attention_backward",
    )(first, q3, k3, v3, kt, start_row, lse, attended, grad_att, cos, sin, cost, sint, attn_in, *(carry if carried else ()), *wait)


def mix_kernel(me_ref, own_ref, gain_ref, *refs, base, own_blocks, others, parts, pieces, per):
    other, refs = refs[:others], refs[others:]
    attended, refs = refs[: parts * pieces], refs[parts * pieces :]
    weights = refs[:parts]
    middle_ref, normed_ref = refs[-2:]
    i = pl.program_id(0)
    mine = (base + i) // own_blocks == me_ref[0]
    x = own_ref[...].astype(f32)
    if others:
        x = jnp.where(mine, x, chosen((base + i) % own_blocks, other, own_blocks // others).astype(f32))
    for n in range(parts):
        x = x + dot(chosen(i, attended[n * pieces : (n + 1) * pieces], per), weights[n][...])
    middle_ref[...] = x
    inverse = lax.rsqrt(jnp.mean(x * x, axis=-1, keepdims=True) + EPSILON)
    normed_ref[...] = (x * inverse * gain_ref[...]).astype(bf16)


def mix(me, low, bucket_rows, own_x, other_x, gain_row, attended, weights, before=None, wait=(), blk=BLK):
    own_rows, dim = own_x.shape
    own_blocks = own_rows // blk
    parts, pieces = len(attended), len(attended[0])
    per = attended[0][0].shape[0] // blk
    base, count = low // blk, pieces * per
    extra = () if before is None else tuple(before)
    at_x = lambda i, m: ((base + i) % own_blocks, 0)
    at = lambda i, m: (base + i, 0)
    return pl.pallas_call(
        functools.partial(
            mix_kernel, base=base, own_blocks=own_blocks, others=len(other_x), parts=parts, pieces=pieces, per=per
        ),
        grid_spec=pltpu.PrefetchScalarGridSpec(
            num_scalar_prefetch=1,
            grid=(count,),
            in_specs=[
                pl.BlockSpec((blk, dim), at_x),
                pl.BlockSpec((1, dim), lambda i, m: (0, 0)),
            ]
            + [
                pl.BlockSpec((blk, dim), lambda i, m, k=k, n=own_blocks // len(other_x): (jnp.clip((base + i) % own_blocks - k * n, 0, n - 1), 0))
                for k in range(len(other_x))
            ]
            + [
                pl.BlockSpec((blk, a.shape[1]), lambda i, m, k=k: (jnp.clip(i - k * per, 0, per - 1), 0))
                for part in attended
                for k, a in enumerate(part)
            ]
            + [pl.BlockSpec(w.shape, lambda i, m: (0, 0), **ONE) for w in weights]
            + [ANY] * (len(extra) + len(wait)),
            out_specs=[pl.BlockSpec((blk, dim), at)] * 2,
        ),
        out_shape=[jax.ShapeDtypeStruct((bucket_rows, dim), f32), jax.ShapeDtypeStruct((bucket_rows, dim), bf16)],
        input_output_aliases={3 + len(other_x) + parts * (pieces + 1) + n: n for n in range(len(extra))},
        compiler_params=params(48),
        name="mix",
    )(scalar(me), own_x, gain_row[None, :], *other_x, *[a for part in attended for a in part], *weights, *extra, *wait)


def ff_forward_kernel(base_ref, x_ref, wg_ref, wu_ref, *refs, rc):
    g_ref, u_ref, act_ref = refs[-3:]

    def by_rows(r, c):
        at = pl.ds(pl.multiple_of(r * rc, rc), rc)
        x = x_ref[at, :]
        g = dot(x, wg_ref[...])
        u = dot(x, wu_ref[...])
        g_ref[at, :] = g
        u_ref[at, :] = u
        act_ref[at, :] = (g * (1.0 / (1.0 + jnp.exp(-g))) * u).astype(bf16)
        return c

    lax.fori_loop(0, x_ref.shape[0] // rc, by_rows, 0)


def ff_forward(x, base, rows, mlp_in, wait=(), hb=512, rc=512):
    dim = x.shape[1]
    hidden = mlp_in.shape[2]
    hb = block_of(hidden, hb)
    rc = block_of(rows, rc)
    return pl.pallas_call(
        functools.partial(ff_forward_kernel, rc=rc),
        grid_spec=pltpu.PrefetchScalarGridSpec(
            num_scalar_prefetch=1,
            grid=(hidden // hb,),
            in_specs=[
                pl.BlockSpec((rows, dim), lambda h, b: (b[0], 0), **ONE),
                pl.BlockSpec((None, dim, hb), lambda h, b: (0, 0, h)),
                pl.BlockSpec((None, dim, hb), lambda h, b: (1, 0, h)),
            ]
            + [ANY] * len(wait),
            out_specs=[pl.BlockSpec((rows, hb), lambda h, b: (0, h))] * 3,
        ),
        out_shape=[jax.ShapeDtypeStruct((rows, hidden), f32)] * 2 + [jax.ShapeDtypeStruct((rows, hidden), bf16)],
        compiler_params=params(60),
        cost_estimate=COST,
        name="ff_forward",
    )(scalar(base), x, mlp_in, mlp_in, *wait)


def ff_output_kernel(me_ref, act_ref, w_ref, *refs, pieces, per, whole):
    total = dot(act_ref[...], w_ref[...])
    if whole:
        total = total + refs[0][...] + chosen(pl.program_id(0), refs[1 : 1 + pieces], per).astype(f32)
    refs[-1][...] = total.astype(bf16)


def ff_output(me, act, low, high, mlp_out, middle=None, got=(), wait=(), blk=BLK):
    hidden, dim = mlp_out.shape
    base, count = low // blk, (high - low) // blk
    whole = middle is not None
    per = got[0].shape[0] // blk if got else 1
    return pl.pallas_call(
        functools.partial(ff_output_kernel, pieces=len(got), per=per, whole=whole),
        grid_spec=pltpu.PrefetchScalarGridSpec(
            num_scalar_prefetch=1,
            grid=(count,),
            in_specs=[pl.BlockSpec((blk, hidden), lambda i, m: (base + i, 0)), pl.BlockSpec((hidden, dim), lambda i, m: (0, 0), **ONE)]
            + [pl.BlockSpec((blk, dim), lambda i, m: (m[0] * count + i, 0))] * (1 if whole else 0)
            + in_turn(len(got), per, blk, dim)
            + [ANY] * len(wait),
            out_specs=pl.BlockSpec((blk, dim), lambda i, m: (i, 0)),
        ),
        out_shape=jax.ShapeDtypeStruct((high - low, dim), bf16),
        compiler_params=params(48),
        cost_estimate=COST,
        name="ff_output",
    )(scalar(me), act, mlp_out, *((middle,) if whole else ()), *got, *wait)


def ff_backward_kernel(*refs, rc, pieces, outs):
    og, refs = refs[:pieces], refs[pieces:]
    g_ref, u_ref, wg_ref, wu_ref, wo_ref = refs[:5]
    gn, (gg_ref, gu_ref, acc_ref) = refs[-3 - outs : -3], refs[-3:]
    rows = acc_ref.shape[0]

    @pl.when(pl.program_id(0) == 0)
    def _():
        acc_ref[...] = jnp.zeros_like(acc_ref)

    def by_rows(og_ref, low, r):
        here = pl.ds(pl.multiple_of(r * rc, rc), rc)
        at = pl.ds(pl.multiple_of(low + r * rc, rc), rc)
        ga = dot(og_ref[here, :], wo_ref[...], NT)
        g = g_ref[at, :]
        s = 1.0 / (1.0 + jnp.exp(-g))
        silu = g * s
        gg = (ga * u_ref[at, :] * (s * (1.0 + g * (1.0 - s)))).astype(bf16)
        gu = (ga * silu).astype(bf16)
        gg_ref[at, :] = gg
        gu_ref[at, :] = gu
        acc_ref[at, :] += dot(gg, wg_ref[...], NT) + dot(gu, wu_ref[...], NT)

    low = 0
    for og_ref in og:
        count = og_ref.shape[0] // rc
        if count == 1:
            by_rows(og_ref, low, 0)
        else:
            lax.fori_loop(0, count, lambda r, c, og_ref=og_ref, low=low: (by_rows(og_ref, low, r), c)[1], 0)
        low += og_ref.shape[0]

    @pl.when(pl.program_id(0) == pl.num_programs(0) - 1)
    def _():
        for n, out in enumerate(gn):
            out[...] = acc_ref[n * out.shape[0] : (n + 1) * out.shape[0], :].astype(out.dtype)


def ff_backward(og, g, u, mlp_in, mlp_out, dtype, outs=1, wait=(), hb=512, rc=512):
    rows, hidden = g.shape
    dim = mlp_out.shape[1]
    hb = block_of(hidden, hb)
    rc = block_of(og[0].shape[0], rc)
    return pl.pallas_call(
        functools.partial(ff_backward_kernel, rc=rc, pieces=len(og), outs=outs),
        grid=(hidden // hb,),
        in_specs=[pl.BlockSpec(a.shape, lambda h: (0, 0), **ONE) for a in og]
        + [
            pl.BlockSpec((rows, hb), lambda h: (0, h)),
            pl.BlockSpec((rows, hb), lambda h: (0, h)),
            pl.BlockSpec((None, dim, hb), lambda h: (0, 0, h)),
            pl.BlockSpec((None, dim, hb), lambda h: (1, 0, h)),
            pl.BlockSpec((hb, dim), lambda h: (h, 0)),
        ]
        + [ANY] * len(wait),
        out_specs=[pl.BlockSpec((rows // outs, dim), lambda h: (0, 0), **ONE)] * outs + [pl.BlockSpec((rows, hb), lambda h: (0, h))] * 2,
        scratch_shapes=[pltpu.VMEM((rows, dim), f32)],
        out_shape=[jax.ShapeDtypeStruct((rows // outs, dim), dtype)] * outs + [jax.ShapeDtypeStruct((rows, hidden), bf16)] * 2,
        compiler_params=params(60),
        cost_estimate=COST,
        name="ff_backward",
    )(*og, g, u, mlp_in, mlp_in, mlp_out, *wait)


def turn_into(turned, x_ref):
    rows, dim = x_ref.shape
    for k in range(0, rows, 256):
        def turn(t, c, k=k):
            at = pl.ds(pl.multiple_of(t * 256, 256), 256)
            turned[at, k : k + 256] = x_ref[k : k + 256, at].T
            return c
        lax.fori_loop(0, dim // 256, turn, 0)


def store_split(total, first, share, side, keep_ref, send_ref):
    for n in range(0, total.shape[0] // share, 2):
        even = total[n * share : (n + 1) * share]
        odd = total[(n + 1) * share : (n + 2) * share]
        at = slice((first // share + n) // 2 * share, ((first // share + n) // 2 + 1) * share)
        keep_ref[at, :] = jnp.where(side == 0, even, odd).astype(bf16)
        send_ref[at, :] = jnp.where(side == 0, odd, even).astype(bf16)


def weights_kernel(base_ref, *refs, pieces, outs, share, cc):
    lhs, rhs, refs = refs[:pieces], refs[pieces : 2 * pieces], refs[2 * pieces :]
    out, turned = refs[-pieces - outs : -pieces], refs[-pieces:]
    dim = lhs[0].shape[1]

    @pl.when(pl.program_id(0) == 0)
    def _():
        for x_ref, t_ref in zip(lhs, turned):
            turn_into(t_ref, x_ref)

    def product(at):
        total = None
        for t_ref, r_ref in zip(turned, rhs):
            part = dot(t_ref[at, :], r_ref[...])
            total = part if total is None else total + part
        return total

    if outs == 2:
        for first in range(0, dim, cc):
            store_split(product(slice(first, first + cc)), first, share, base_ref[1], *out)
        return

    def by_columns(t, c):
        at = pl.ds(pl.multiple_of(t * cc, cc), cc)
        out[0][at, :] = product(at).astype(bf16)
        return c

    lax.fori_loop(0, dim // cc, by_columns, 0)


def weight_gradient(base, terms, side=None, share=None, wait=(), hb=512, cc=640):
    dim = terms[0][0].shape[1]
    columns = terms[0][2].shape[1]
    hb = block_of(columns, hb)
    outs = 1 if side is None else 2
    table = jnp.stack([jnp.asarray(base, jnp.int32), jnp.asarray(0 if side is None else side, jnp.int32)])
    return pl.pallas_call(
        functools.partial(weights_kernel, pieces=len(terms), outs=outs, share=share, cc=cc),
        grid_spec=pltpu.PrefetchScalarGridSpec(
            num_scalar_prefetch=1,
            grid=(columns // hb,),
            in_specs=[pl.BlockSpec((n, dim), lambda h, b, m=m: (m(b[0]), 0), **ONE) for _, m, _, _, n in terms]
            + [pl.BlockSpec((n, hb), lambda h, b, k=k: (k, h)) for _, _, _, k, n in terms]
            + [ANY] * len(wait),
            out_specs=[pl.BlockSpec((dim // outs, hb), lambda h, b: (0, h))] * outs,
            scratch_shapes=[pltpu.VMEM((dim, n), bf16) for *_, n in terms],
        ),
        out_shape=[jax.ShapeDtypeStruct((dim // outs, columns), bf16)] * outs,
        compiler_params=params(60),
        cost_estimate=COST,
        name="weight_gradient",
    )(table, *[t[0] for t in terms], *[t[2] for t in terms], *wait)


def attn_weights_kernel(n_ref, *refs, lows, cc):
    parts, out_ref, turned = refs[: len(lows)], refs[-2], refs[-1]
    rows, dim = n_ref.shape

    @pl.when(pl.program_id(0) == 0)
    def _():
        turn_into(turned, n_ref)

    def by_columns(t, c):
        at = pl.ds(pl.multiple_of(t * cc, cc), cc)
        total = None
        for low, g_ref in zip(lows, parts):
            part = dot(turned[at, low : low + g_ref.shape[0]], g_ref[...])
            total = part if total is None else total + part
        out_ref[at, :] = total.astype(bf16)
        return c

    lax.fori_loop(0, dim // cc, by_columns, 0)


def attn_weight_gradient(normed_one, lows, grad_qkv, wait=(), cc=640):
    rows, dim = normed_one.shape
    cols = grad_qkv[0].shape[2]
    return pl.pallas_call(
        functools.partial(attn_weights_kernel, lows=lows, cc=cc),
        grid=(3,),
        in_specs=[pl.BlockSpec((rows, dim), lambda j: (0, 0), **ONE)]
        + [pl.BlockSpec((None, g.shape[1], cols), lambda j: (j, 0, 0)) for g in grad_qkv]
        + [ANY] * len(wait),
        out_specs=pl.BlockSpec((dim, cols), lambda j: (0, j)) if cols % LANES == 0 else pl.BlockSpec((None, dim, cols), lambda j: (j, 0, 0)),
        scratch_shapes=[pltpu.VMEM((dim, rows), bf16)],
        out_shape=jax.ShapeDtypeStruct((dim, 3 * cols) if cols % LANES == 0 else (3, dim, cols), bf16),
        compiler_params=params(56),
        cost_estimate=COST,
        name="attn_weight_gradient",
    )(normed_one, *grad_qkv, *wait)


def norm_input_part(z, gain, e):
    inverse = lax.rsqrt(jnp.mean(z * z, axis=-1, keepdims=True) + EPSILON)
    weighted = e * gain
    inner = jnp.mean(weighted * z, axis=-1, keepdims=True)
    return weighted * inverse - z * (inverse * inverse * inverse) * inner


def middle_backward_kernel(me_ref, og_ref, z_ref, own_ref, gain_ref, *refs, pieces, per, parts):
    got, refs = refs[:pieces], refs[pieces:]
    weights, refs = refs[:parts], refs[-2 - parts :]
    i = pl.program_id(0)
    e = own_ref[...]
    if pieces:
        e = e + chosen(i, got, per).astype(f32)
    grad = og_ref[...].astype(f32) + norm_input_part(z_ref[...], gain_ref[...], e)
    refs[0][...] = grad
    branch = grad.astype(bf16)
    refs[1][...] = branch
    for w, out in zip(weights, refs[2:]):
        out[...] = dot(branch, w[...], NT).astype(bf16)


def middle_backward(me, out_grad, middle, gn_own, got_gn, gain_row, weights, wait=(), blk=BLK):
    rows, dim = out_grad.shape
    pieces = len(got_gn)
    per = got_gn[0].shape[0] // blk if pieces else 1
    own_blocks = rows // blk
    at = lambda i, m: (i, 0)
    return pl.pallas_call(
        functools.partial(middle_backward_kernel, pieces=pieces, per=per, parts=len(weights)),
        grid_spec=pltpu.PrefetchScalarGridSpec(
            num_scalar_prefetch=1,
            grid=(own_blocks,),
            in_specs=[
                pl.BlockSpec((blk, dim), at),
                pl.BlockSpec((blk, dim), lambda i, m: (m[0] * own_blocks + i, 0)),
                pl.BlockSpec((blk, dim), at),
                pl.BlockSpec((1, dim), lambda i, m: (0, 0)),
            ]
            + in_turn(pieces, per, blk, dim)
            + [pl.BlockSpec(w.shape, lambda i, m: (0, 0), **ONE) for w in weights]
            + [ANY] * len(wait),
            out_specs=[pl.BlockSpec((blk, dim), at)] * 2 + [pl.BlockSpec((blk, w.shape[0]), at) for w in weights],
        ),
        out_shape=[jax.ShapeDtypeStruct((rows, dim), f32), jax.ShapeDtypeStruct((rows, dim), bf16)]
        + [jax.ShapeDtypeStruct((rows, w.shape[0]), bf16) for w in weights],
        compiler_params=params(48),
        cost_estimate=COST,
        name="middle_backward",
    )(scalar(me), out_grad, middle, gn_own, gain_row[None, :], *got_gn, *weights, *wait)


def tokens_backward_kernel(me_ref, x_ref, grad_ref, gain_ref, *refs, sides):
    i = pl.program_id(0)
    out_ref, refs = refs[-1], refs[:-1]
    e = None
    for n, ((count, each), (more, every)) in enumerate(sides):
        own, got, refs = refs[:count], refs[count : count + more], refs[count + more :]
        here = chosen(i, own, each) + chosen(i, got, every).astype(f32)
        e = here if e is None else jnp.where(me_ref[0] == n, here, e)
    out_ref[...] = (grad_ref[...] + norm_input_part(x_ref[...].astype(f32), gain_ref[...], e)).astype(bf16)


def tokens_backward(me, tokens, grad_middle, gain_row, sides, blk=BLK):
    rows, dim = tokens.shape
    at = lambda i, m: (i, 0)
    shape = tuple(tuple((len(part), part[0].shape[0] // blk) for part in side) for side in sides)
    specs = [spec for side in shape for part in side for spec in in_turn(*part, blk, dim)]
    return pl.pallas_call(
        functools.partial(tokens_backward_kernel, sides=shape),
        grid_spec=pltpu.PrefetchScalarGridSpec(
            num_scalar_prefetch=1,
            grid=(rows // blk,),
            in_specs=[pl.BlockSpec((blk, dim), at), pl.BlockSpec((blk, dim), at), pl.BlockSpec((1, dim), lambda i, m: (0, 0))] + specs,
            out_specs=pl.BlockSpec((blk, dim), at),
        ),
        out_shape=jax.ShapeDtypeStruct((rows, dim), bf16),
        compiler_params=params(48),
        cost_estimate=COST,
        name="tokens_backward",
    )(scalar(me), tokens, grad_middle, gain_row[None, :], *[a for own, got in sides for a in (*own, *got)])


def contract(a, b, dims):
    return lax.dot_general(a, b, (dims, ((), ())), preferred_element_type=f32)


def after(value, *others):
    return lax.optimization_barrier((value, *others))[0]


SWAP = ((0, 1), (1, 0))


def halving_step(state, group, n_dp, behind):
    bit, send, keep = state
    got = lax.ppermute(send, "dp", [(n, n ^ (1 << bit)) for n in range(n_dp)])
    keep, behind = lax.optimization_barrier((keep, behind))
    if n_dp >> bit == 2:
        return (bit + 1, got, keep), behind
    split = lambda a: a.reshape(n_dp >> (bit + 2), 2, -1, a.shape[-1])
    side = (group >> (bit + 1)) & 1

    def pick(at):
        parts = [lax.dynamic_index_in_dim(split(a), at, 1, False).astype(f32) for a in (keep, got)]
        return (parts[0] + parts[1]).astype(bf16).reshape(-1, keep.shape[-1])

    return (bit + 1, pick(1 - side), pick(side)), behind


def halving_end(state):
    _, got, keep = state
    return keep.astype(f32) + got.astype(f32)


def per_device(tokens, norm_gains, attn_in, attn_out, mlp_in, mlp_out, lengths, out_grad):
    n_mp = lax.axis_size("mp")
    n_dp = lax.axis_size("dp")
    me = lax.axis_index("mp")
    group = lax.axis_index("dp")
    rows, dim = tokens.shape
    bucket = rows * n_mp
    hd = HEAD_DIM
    cols = attn_out.shape[0]
    hidden = mlp_out.shape[0]
    share = dim // n_dp
    scale = hd**-0.5
    pair = n_mp == 2
    hb = block_of(hidden, 512)
    places, starts = layout(lengths[0], bucket)
    tables = turning(places - starts, hd)
    cos, sin = tables[:2]
    first = starts[::BLK] // BLK
    start_row = starts.reshape(bucket // BLK, 1, BLK)
    own_blocks = rows // BLK

    def mine(array, axis, size):
        return lax.dynamic_slice_in_dim(array, group * size, size, axis)

    def swap(array):
        return lax.ppermute(array, "mp", SWAP)

    def scatter(array):
        return lax.psum_scatter(array, "dp", scatter_dimension=0, tiled=True)

    chunk = rows // 2
    halves = (0, chunk)
    whole = lambda b: 0
    if pair:
        piece = swap(mine(attn_out, 0, cols // n_dp))
        other_attn_out = lax.all_gather(piece, "dp", axis=0, tiled=True)
        other_x = [swap(tokens[low : low + chunk]) for low in halves]
        projected = project(tokens, me * own_blocks, bucket, norm_gains[0], attn_in, cos, sin, hd, wait=(piece,))
        att, lse, att_got = [], [], []
        for n, low in enumerate(range(0, bucket, chunk)):
            if n < 2:
                projected = project(
                    other_x[n], (1 - me) * own_blocks + n * own_blocks // 2, bucket, norm_gains[0], attn_in, cos, sin, hd,
                    projected, wait=tuple(att),
                )
            normed_one, q3, k3, v3, kt, vt = projected
            wait = tuple(att_got[n - 2 : n - 1]) if n > 1 else ()
            if n == 1:
                wait = (other_attn_out,)
            a, l = attention_forward(first, low, low + chunk, q3, k3, vt, start_row, hd, scale, tuple(att[-1:]) + wait)
            att.append(a)
            lse.append(l)
            att_got.append(swap(a))
        got_grad = [out_grad[low : low + chunk] for low in halves]
        *got_grad, att_got[2] = lax.optimization_barrier((*got_grad, att_got[2]))
        got_grad = [swap(a) for a in got_grad]
        mix_rows = lambda low, these, before: mix(
            me, low, bucket, tokens, other_x, norm_gains[1], (att[these], att_got[these]), (attn_out, other_attn_out), before
        )
        middle_all, normed_two = mix_rows(3 * chunk, slice(3, 4), mix_rows(0, slice(0, 3), None))
        other = 1 - me
        g_b, u_b, act_b = ff_forward(normed_two, other, rows, mlp_in)
        g_a, u_a, act_a = ff_forward(normed_two, me, rows, mlp_in, wait=(act_b, got_grad[0]))
        (gw_out,) = weight_gradient(
            0,
            [(got_grad[n], whole, act_b, n, chunk) for n in range(2)] + [(out_grad, whole, act_a, 0, rows)],
            wait=(act_a,),
        )
        sum_out = scatter(gw_out)
        *got_gn, gg_b, gu_b = ff_backward(got_grad, g_b, u_b, mlp_in, mlp_out, bf16, 2, wait=(gw_out,))
        got_gn = [swap(a) for a in got_gn]
        gn_a, gg_a, gu_a = ff_backward([out_grad], g_a, u_a, mlp_in, mlp_out, f32, wait=(gg_b,))
        side = lambda b, a: [(normed_two, lambda b: 1 - b, b, 0, rows), (normed_two, lambda b: b, a, 0, rows)]
        (gw_gate,) = weight_gradient(me, side(gg_b, gg_a), wait=(gn_a, got_gn[0]))
        sum_gate = scatter(gw_gate)
        grad_middle, branch_grad, do_own, do_send = middle_backward(
            me, out_grad, middle_all, gn_a, got_gn, norm_gains[1], (attn_out, other_attn_out), wait=(gw_gate,)
        )
    else:
        all_x = lax.all_gather(tokens, "mp", axis=0, tiled=True)
        normed_one, q3, k3, v3, kt, vt = project(all_x, 0, bucket, norm_gains[0], attn_in, cos, sin, hd)
        att_all, lse_all = attention_forward(first, 0, bucket, q3, k3, vt, start_row, hd, scale)
        every_head = lax.all_gather(att_all, "mp", axis=1, tiled=True)
        every_out = lax.all_gather(attn_out, "mp", axis=0, tiled=True)
        middle_all, normed_two = mix(0, 0, bucket, all_x, (), norm_gains[1], ((every_head,),), (every_out,))
        all_grad = lax.all_gather(out_grad, "mp", axis=0, tiled=True)
        g_b, u_b, act_b = ff_forward(normed_two, 0, bucket, mlp_in)
        gn_b, gg_b, gu_b = ff_backward([all_grad], g_b, u_b, mlp_in, mlp_out, bf16)
        sum_out = scatter(weight_gradient(0, [(all_grad, whole, act_b, 0, bucket)])[0])
        sum_gate = scatter(weight_gradient(0, [(normed_two, whole, gg_b, 0, bucket)])[0])
        sum_up = scatter(weight_gradient(0, [(normed_two, whole, gu_b, 0, bucket)])[0])
        grad_normed_two = lax.psum_scatter(gn_b, "mp", scatter_dimension=0, tiled=True).astype(f32)
        grad_middle, branch_grad = middle_backward(me, out_grad, middle_all, grad_normed_two, (), norm_gains[1], ())
        middle = lax.dynamic_slice_in_dim(middle_all, me * rows, rows, 0)
        out_b = ff_output(0, act_b, 0, bucket, mlp_out)
        output = (middle + lax.psum_scatter(out_b, "mp", scatter_dimension=0, tiled=True).astype(f32)).astype(bf16)
    if pair:
        do_got = swap(do_send)
        up_keep, up_send = weight_gradient(me, side(gu_b, gu_a), group & 1, share, wait=(do_send,))
        up = (0, up_send, up_keep)
        out_b = [ff_output(me, act_b, low, low + chunk, mlp_out, wait=(up_keep,)) for low in halves]
        att_own = jnp.where(me == 0, jnp.concatenate(att[:2]), jnp.concatenate(att[2:]))
        att_other = jnp.where(me == 0, jnp.concatenate(att_got[:2]), jnp.concatenate(att_got[2:]))
        gw_attn_out = jnp.concatenate(
            [contract(branch_grad, a, ((0,), (0,))).astype(bf16) for a in (att_own, att_other)], axis=1
        )
        up, gw_attn_out = halving_step(up, group, n_dp, gw_attn_out)
        sum_attn_out = scatter(gw_attn_out)
        got_out = [swap(a) for a in out_b]
        do_low = jnp.where(me == 0, do_own, do_got)
        do_high = jnp.where(me == 0, do_got, do_own)
        grad_att = {0: do_low[:chunk], chunk: do_low[chunk:], rows: do_high}
        lse_of = {0: lse[0], chunk: lse[1], rows: jnp.concatenate(lse[2:], axis=1)}
        att_of = {0: att[0], chunk: att[1], rows: jnp.concatenate(att[2:], axis=0)}
        carry, grad_qkv, own_part, got_part = None, {}, {}, {}
        for low, high in ((rows, bucket), (chunk, rows), (0, chunk)):
            wait = {rows: (sum_out,), chunk: (sum_gate, got_out[0]), 0: (got_out[1],) + tuple(got_part.get(rows, ())[:1])}[low]
            made = attention_backward(
                first, low, high, q3, k3, v3, kt, start_row, lse_of[low], att_of[low], grad_att[low], tables, attn_in, hd, scale,
                carry, (high - low) // chunk, wait + (up[1],),
            )
            send = made[2 : 2 + (high - low) // chunk]
            own_part[low], carry = made[1], made[2 + len(send) :]
            up, grad_qkv[low] = halving_step(up, group, n_dp, made[0])
            path = ((0, 1),) if low == rows else ((1, 0),)
            got_part[low] = [lax.ppermute(a, "mp", path) for a in send]
        grad_tokens = tokens_backward(
            me,
            tokens,
            grad_middle,
            norm_gains[0],
            (([own_part[0], own_part[chunk]], got_part[0] + got_part[chunk]), ([own_part[rows]], got_part[rows])),
        )
        lows = (0, chunk, rows)
        gw_attn_in = attn_weight_gradient(normed_one, lows, [grad_qkv[low] for low in lows], wait=(sum_attn_out, got_part[rows][1], got_part[chunk][0]))
        sum_up = halving_end(up)
    else:
        all_branch = lax.all_gather(branch_grad, "mp", axis=0, tiled=True)
        grad_heads = contract(all_branch, attn_out, ((1,), (1,))).astype(bf16)
        gw_attn_out = contract(all_branch, att_all, ((0,), (0,))).astype(bf16)
        made = attention_backward(
            first, 0, bucket, q3, k3, v3, kt, start_row, lse_all, att_all, grad_heads, tables, attn_in, hd, scale, None
        )
        grad_qkv, grad_normed_one = made[0], lax.psum_scatter(made[2], "mp", scatter_dimension=0, tiled=True)
        nothing = jnp.zeros((rows, dim), f32)
        grad_tokens = tokens_backward(0, tokens, grad_middle, norm_gains[0], (((nothing,), (grad_normed_one,)),))
        gw_attn_in = attn_weight_gradient(normed_one, (0,), [grad_qkv])
        if gw_attn_in.ndim == 3:
            gw_attn_in = gw_attn_in.transpose(1, 0, 2).reshape(dim, 3 * cols)
    if pair:
        output = ff_output(me, act_a, 0, rows, mlp_out, middle_all, got_out, wait=(gw_attn_in,))
    sum_in = jnp.stack([sum_gate.astype(f32), sum_up.astype(f32)])
    sum_out = sum_out.astype(f32)
    if not pair:
        sum_attn_out = scatter(gw_attn_out)
    sum_attn_out = sum_attn_out.astype(f32)
    if pair:
        sum_attn_out = sum_attn_out[:, :cols] + swap(sum_attn_out[:, cols:].astype(bf16)).astype(f32)
    sum_attn_in = scatter(gw_attn_in).astype(f32).reshape(share, 3, cols).transpose(1, 0, 2)
    gain_one = jnp.sum(mine(attn_in, 1, share).astype(f32) * sum_attn_in, axis=(0, 2))
    gain_two = jnp.sum(mine(mlp_in, 1, share).astype(f32) * sum_in, axis=(0, 2))
    gains = jnp.stack([gain_one, gain_two]) / mine(norm_gains, 1, share)
    if pair:
        halves = gains.reshape(2, 2, share // 2)
        gains = lax.dynamic_index_in_dim(halves, me, 1, False) + swap(lax.dynamic_index_in_dim(halves, 1 - me, 1, False))
    else:
        gains = lax.psum_scatter(gains, "mp", scatter_dimension=1, tiled=True)
    return (output, grad_tokens, gains, sum_attn_in, sum_attn_out.T, sum_in, sum_out.T)


def solution(mesh):
    placed = (
        P(("dp", "mp"), None),
        P(),
        P(None, None, "mp"),
        P("mp", None),
        P(None, None, "mp"),
        P("mp", None),
        P("dp", None),
        P(("dp", "mp"), None),
    )
    return jax.shard_map(
        per_device,
        mesh=mesh,
        in_specs=placed,
        out_specs=(
            P(("dp", "mp"), None),
            P(("dp", "mp"), None),
            P(None, ("dp", "mp")),
            P(None, "dp", "mp"),
            P("mp", "dp"),
            P(None, "dp", "mp"),
            P("mp", "dp"),
        ),
        check_vma=False,
    )
```

```python
import functools

import jax
import jax.numpy as jnp
from jax import lax
from jax.experimental import pallas as pl
from jax.experimental.pallas import tpu as pltpu
from jax.sharding import PartitionSpec as P

BLK = 256
LANES = 128
HEAD_DIM = 80
EPSILON = 1e-06
LOG2E = 1.4426950408889634
NEG = -1e30
bf16 = jnp.bfloat16
f32 = jnp.float32
NT = (((1,), (1,)), ((), ()))
NN = (((1,), (0,)), ((), ()))
TN = (((0,), (0,)), ((), ()))
FLOPS = 2_500_000_000
ONE = dict(pipeline_mode=pl.Buffered(1))


def dot(a, b, contract=NN):
    return lax.dot_general(a, b, contract, preferred_element_type=f32)


ANY = pl.BlockSpec(memory_space=pl.ANY)


def taking(micros):
    return pl.CostEstimate(flops=int(micros * FLOPS), bytes_accessed=1 << 20, transcendentals=0)


def params(mib):
    return pltpu.CompilerParams(vmem_limit_bytes=mib << 20)


def block_of(size, most):
    return next(b for b in (most, 1024, 512, 256, 128) if b <= most and size % b == 0)


def scalar(value):
    return jnp.reshape(value, (1,)).astype(jnp.int32)


def chosen(i, refs, per):
    value = refs[0][...]
    for k in range(1, len(refs)):
        value = jnp.where(i // per == k, refs[k][...], value)
    return value


def in_turn(count, per, blk, wide):
    return [pl.BlockSpec((blk, wide), lambda i, m, k=k: (jnp.clip(i - k * per, 0, per - 1), 0)) for k in range(count)]


def layout(lengths_row, bucket_rows):
    series_ends = jnp.cumsum(lengths_row, dtype=jnp.int32)
    places = jnp.arange(bucket_rows, dtype=jnp.int32)
    before = series_ends[None, :] <= places[:, None]
    starts = jnp.sum(jnp.where(before, lengths_row[None, :], 0), axis=1, dtype=jnp.int32)
    return places, starts


def turning(position, hd):
    half = hd // 2
    frequency = 10000.0 ** (-(jnp.arange(half, dtype=f32) * 2.0 / hd))
    place = position.astype(f32)
    turned = frequency[:, None] * place[None, :]
    wide = jnp.concatenate([frequency, frequency, jnp.zeros((LANES - hd,), f32)])
    angles = place[:, None] * wide[None, :]
    return jnp.cos(angles), jnp.sin(angles), jnp.cos(turned), jnp.sin(turned)


def project_kernel(base_ref, x_ref, gain_ref, w_ref, cos_ref, sin_ref, *refs, hd):
    n_ref, q_ref, k_ref, v_ref, kt_ref, vt_ref = refs[-6:]
    heads, rows, lanes = q_ref.shape
    half = hd // 2
    x = x_ref[...].astype(f32)
    inverse = lax.rsqrt(jnp.mean(x * x, axis=-1, keepdims=True) + EPSILON)
    normed = (x * inverse * gain_ref[...]).astype(bf16)
    n_ref[...] = normed
    cos, sin = cos_ref[...], sin_ref[...]
    lane = lax.broadcasted_iota(jnp.int32, (rows, lanes), 1)
    pad = jnp.zeros((rows, lanes - hd), f32)
    for j, out in enumerate((q_ref, k_ref, v_ref)):
        y = dot(normed, w_ref[j])
        for h in range(heads):
            part = jnp.concatenate([y[:, h * hd : (h + 1) * hd], pad], axis=1)
            if j < 2:
                other = jnp.where(lane < half, -pltpu.roll(part, lanes - half, 1), pltpu.roll(part, half, 1))
                part = part * cos + other * sin
                part = jnp.where(lane < hd, part, 0.0)
            part = part.astype(bf16)
            out[h] = part
            if j == 1:
                kt_ref[h] = part.T
            if j == 2:
                vt_ref[h] = part.T


def project(x, base, bucket_rows, gain_row, attn_in, cos, sin, hd, before=None, wait=(), blk=BLK):
    rows, dim = x.shape
    heads = attn_in.shape[2] // hd
    at = lambda i, b: (b[0] + i, 0)
    at_heads = lambda i, b: (0, b[0] + i, 0)
    at_turned = lambda i, b: (0, 0, b[0] + i)
    extra = () if before is None else tuple(before)
    return pl.pallas_call(
        functools.partial(project_kernel, hd=hd),
        grid_spec=pltpu.PrefetchScalarGridSpec(
            num_scalar_prefetch=1,
            grid=(rows // blk,),
            in_specs=[
                pl.BlockSpec((blk, dim), lambda i, b: (i, 0)),
                pl.BlockSpec((1, dim), lambda i, b: (0, 0)),
                pl.BlockSpec(attn_in.shape, lambda i, b: (0, 0, 0), **ONE),
                pl.BlockSpec((blk, LANES), at),
                pl.BlockSpec((blk, LANES), at),
            ]
            + [ANY] * (len(extra) + len(wait)),
            out_specs=[pl.BlockSpec((blk, dim), at)]
            + [pl.BlockSpec((heads, blk, LANES), at_heads)] * 3
            + [pl.BlockSpec((heads, LANES, blk), at_turned)] * 2,
        ),
        out_shape=[jax.ShapeDtypeStruct((bucket_rows, dim), bf16)]
        + [jax.ShapeDtypeStruct((heads, bucket_rows, LANES), bf16)] * 3
        + [jax.ShapeDtypeStruct((heads, LANES, bucket_rows), bf16)] * 2,
        input_output_aliases={6 + n: n for n in range(len(extra))},
        compiler_params=params(56),
        cost_estimate=taking(20 * rows // 1024),
        name="project",
    )(scalar(base), x, gain_row[None, :], attn_in, cos, sin, *extra, *wait)


def allowed_mask(j, i, start_row, blk):
    kpos = j * blk + lax.broadcasted_iota(jnp.int32, (blk, blk), 0)
    qpos = i * blk + lax.broadcasted_iota(jnp.int32, (blk, blk), 1)
    return (kpos >= start_row) & (kpos <= qpos)


def attention_forward_kernel(first_ref, q_ref, k_ref, vt_ref, start_ref, *refs, base, blk, hd, scale):
    o_ref, lse_ref, acc_ref, m_ref, l_ref, a_ref, s_ref, p_ref = refs[-8:]
    heads = k_ref.shape[0]
    i = base + pl.program_id(0)
    acc_ref[...] = jnp.zeros_like(acc_ref)
    m_ref[...] = jnp.full_like(m_ref, NEG)
    l_ref[...] = jnp.zeros_like(l_ref)
    c2 = scale * LOG2E

    def step(j, carry):
        mask = allowed_mask(j, i, start_ref[0], blk)
        rows = pl.ds(pl.multiple_of(j * blk, blk), blk)
        for h in range(heads):
            s_ref[h] = dot(k_ref[h, rows, :], q_ref[h], NT)
        for h in range(heads):
            s = jnp.where(mask, s_ref[h] * c2, NEG)
            m_old = m_ref[h : h + 1]
            m_new = jnp.maximum(m_old, jnp.max(s, axis=0, keepdims=True))
            alpha = jnp.exp2(m_old - m_new)
            p = jnp.exp2(s - m_new)
            l_ref[h : h + 1] = alpha * l_ref[h : h + 1] + jnp.sum(p, axis=0, keepdims=True)
            m_ref[h : h + 1] = m_new
            a_ref[h : h + 1] = alpha
            p_ref[h] = p.astype(bf16)
        for h in range(heads):
            part = slice(h * hd, (h + 1) * hd)
            acc_ref[part, :] = a_ref[h : h + 1] * acc_ref[part, :] + dot(vt_ref[h, :hd, rows], p_ref[h])
        return carry

    step(i, 0)
    lax.fori_loop(first_ref[i], i, step, 0)
    for h in range(heads):
        part = slice(h * hd, (h + 1) * hd)
        acc_ref[part, :] = acc_ref[part, :] / l_ref[h : h + 1]
    o_ref[...] = acc_ref[...].T.astype(bf16)
    lse_ref[...] = m_ref[...] + jnp.log2(l_ref[...])


def attention_forward(first, low, high, q3, k3, vt, start_row, hd, scale, wait=(), blk=BLK):
    heads, rows, lanes = k3.shape
    base, count = low // blk, (high - low) // blk
    return pl.pallas_call(
        functools.partial(attention_forward_kernel, base=base, blk=blk, hd=hd, scale=scale),
        grid_spec=pltpu.PrefetchScalarGridSpec(
            num_scalar_prefetch=1,
            grid=(count,),
            in_specs=[
                pl.BlockSpec((heads, blk, lanes), lambda i, t: (0, i + base, 0)),
                pl.BlockSpec((heads, high, lanes), lambda i, t: (0, 0, 0), **ONE),
                pl.BlockSpec((heads, lanes, high), lambda i, t: (0, 0, 0), **ONE),
                pl.BlockSpec((1, 1, blk), lambda i, t: (i + base, 0, 0)),
            ]
            + [ANY] * len(wait),
            out_specs=[
                pl.BlockSpec((blk, heads * hd), lambda i, t: (i, 0)),
                pl.BlockSpec((heads, blk), lambda i, t: (0, i)),
            ],
            scratch_shapes=[
                pltpu.VMEM((heads * hd, blk), f32),
                pltpu.VMEM((heads, blk), f32),
                pltpu.VMEM((heads, blk), f32),
                pltpu.VMEM((heads, blk), f32),
                pltpu.VMEM((heads, blk, blk), f32),
                pltpu.VMEM((heads, blk, blk), bf16),
            ],
        ),
        out_shape=[
            jax.ShapeDtypeStruct((count * blk, heads * hd), bf16),
            jax.ShapeDtypeStruct((heads, count * blk), f32),
        ],
        compiler_params=params(56),
        cost_estimate=taking(5 * count),
        name="attention_forward",
    )(first, q3, k3, vt, start_row, *wait)


def attention_backward_kernel(
    first_ref, q_ref, k_ref, v_ref, kt_ref, start_ref, lse_ref, o_ref, do_ref, cos_ref, sin_ref, cost_ref, sint_ref, w_ref, *refs,
    base, count, blk, hd, scale, carried, waits, outs,
):
    carry_in, refs = (refs[:2], refs[2:]) if carried else ((), refs)
    refs = refs[waits:]
    g_ref, wide_ref, narrow, refs = *refs[:2], refs[2 : 2 + outs], refs[2 + outs :]
    carry_out, refs = (refs[:2], refs[2:]) if base else ((), refs)
    do3_ref, dk_ref, dv_ref, dqt_ref, d_ref, s_ref, dp_ref, p_ref, ds_ref = refs
    heads, rows, lanes = k_ref.shape
    half = hd // 2
    step_at = pl.program_id(0)
    i = base + count - 1 - step_at

    @pl.when(step_at == 0)
    def _():
        do3_ref[...] = jnp.zeros_like(do3_ref)
        if carried:
            dk_ref[...] = carry_in[0][...]
            dv_ref[...] = carry_in[1][...]
        else:
            dk_ref[...] = jnp.zeros_like(dk_ref)
            dv_ref[...] = jnp.zeros_like(dv_ref)

    for h in range(heads):
        do3_ref[h, :, :hd] = do_ref[:, h * hd : (h + 1) * hd]
    prod = do_ref[...].astype(f32) * o_ref[...].astype(f32)
    high = prod.astype(bf16)
    low = (prod - high.astype(f32)).astype(bf16)
    pad_heads = d_ref.shape[0]
    owner = lax.broadcasted_iota(jnp.int32, (pad_heads, heads * hd), 1) // hd
    pick = (owner == lax.broadcasted_iota(jnp.int32, (pad_heads, heads * hd), 0)).astype(f32).astype(bf16)
    d_ref[...] = dot(pick, high, NT) + dot(pick, low, NT)
    dqt_ref[...] = jnp.zeros_like(dqt_ref)
    c2 = scale * LOG2E

    def step(j, carry):
        mask = allowed_mask(j, i, start_ref[0], blk)
        at = pl.ds(pl.multiple_of(j * blk, blk), blk)
        for h in range(heads):
            s_ref[h] = dot(k_ref[h, at, :], q_ref[h], NT)
            dp_ref[h] = dot(v_ref[h, at, :], do3_ref[h], NT)
        for h in range(heads):
            p = jnp.where(mask, jnp.exp2(s_ref[h] * c2 - lse_ref[h : h + 1]), 0.0)
            p_ref[h] = p.astype(bf16)
            ds_ref[h] = (p * (dp_ref[h] - d_ref[h : h + 1])).astype(bf16)
        for h in range(heads):
            dv_ref[h, at, :] += dot(p_ref[h], do3_ref[h])
            dk_ref[h, at, :] += dot(ds_ref[h], q_ref[h])
            part = slice(h * hd, (h + 1) * hd)
            dqt_ref[part, :] += dot(kt_ref[h, :hd, at], ds_ref[h])
        return carry

    lax.fori_loop(first_ref[i], i + 1, step, 0)
    ct = cost_ref[...]
    st = sint_ref[...]
    for h in range(heads):
        a = dqt_ref[h * hd : h * hd + half, :] * scale
        b = dqt_ref[h * hd + half : (h + 1) * hd, :] * scale
        dqt_ref[h * hd : h * hd + half, :] = a * ct + b * st
        dqt_ref[h * hd + half : (h + 1) * hd, :] = b * ct - a * st
    g_ref[0] = dqt_ref[...].T.astype(bf16)
    at = pl.ds(pl.multiple_of(i * blk, blk), blk)
    cos, sin = cos_ref[...], sin_ref[...]
    lane = lax.broadcasted_iota(jnp.int32, (blk, lanes), 1)
    for h in range(heads):
        x = dk_ref[h, at, :] * scale
        other = jnp.where(lane < half, pltpu.roll(x, lanes - half, 1), -pltpu.roll(x, half, 1))
        g_ref[1, :, h * hd : (h + 1) * hd] = (x * cos + other * sin).astype(bf16)[:, :hd]
        g_ref[2, :, h * hd : (h + 1) * hd] = dv_ref[h, at, :].astype(bf16)[:, :hd]
    total = dot(g_ref[0], w_ref[0], NT) + dot(g_ref[1], w_ref[1], NT) + dot(g_ref[2], w_ref[2], NT)
    wide_ref[...] = total
    for n in range(outs):

        @pl.when((i - base) // (count // outs) == n)
        def _():
            narrow[n][...] = total.astype(bf16)
    if base:

        @pl.when(step_at == count - 1)
        def _():
            carry_out[0][...] = dk_ref[:, : base * blk, :]
            carry_out[1][...] = dv_ref[:, : base * blk, :]


def attention_backward(first, low, high, q3, k3, v3, kt, start_row, lse, attended, grad_att, tables, attn_in, hd, scale, carry, outs=1, wait=(), blk=BLK):
    heads, rows, lanes = k3.shape
    base, count = low // blk, (high - low) // blk
    cos, sin, cost, sint = tables
    pad_heads = max(8, heads)
    half = hd // 2
    here = lambda i: count - 1 - i
    there = lambda i: base + count - 1 - i
    carried = carry is not None
    before = jax.ShapeDtypeStruct((heads, low, lanes), f32)
    return pl.pallas_call(
        functools.partial(attention_backward_kernel, base=base, count=count, blk=blk, hd=hd, scale=scale, carried=carried, waits=len(wait), outs=outs),
        grid_spec=pltpu.PrefetchScalarGridSpec(
            num_scalar_prefetch=1,
            grid=(count,),
            in_specs=[
                pl.BlockSpec((heads, blk, lanes), lambda i, t: (0, there(i), 0)),
                pl.BlockSpec((heads, high, lanes), lambda i, t: (0, 0, 0), **ONE),
                pl.BlockSpec((heads, high, lanes), lambda i, t: (0, 0, 0), **ONE),
                pl.BlockSpec((heads, lanes, high), lambda i, t: (0, 0, 0), **ONE),
                pl.BlockSpec((1, 1, blk), lambda i, t: (there(i), 0, 0)),
                pl.BlockSpec((heads, blk), lambda i, t: (0, here(i))),
                pl.BlockSpec((blk, heads * hd), lambda i, t: (here(i), 0)),
                pl.BlockSpec((blk, heads * hd), lambda i, t: (here(i), 0)),
                pl.BlockSpec((blk, lanes), lambda i, t: (there(i), 0)),
                pl.BlockSpec((blk, lanes), lambda i, t: (there(i), 0)),
                pl.BlockSpec((half, blk), lambda i, t: (0, there(i))),
                pl.BlockSpec((half, blk), lambda i, t: (0, there(i))),
                pl.BlockSpec(attn_in.shape, lambda i, t: (0, 0, 0), **ONE),
            ]
            + [pl.BlockSpec((heads, high, lanes), lambda i, t: (0, 0, 0), **ONE)] * (2 if carried else 0)
            + [ANY] * len(wait),
            out_specs=[pl.BlockSpec((3, blk, heads * hd), lambda i, t: (0, here(i), 0))]
            + [pl.BlockSpec((blk, attn_in.shape[1]), lambda i, t: (here(i), 0))]
            + [
                pl.BlockSpec((blk, attn_in.shape[1]), lambda i, t, k=k, n=count // outs: (jnp.clip(here(i) - k * n, 0, n - 1), 0))
                for k in range(outs)
            ]
            + [pl.BlockSpec((heads, low, lanes), lambda i, t: (0, 0, 0), **ONE)] * (2 if base else 0),
            scratch_shapes=[
                pltpu.VMEM((heads, blk, lanes), bf16),
                pltpu.VMEM((heads, high, lanes), f32),
                pltpu.VMEM((heads, high, lanes), f32),
                pltpu.VMEM((heads * hd, blk), f32),
                pltpu.VMEM((pad_heads, blk), f32),
                pltpu.VMEM((heads, blk, blk), f32),
                pltpu.VMEM((heads, blk, blk), f32),
                pltpu.VMEM((heads, blk, blk), bf16),
                pltpu.VMEM((heads, blk, blk), bf16),
            ],
        ),
        out_shape=[
            jax.ShapeDtypeStruct((3, count * blk, heads * hd), bf16),
            jax.ShapeDtypeStruct((count * blk, attn_in.shape[1]), f32),
        ]
        + [jax.ShapeDtypeStruct((count * blk // outs, attn_in.shape[1]), bf16)] * outs
        + [before] * (2 if base else 0),
        compiler_params=params(60),
        cost_estimate=taking(10 * count),
        name="attention_backward",
    )(first, q3, k3, v3, kt, start_row, lse, attended, grad_att, cos, sin, cost, sint, attn_in, *(carry if carried else ()), *wait)


def mix_kernel(me_ref, own_ref, gain_ref, *refs, base, own_blocks, others, parts, pieces, per):
    other, refs = refs[:others], refs[others:]
    attended, refs = refs[: parts * pieces], refs[parts * pieces :]
    weights = refs[:parts]
    middle_ref, normed_ref = refs[-2:]
    i = pl.program_id(0)
    mine = (base + i) // own_blocks == me_ref[0]
    x = own_ref[...].astype(f32)
    if others:
        x = jnp.where(mine, x, chosen((base + i) % own_blocks, other, own_blocks // others).astype(f32))
    for n in range(parts):
        x = x + dot(chosen(i, attended[n * pieces : (n + 1) * pieces], per), weights[n][...])
    middle_ref[...] = x
    inverse = lax.rsqrt(jnp.mean(x * x, axis=-1, keepdims=True) + EPSILON)
    normed_ref[...] = (x * inverse * gain_ref[...]).astype(bf16)


def mix(me, low, bucket_rows, own_x, other_x, gain_row, attended, weights, before=None, wait=(), blk=BLK):
    own_rows, dim = own_x.shape
    own_blocks = own_rows // blk
    parts, pieces = len(attended), len(attended[0])
    per = attended[0][0].shape[0] // blk
    base, count = low // blk, pieces * per
    extra = () if before is None else tuple(before)
    at_x = lambda i, m: ((base + i) % own_blocks, 0)
    at = lambda i, m: (base + i, 0)
    return pl.pallas_call(
        functools.partial(
            mix_kernel, base=base, own_blocks=own_blocks, others=len(other_x), parts=parts, pieces=pieces, per=per
        ),
        grid_spec=pltpu.PrefetchScalarGridSpec(
            num_scalar_prefetch=1,
            grid=(count,),
            in_specs=[
                pl.BlockSpec((blk, dim), at_x),
                pl.BlockSpec((1, dim), lambda i, m: (0, 0)),
            ]
            + [
                pl.BlockSpec((blk, dim), lambda i, m, k=k, n=own_blocks // len(other_x): (jnp.clip((base + i) % own_blocks - k * n, 0, n - 1), 0))
                for k in range(len(other_x))
            ]
            + [
                pl.BlockSpec((blk, a.shape[1]), lambda i, m, k=k: (jnp.clip(i - k * per, 0, per - 1), 0))
                for part in attended
                for k, a in enumerate(part)
            ]
            + [pl.BlockSpec(w.shape, lambda i, m: (0, 0), **ONE) for w in weights]
            + [ANY] * (len(extra) + len(wait)),
            out_specs=[pl.BlockSpec((blk, dim), at)] * 2,
        ),
        out_shape=[jax.ShapeDtypeStruct((bucket_rows, dim), f32), jax.ShapeDtypeStruct((bucket_rows, dim), bf16)],
        input_output_aliases={3 + len(other_x) + parts * (pieces + 1) + n: n for n in range(len(extra))},
        compiler_params=params(48),
        name="mix",
    )(scalar(me), own_x, gain_row[None, :], *other_x, *[a for part in attended for a in part], *weights, *extra, *wait)


def ff_forward_kernel(base_ref, x_ref, wg_ref, wu_ref, *refs, rc):
    g_ref, u_ref, act_ref = refs[-3:]

    for low in range(0, x_ref.shape[0], rc):
        at = slice(low, low + rc)
        x = x_ref[at, :]
        g = dot(x, wg_ref[...])
        u = dot(x, wu_ref[...])
        g_ref[at, :] = g
        u_ref[at, :] = u
        act_ref[at, :] = (g * (1.0 / (1.0 + jnp.exp(-g))) * u).astype(bf16)


def ff_forward(x, base, rows, mlp_in, wait=(), hb=512, rc=512):
    dim = x.shape[1]
    hidden = mlp_in.shape[2]
    hb = block_of(hidden, hb)
    rc = block_of(rows, rc)
    return pl.pallas_call(
        functools.partial(ff_forward_kernel, rc=rc),
        grid_spec=pltpu.PrefetchScalarGridSpec(
            num_scalar_prefetch=1,
            grid=(hidden // hb,),
            in_specs=[
                pl.BlockSpec((rows, dim), lambda h, b: (b[0], 0), **ONE),
                pl.BlockSpec((None, dim, hb), lambda h, b: (0, 0, h)),
                pl.BlockSpec((None, dim, hb), lambda h, b: (1, 0, h)),
            ]
            + [ANY] * len(wait),
            out_specs=[pl.BlockSpec((rows, hb), lambda h, b: (0, h))] * 3,
        ),
        out_shape=[jax.ShapeDtypeStruct((rows, hidden), f32)] * 2 + [jax.ShapeDtypeStruct((rows, hidden), bf16)],
        compiler_params=params(60),
        cost_estimate=taking(19),
        name="ff_forward",
    )(scalar(base), x, mlp_in, mlp_in, *wait)


def ff_output_kernel(me_ref, act_ref, w_ref, *refs, pieces, per, whole):
    total = dot(act_ref[...], w_ref[...])
    if whole:
        total = total + refs[0][...] + chosen(pl.program_id(0), refs[1 : 1 + pieces], per).astype(f32)
    refs[-1][...] = total.astype(bf16)


def ff_output(me, act, low, high, mlp_out, middle=None, got=(), wait=(), blk=BLK):
    hidden, dim = mlp_out.shape
    base, count = low // blk, (high - low) // blk
    whole = middle is not None
    per = got[0].shape[0] // blk if got else 1
    return pl.pallas_call(
        functools.partial(ff_output_kernel, pieces=len(got), per=per, whole=whole),
        grid_spec=pltpu.PrefetchScalarGridSpec(
            num_scalar_prefetch=1,
            grid=(count,),
            in_specs=[pl.BlockSpec((blk, hidden), lambda i, m: (base + i, 0)), pl.BlockSpec((hidden, dim), lambda i, m: (0, 0), **ONE)]
            + [pl.BlockSpec((blk, dim), lambda i, m: (m[0] * count + i, 0))] * (1 if whole else 0)
            + in_turn(len(got), per, blk, dim)
            + [ANY] * len(wait),
            out_specs=pl.BlockSpec((blk, dim), lambda i, m: (i, 0)),
        ),
        out_shape=jax.ShapeDtypeStruct((high - low, dim), bf16),
        compiler_params=params(48),
        cost_estimate=taking(1.8 * count),
        name="ff_output",
    )(scalar(me), act, mlp_out, *((middle,) if whole else ()), *got, *wait)


def ff_backward_kernel(*refs, rc, pieces, outs):
    og, refs = refs[:pieces], refs[pieces:]
    g_ref, u_ref, wg_ref, wu_ref, wo_ref = refs[:5]
    gn, (gg_ref, gu_ref, acc_ref) = refs[-3 - outs : -3], refs[-3:]
    rows = acc_ref.shape[0]

    @pl.when(pl.program_id(0) == 0)
    def _():
        acc_ref[...] = jnp.zeros_like(acc_ref)

    def by_rows(og_ref, low, r):
        here = slice(r * rc, (r + 1) * rc)
        at = slice(low + r * rc, low + (r + 1) * rc)
        ga = dot(og_ref[here, :], wo_ref[...], NT)
        g = g_ref[at, :]
        s = 1.0 / (1.0 + jnp.exp(-g))
        silu = g * s
        gg = (ga * u_ref[at, :] * (s * (1.0 + g * (1.0 - s)))).astype(bf16)
        gu = (ga * silu).astype(bf16)
        gg_ref[at, :] = gg
        gu_ref[at, :] = gu
        acc_ref[at, :] += dot(gg, wg_ref[...], NT) + dot(gu, wu_ref[...], NT)

    low = 0
    for og_ref in og:
        count = og_ref.shape[0] // rc
        for r in range(count):
            by_rows(og_ref, low, r)
        low += og_ref.shape[0]

    @pl.when(pl.program_id(0) == pl.num_programs(0) - 1)
    def _():
        for n, out in enumerate(gn):
            out[...] = acc_ref[n * out.shape[0] : (n + 1) * out.shape[0], :].astype(out.dtype)


def ff_backward(og, g, u, mlp_in, mlp_out, dtype, outs=1, wait=(), hb=512, rc=512):
    rows, hidden = g.shape
    dim = mlp_out.shape[1]
    hb = block_of(hidden, hb)
    rc = block_of(og[0].shape[0], rc)
    return pl.pallas_call(
        functools.partial(ff_backward_kernel, rc=rc, pieces=len(og), outs=outs),
        grid=(hidden // hb,),
        in_specs=[pl.BlockSpec(a.shape, lambda h: (0, 0), **ONE) for a in og]
        + [
            pl.BlockSpec((rows, hb), lambda h: (0, h)),
            pl.BlockSpec((rows, hb), lambda h: (0, h)),
            pl.BlockSpec((None, dim, hb), lambda h: (0, 0, h)),
            pl.BlockSpec((None, dim, hb), lambda h: (1, 0, h)),
            pl.BlockSpec((hb, dim), lambda h: (h, 0)),
        ]
        + [ANY] * len(wait),
        out_specs=[pl.BlockSpec((rows // outs, dim), lambda h: (0, 0), **ONE)] * outs + [pl.BlockSpec((rows, hb), lambda h: (0, h))] * 2,
        scratch_shapes=[pltpu.VMEM((rows, dim), f32)],
        out_shape=[jax.ShapeDtypeStruct((rows // outs, dim), dtype)] * outs + [jax.ShapeDtypeStruct((rows, hidden), bf16)] * 2,
        compiler_params=params(60),
        cost_estimate=taking(33),
        name="ff_backward",
    )(*og, g, u, mlp_in, mlp_in, mlp_out, *wait)


def store_split(total, first, share, side, keep_ref, send_ref):
    for n in range(0, total.shape[0] // share, 2):
        even = total[n * share : (n + 1) * share]
        odd = total[(n + 1) * share : (n + 2) * share]
        at = slice((first // share + n) // 2 * share, ((first // share + n) // 2 + 1) * share)
        keep_ref[at, :] = jnp.where(side == 0, even, odd).astype(bf16)
        send_ref[at, :] = jnp.where(side == 0, odd, even).astype(bf16)


def weights_kernel(base_ref, *refs, pieces, outs, share, cc):
    lhs, rhs, out = refs[:pieces], refs[pieces : 2 * pieces], refs[-outs:]
    dim = lhs[0].shape[1]

    def product(at):
        total = None
        for x_ref, r_ref in zip(lhs, rhs):
            part = dot(x_ref[:, at], r_ref[...], TN)
            total = part if total is None else total + part
        return total

    if outs == 2:
        for first in range(0, dim, cc):
            store_split(product(slice(first, first + cc)), first, share, base_ref[1], *out)
        return

    def by_columns(t, c):
        at = pl.ds(pl.multiple_of(t * cc, cc), cc)
        out[0][at, :] = product(at).astype(bf16)
        return c

    lax.fori_loop(0, dim // cc, by_columns, 0)


def weight_gradient(base, terms, side=None, share=None, wait=(), hb=512, cc=640):
    dim = terms[0][0].shape[1]
    columns = terms[0][2].shape[1]
    hb = block_of(columns, hb)
    outs = 1 if side is None else 2
    table = jnp.stack([jnp.asarray(base, jnp.int32), jnp.asarray(0 if side is None else side, jnp.int32)])
    return pl.pallas_call(
        functools.partial(weights_kernel, pieces=len(terms), outs=outs, share=share, cc=cc),
        grid_spec=pltpu.PrefetchScalarGridSpec(
            num_scalar_prefetch=1,
            grid=(columns // hb,),
            in_specs=[pl.BlockSpec((n, dim), lambda h, b, m=m: (m(b[0]), 0), **ONE) for _, m, _, _, n in terms]
            + [pl.BlockSpec((n, hb), lambda h, b, k=k: (k, h)) for _, _, _, k, n in terms]
            + [ANY] * len(wait),
            out_specs=[pl.BlockSpec((dim // outs, hb), lambda h, b: (0, h))] * outs,
        ),
        out_shape=[jax.ShapeDtypeStruct((dim // outs, columns), bf16)] * outs,
        compiler_params=params(60),
        cost_estimate=taking(20),
        name="weight_gradient",
    )(table, *[t[0] for t in terms], *[t[2] for t in terms], *wait)


def attn_weights_kernel(n_ref, *refs, lows, cc):
    parts, out_ref = refs[: len(lows)], refs[-1]

    def by_columns(t, c):
        at = pl.ds(pl.multiple_of(t * cc, cc), cc)
        total = None
        for low, g_ref in zip(lows, parts):
            part = dot(n_ref[low : low + g_ref.shape[0], at], g_ref[...], TN)
            total = part if total is None else total + part
        out_ref[at, :] = total.astype(bf16)
        return c

    lax.fori_loop(0, n_ref.shape[1] // cc, by_columns, 0)


def attn_weight_gradient(normed_one, lows, grad_qkv, wait=(), cc=640):
    rows, dim = normed_one.shape
    cols = grad_qkv[0].shape[2]
    return pl.pallas_call(
        functools.partial(attn_weights_kernel, lows=lows, cc=cc),
        grid=(3,),
        in_specs=[pl.BlockSpec((rows, dim), lambda j: (0, 0), **ONE)]
        + [pl.BlockSpec((None, g.shape[1], cols), lambda j: (j, 0, 0)) for g in grad_qkv]
        + [ANY] * len(wait),
        out_specs=pl.BlockSpec((dim, cols), lambda j: (0, j)) if cols % LANES == 0 else pl.BlockSpec((None, dim, cols), lambda j: (j, 0, 0)),
        out_shape=jax.ShapeDtypeStruct((dim, 3 * cols) if cols % LANES == 0 else (3, dim, cols), bf16),
        compiler_params=params(56),
        cost_estimate=taking(18),
        name="attn_weight_gradient",
    )(normed_one, *grad_qkv, *wait)


def norm_input_part(z, gain, e):
    inverse = lax.rsqrt(jnp.mean(z * z, axis=-1, keepdims=True) + EPSILON)
    weighted = e * gain
    inner = jnp.mean(weighted * z, axis=-1, keepdims=True)
    return weighted * inverse - z * (inverse * inverse * inverse) * inner


def middle_backward_kernel(me_ref, og_ref, z_ref, own_ref, gain_ref, *refs, pieces, per, parts):
    got, refs = refs[:pieces], refs[pieces:]
    weights, refs = refs[:parts], refs[-2 - parts :]
    i = pl.program_id(0)
    e = own_ref[...]
    if pieces:
        e = e + chosen(i, got, per).astype(f32)
    grad = og_ref[...].astype(f32) + norm_input_part(z_ref[...], gain_ref[...], e)
    refs[0][...] = grad
    branch = grad.astype(bf16)
    refs[1][...] = branch
    for w, out in zip(weights, refs[2:]):
        out[...] = dot(branch, w[...], NT).astype(bf16)


def middle_backward(me, out_grad, middle, gn_own, got_gn, gain_row, weights, wait=(), blk=BLK):
    rows, dim = out_grad.shape
    pieces = len(got_gn)
    per = got_gn[0].shape[0] // blk if pieces else 1
    own_blocks = rows // blk
    at = lambda i, m: (i, 0)
    return pl.pallas_call(
        functools.partial(middle_backward_kernel, pieces=pieces, per=per, parts=len(weights)),
        grid_spec=pltpu.PrefetchScalarGridSpec(
            num_scalar_prefetch=1,
            grid=(own_blocks,),
            in_specs=[
                pl.BlockSpec((blk, dim), at),
                pl.BlockSpec((blk, dim), lambda i, m: (m[0] * own_blocks + i, 0)),
                pl.BlockSpec((blk, dim), at),
                pl.BlockSpec((1, dim), lambda i, m: (0, 0)),
            ]
            + in_turn(pieces, per, blk, dim)
            + [pl.BlockSpec(w.shape, lambda i, m: (0, 0), **ONE) for w in weights]
            + [ANY] * len(wait),
            out_specs=[pl.BlockSpec((blk, dim), at)] * 2 + [pl.BlockSpec((blk, w.shape[0]), at) for w in weights],
        ),
        out_shape=[jax.ShapeDtypeStruct((rows, dim), f32), jax.ShapeDtypeStruct((rows, dim), bf16)]
        + [jax.ShapeDtypeStruct((rows, w.shape[0]), bf16) for w in weights],
        compiler_params=params(48),
        cost_estimate=taking(12),
        name="middle_backward",
    )(scalar(me), out_grad, middle, gn_own, gain_row[None, :], *got_gn, *weights, *wait)


def tokens_backward_kernel(me_ref, x_ref, grad_ref, gain_ref, *refs, sides):
    i = pl.program_id(0)
    out_ref, refs = refs[-1], refs[:-1]
    e = None
    for n, ((count, each), (more, every)) in enumerate(sides):
        own, got, refs = refs[:count], refs[count : count + more], refs[count + more :]
        here = chosen(i, own, each) + chosen(i, got, every).astype(f32)
        e = here if e is None else jnp.where(me_ref[0] == n, here, e)
    out_ref[...] = (grad_ref[...] + norm_input_part(x_ref[...].astype(f32), gain_ref[...], e)).astype(bf16)


def tokens_backward(me, tokens, grad_middle, gain_row, sides, blk=BLK):
    rows, dim = tokens.shape
    at = lambda i, m: (i, 0)
    shape = tuple(tuple((len(part), part[0].shape[0] // blk) for part in side) for side in sides)
    specs = [spec for side in shape for part in side for spec in in_turn(*part, blk, dim)]
    return pl.pallas_call(
        functools.partial(tokens_backward_kernel, sides=shape),
        grid_spec=pltpu.PrefetchScalarGridSpec(
            num_scalar_prefetch=1,
            grid=(rows // blk,),
            in_specs=[pl.BlockSpec((blk, dim), at), pl.BlockSpec((blk, dim), at), pl.BlockSpec((1, dim), lambda i, m: (0, 0))] + specs,
            out_specs=pl.BlockSpec((blk, dim), at),
        ),
        out_shape=jax.ShapeDtypeStruct((rows, dim), bf16),
        compiler_params=params(48),
        cost_estimate=taking(10),
        name="tokens_backward",
    )(scalar(me), tokens, grad_middle, gain_row[None, :], *[a for own, got in sides for a in (*own, *got)])


def contract(a, b, dims):
    return lax.dot_general(a, b, (dims, ((), ())), preferred_element_type=f32)


def after(value, *others):
    return lax.optimization_barrier((value, *others))[0]


SWAP = ((0, 1), (1, 0))


def halving_step(state, group, n_dp, behind):
    bit, send, keep = state
    got = lax.ppermute(send, "dp", [(n, n ^ (1 << bit)) for n in range(n_dp)])
    keep, behind = lax.optimization_barrier((keep, behind))
    if n_dp >> bit == 2:
        return (bit + 1, got, keep), behind
    split = lambda a: a.reshape(n_dp >> (bit + 2), 2, -1, a.shape[-1])
    side = (group >> (bit + 1)) & 1

    def pick(at):
        parts = [lax.dynamic_index_in_dim(split(a), at, 1, False).astype(f32) for a in (keep, got)]
        return (parts[0] + parts[1]).astype(bf16).reshape(-1, keep.shape[-1])

    return (bit + 1, pick(1 - side), pick(side)), behind


def halving_end(state):
    _, got, keep = state
    return keep.astype(f32) + got.astype(f32)


def per_device(tokens, norm_gains, attn_in, attn_out, mlp_in, mlp_out, lengths, out_grad):
    n_mp = lax.axis_size("mp")
    n_dp = lax.axis_size("dp")
    me = lax.axis_index("mp")
    group = lax.axis_index("dp")
    rows, dim = tokens.shape
    bucket = rows * n_mp
    hd = HEAD_DIM
    cols = attn_out.shape[0]
    hidden = mlp_out.shape[0]
    share = dim // n_dp
    scale = hd**-0.5
    pair = n_mp == 2
    hb = block_of(hidden, 512)
    places, starts = layout(lengths[0], bucket)
    tables = turning(places - starts, hd)
    cos, sin = tables[:2]
    first = starts[::BLK] // BLK
    start_row = starts.reshape(bucket // BLK, 1, BLK)
    own_blocks = rows // BLK

    def mine(array, axis, size):
        return lax.dynamic_slice_in_dim(array, group * size, size, axis)

    def swap(array):
        return lax.ppermute(array, "mp", SWAP)

    def scatter(array):
        return lax.psum_scatter(array, "dp", scatter_dimension=0, tiled=True)

    chunk = rows // 2
    halves = (0, chunk)
    whole = lambda b: 0
    if pair:
        piece = swap(mine(attn_out, 0, cols // n_dp))
        other_attn_out = lax.all_gather(piece, "dp", axis=0, tiled=True)
        other_x = [swap(tokens[low : low + chunk]) for low in halves]
        projected = project(tokens, me * own_blocks, bucket, norm_gains[0], attn_in, cos, sin, hd, wait=(piece,))
        att, lse, att_got = [], [], []
        for n, low in enumerate(range(0, bucket, chunk)):
            if n < 2:
                projected = project(
                    other_x[n], (1 - me) * own_blocks + n * own_blocks // 2, bucket, norm_gains[0], attn_in, cos, sin, hd,
                    projected, wait=tuple(att),
                )
            normed_one, q3, k3, v3, kt, vt = projected
            wait = tuple(att_got[n - 2 : n - 1]) if n > 1 else ()
            if n == 1:
                wait = (other_attn_out,)
            a, l = attention_forward(first, low, low + chunk, q3, k3, vt, start_row, hd, scale, tuple(att[-1:]) + wait)
            att.append(a)
            lse.append(l)
            att_got.append(swap(a))
        got_grad = [out_grad[low : low + chunk] for low in halves]
        *got_grad, att_got[2] = lax.optimization_barrier((*got_grad, att_got[2]))
        got_grad = [swap(a) for a in got_grad]
        mix_rows = lambda low, these, before: mix(
            me, low, bucket, tokens, other_x, norm_gains[1], (att[these], att_got[these]), (attn_out, other_attn_out), before
        )
        middle_all, normed_two = mix_rows(3 * chunk, slice(3, 4), mix_rows(0, slice(0, 3), None))
        other = 1 - me
        g_b, u_b, act_b = ff_forward(normed_two, other, rows, mlp_in)
        g_a, u_a, act_a = ff_forward(normed_two, me, rows, mlp_in, wait=(act_b, got_grad[0]))
        (gw_out,) = weight_gradient(
            0,
            [(got_grad[n], whole, act_b, n, chunk) for n in range(2)] + [(out_grad, whole, act_a, 0, rows)],
            wait=(act_a,),
        )
        sum_out = scatter(gw_out)
        *got_gn, gg_b, gu_b = ff_backward(got_grad, g_b, u_b, mlp_in, mlp_out, bf16, 2, wait=(gw_out,))
        got_gn = [swap(a) for a in got_gn]
        gn_a, gg_a, gu_a = ff_backward([out_grad], g_a, u_a, mlp_in, mlp_out, f32, wait=(gg_b,))
        side = lambda b, a: [(normed_two, lambda b: 1 - b, b, 0, rows), (normed_two, lambda b: b, a, 0, rows)]
        (gw_gate,) = weight_gradient(me, side(gg_b, gg_a), wait=(gn_a, got_gn[0]))
        sum_gate = scatter(gw_gate)
        grad_middle, branch_grad, do_own, do_send = middle_backward(
            me, out_grad, middle_all, gn_a, got_gn, norm_gains[1], (attn_out, other_attn_out), wait=(gw_gate,)
        )
    else:
        all_x = lax.all_gather(tokens, "mp", axis=0, tiled=True)
        normed_one, q3, k3, v3, kt, vt = project(all_x, 0, bucket, norm_gains[0], attn_in, cos, sin, hd)
        att_all, lse_all = attention_forward(first, 0, bucket, q3, k3, vt, start_row, hd, scale)
        every_head = lax.all_gather(att_all, "mp", axis=1, tiled=True)
        every_out = lax.all_gather(attn_out, "mp", axis=0, tiled=True)
        middle_all, normed_two = mix(0, 0, bucket, all_x, (), norm_gains[1], ((every_head,),), (every_out,))
        all_grad = lax.all_gather(out_grad, "mp", axis=0, tiled=True)
        g_b, u_b, act_b = ff_forward(normed_two, 0, bucket, mlp_in)
        gn_b, gg_b, gu_b = ff_backward([all_grad], g_b, u_b, mlp_in, mlp_out, bf16)
        sum_out = scatter(weight_gradient(0, [(all_grad, whole, act_b, 0, bucket)])[0])
        sum_gate = scatter(weight_gradient(0, [(normed_two, whole, gg_b, 0, bucket)])[0])
        sum_up = scatter(weight_gradient(0, [(normed_two, whole, gu_b, 0, bucket)])[0])
        grad_normed_two = lax.psum_scatter(gn_b, "mp", scatter_dimension=0, tiled=True).astype(f32)
        grad_middle, branch_grad = middle_backward(me, out_grad, middle_all, grad_normed_two, (), norm_gains[1], ())
        middle = lax.dynamic_slice_in_dim(middle_all, me * rows, rows, 0)
        out_b = ff_output(0, act_b, 0, bucket, mlp_out)
        output = (middle + lax.psum_scatter(out_b, "mp", scatter_dimension=0, tiled=True).astype(f32)).astype(bf16)
    if pair:
        do_got = swap(do_send)
        up_keep, up_send = weight_gradient(me, side(gu_b, gu_a), group & 1, share, wait=(do_send,))
        up = (0, up_send, up_keep)
        out_b = [ff_output(me, act_b, low, low + chunk, mlp_out, wait=(up_keep,)) for low in halves]
        att_own = jnp.where(me == 0, jnp.concatenate(att[:2]), jnp.concatenate(att[2:]))
        att_other = jnp.where(me == 0, jnp.concatenate(att_got[:2]), jnp.concatenate(att_got[2:]))
        gw_attn_out = jnp.concatenate(
            [contract(branch_grad, a, ((0,), (0,))).astype(bf16) for a in (att_own, att_other)], axis=1
        )
        up, gw_attn_out = halving_step(up, group, n_dp, gw_attn_out)
        sum_attn_out = scatter(gw_attn_out)
        got_out = [swap(a) for a in out_b]
        do_low = jnp.where(me == 0, do_own, do_got)
        do_high = jnp.where(me == 0, do_got, do_own)
        grad_att = {0: do_low[:chunk], chunk: do_low[chunk:], rows: do_high}
        lse_of = {0: lse[0], chunk: lse[1], rows: jnp.concatenate(lse[2:], axis=1)}
        att_of = {0: att[0], chunk: att[1], rows: jnp.concatenate(att[2:], axis=0)}
        carry, grad_qkv, own_part, got_part = None, {}, {}, {}
        for low, high in ((rows, bucket), (chunk, rows), (0, chunk)):
            wait = {rows: (sum_out,), chunk: (sum_gate, got_out[0]), 0: (got_out[1],) + tuple(got_part.get(rows, ())[:1])}[low]
            made = attention_backward(
                first, low, high, q3, k3, v3, kt, start_row, lse_of[low], att_of[low], grad_att[low], tables, attn_in, hd, scale,
                carry, (high - low) // chunk, wait + (up[1],),
            )
            send = made[2 : 2 + (high - low) // chunk]
            own_part[low], carry = made[1], made[2 + len(send) :]
            up, grad_qkv[low] = halving_step(up, group, n_dp, made[0])
            path = ((0, 1),) if low == rows else ((1, 0),)
            got_part[low] = [lax.ppermute(a, "mp", path) for a in send]
        grad_tokens = tokens_backward(
            me,
            tokens,
            grad_middle,
            norm_gains[0],
            (([own_part[0], own_part[chunk]], got_part[0] + got_part[chunk]), ([own_part[rows]], got_part[rows])),
        )
        lows = (0, chunk, rows)
        gw_attn_in = attn_weight_gradient(normed_one, lows, [grad_qkv[low] for low in lows], wait=(sum_attn_out, got_part[rows][1], got_part[chunk][0]))
        sum_up = halving_end(up)
    else:
        all_branch = lax.all_gather(branch_grad, "mp", axis=0, tiled=True)
        grad_heads = contract(all_branch, attn_out, ((1,), (1,))).astype(bf16)
        gw_attn_out = contract(all_branch, att_all, ((0,), (0,))).astype(bf16)
        made = attention_backward(
            first, 0, bucket, q3, k3, v3, kt, start_row, lse_all, att_all, grad_heads, tables, attn_in, hd, scale, None
        )
        grad_qkv, grad_normed_one = made[0], lax.psum_scatter(made[2], "mp", scatter_dimension=0, tiled=True)
        nothing = jnp.zeros((rows, dim), f32)
        grad_tokens = tokens_backward(0, tokens, grad_middle, norm_gains[0], (((nothing,), (grad_normed_one,)),))
        gw_attn_in = attn_weight_gradient(normed_one, (0,), [grad_qkv])
        if gw_attn_in.ndim == 3:
            gw_attn_in = gw_attn_in.transpose(1, 0, 2).reshape(dim, 3 * cols)
    if pair:
        output = ff_output(me, act_a, 0, rows, mlp_out, middle_all, got_out, wait=(gw_attn_in,))
    sum_in = jnp.stack([sum_gate.astype(f32), sum_up.astype(f32)])
    sum_out = sum_out.astype(f32)
    if not pair:
        sum_attn_out = scatter(gw_attn_out)
    sum_attn_out = sum_attn_out.astype(f32)
    if pair:
        sum_attn_out = sum_attn_out[:, :cols] + swap(sum_attn_out[:, cols:].astype(bf16)).astype(f32)
    sum_attn_in, grad_tokens, output = lax.optimization_barrier((scatter(gw_attn_in), grad_tokens, output))
    sum_attn_in = sum_attn_in.astype(f32).reshape(share, 3, cols).transpose(1, 0, 2)
    gain_one = jnp.sum(mine(attn_in, 1, share).astype(f32) * sum_attn_in, axis=(0, 2))
    gain_two = jnp.sum(mine(mlp_in, 1, share).astype(f32) * sum_in, axis=(0, 2))
    gains = jnp.stack([gain_one, gain_two]) / mine(norm_gains, 1, share)
    if pair:
        halves = gains.reshape(2, 2, share // 2)
        gains = lax.dynamic_index_in_dim(halves, me, 1, False) + swap(lax.dynamic_index_in_dim(halves, 1 - me, 1, False))
    else:
        gains = lax.psum_scatter(gains, "mp", scatter_dimension=1, tiled=True)
    return (output, grad_tokens, gains, sum_attn_in, sum_attn_out.T, sum_in, sum_out.T)


def solution(mesh):
    placed = (
        P(("dp", "mp"), None),
        P(),
        P(None, None, "mp"),
        P("mp", None),
        P(None, None, "mp"),
        P("mp", None),
        P("dp", None),
        P(("dp", "mp"), None),
    )
    return jax.shard_map(
        per_device,
        mesh=mesh,
        in_specs=placed,
        out_specs=(
            P(("dp", "mp"), None),
            P(("dp", "mp"), None),
            P(None, ("dp", "mp")),
            P(None, "dp", "mp"),
            P("mp", "dp"),
            P(None, "dp", "mp"),
            P("mp", "dp"),
        ),
        check_vma=False,
    )
```

```python
import functools

import jax
import jax.numpy as jnp
from jax import lax
from jax.experimental import pallas as pl
from jax.experimental.pallas import tpu as pltpu
from jax.sharding import PartitionSpec as P

BLK = 256
LANES = 128
HEAD_DIM = 80
EPSILON = 1e-06
LOG2E = 1.4426950408889634
NEG = -1e30
bf16 = jnp.bfloat16
f32 = jnp.float32
NT = (((1,), (1,)), ((), ()))
NN = (((1,), (0,)), ((), ()))
TN = (((0,), (0,)), ((), ()))
FLOPS = 2_500_000_000
ONE = dict(pipeline_mode=pl.Buffered(1))


def dot(a, b, contract=NN):
    return lax.dot_general(a, b, contract, preferred_element_type=f32)


ANY = pl.BlockSpec(memory_space=pl.ANY)


def taking(micros):
    return pl.CostEstimate(flops=int(micros * FLOPS), bytes_accessed=1 << 20, transcendentals=0)


def params(mib):
    return pltpu.CompilerParams(vmem_limit_bytes=mib << 20)


def block_of(size, most):
    return next(b for b in (most, 1024, 512, 256, 128) if b <= most and size % b == 0)


def scalar(value):
    return jnp.reshape(value, (1,)).astype(jnp.int32)


def chosen(i, refs, per):
    value = refs[0][...]
    for k in range(1, len(refs)):
        value = jnp.where(i // per == k, refs[k][...], value)
    return value


def in_turn(count, per, blk, wide):
    return [pl.BlockSpec((blk, wide), lambda i, m, k=k: (jnp.clip(i - k * per, 0, per - 1), 0)) for k in range(count)]


def layout(lengths_row, bucket_rows):
    series_ends = jnp.cumsum(lengths_row, dtype=jnp.int32)
    places = jnp.arange(bucket_rows, dtype=jnp.int32)
    before = series_ends[None, :] <= places[:, None]
    starts = jnp.sum(jnp.where(before, lengths_row[None, :], 0), axis=1, dtype=jnp.int32)
    return places, starts


def turning(position, hd):
    half = hd // 2
    frequency = 10000.0 ** (-(jnp.arange(half, dtype=f32) * 2.0 / hd))
    place = position.astype(f32)
    turned = frequency[:, None] * place[None, :]
    wide = jnp.concatenate([frequency, frequency, jnp.zeros((LANES - hd,), f32)])
    angles = place[:, None] * wide[None, :]
    return jnp.cos(angles), jnp.sin(angles), jnp.cos(turned), jnp.sin(turned)


def project_kernel(base_ref, x_ref, gain_ref, w_ref, cos_ref, sin_ref, *refs, hd):
    n_ref, q_ref, k_ref, v_ref, kt_ref, vt_ref = refs[-6:]
    heads, rows, lanes = q_ref.shape
    half = hd // 2
    x = x_ref[...].astype(f32)
    inverse = lax.rsqrt(jnp.mean(x * x, axis=-1, keepdims=True) + EPSILON)
    normed = (x * inverse * gain_ref[...]).astype(bf16)
    n_ref[...] = normed
    cos = cos_ref[...]
    lane = lax.broadcasted_iota(jnp.int32, (rows, lanes), 1)
    sin = jnp.where(lane < half, -sin_ref[...], sin_ref[...])
    pad = jnp.zeros((rows, lanes - hd), f32)
    for j, out in enumerate((q_ref, k_ref, v_ref)):
        y = dot(normed, w_ref[j])
        for h in range(heads):
            part = jnp.concatenate([y[:, h * hd : (h + 1) * hd], pad], axis=1)
            if j < 2:
                part = part * cos + jnp.where(lane < half, pltpu.roll(part, lanes - half, 1), pltpu.roll(part, half, 1)) * sin
            part = part.astype(bf16)
            out[h] = part
            if j == 1:
                kt_ref[h] = part.T
            if j == 2:
                vt_ref[h] = part.T


def project(x, base, bucket_rows, gain_row, attn_in, cos, sin, hd, before=None, wait=(), blk=BLK):
    rows, dim = x.shape
    heads = attn_in.shape[2] // hd
    at = lambda i, b: (b[0] + i, 0)
    at_heads = lambda i, b: (0, b[0] + i, 0)
    at_turned = lambda i, b: (0, 0, b[0] + i)
    extra = () if before is None else tuple(before)
    return pl.pallas_call(
        functools.partial(project_kernel, hd=hd),
        grid_spec=pltpu.PrefetchScalarGridSpec(
            num_scalar_prefetch=1,
            grid=(rows // blk,),
            in_specs=[
                pl.BlockSpec((blk, dim), lambda i, b: (i, 0)),
                pl.BlockSpec((1, dim), lambda i, b: (0, 0)),
                pl.BlockSpec(attn_in.shape, lambda i, b: (0, 0, 0), **ONE),
                pl.BlockSpec((blk, LANES), at),
                pl.BlockSpec((blk, LANES), at),
            ]
            + [ANY] * (len(extra) + len(wait)),
            out_specs=[pl.BlockSpec((blk, dim), at)]
            + [pl.BlockSpec((heads, blk, LANES), at_heads)] * 3
            + [pl.BlockSpec((heads, LANES, blk), at_turned)] * 2,
        ),
        out_shape=[jax.ShapeDtypeStruct((bucket_rows, dim), bf16)]
        + [jax.ShapeDtypeStruct((heads, bucket_rows, LANES), bf16)] * 3
        + [jax.ShapeDtypeStruct((heads, LANES, bucket_rows), bf16)] * 2,
        input_output_aliases={6 + n: n for n in range(len(extra))},
        compiler_params=params(56),
        cost_estimate=taking(20 * rows // 1024),
        name="project",
    )(scalar(base), x, gain_row[None, :], attn_in, cos, sin, *extra, *wait)


def allowed_mask(j, i, start_row, blk):
    kpos = j * blk + lax.broadcasted_iota(jnp.int32, (blk, blk), 0)
    qpos = i * blk + lax.broadcasted_iota(jnp.int32, (blk, blk), 1)
    return (kpos >= start_row) & (kpos <= qpos)


def attention_forward_kernel(first_ref, q_ref, k_ref, vt_ref, start_ref, *refs, base, blk, hd, scale):
    o_ref, lse_ref, acc_ref, m_ref, l_ref, a_ref, s_ref, p_ref = refs[-8:]
    heads = k_ref.shape[0]
    i = base + pl.program_id(0)
    acc_ref[...] = jnp.zeros_like(acc_ref)
    m_ref[...] = jnp.full_like(m_ref, NEG)
    l_ref[...] = jnp.zeros_like(l_ref)
    c2 = scale * LOG2E

    def step(j, carry):
        mask = allowed_mask(j, i, start_ref[0], blk)
        rows = pl.ds(pl.multiple_of(j * blk, blk), blk)
        for h in range(heads):
            s_ref[h] = dot(k_ref[h, rows, :], q_ref[h], NT)
        for h in range(heads):
            s = jnp.where(mask, s_ref[h] * c2, NEG)
            m_old = m_ref[h : h + 1]
            m_new = jnp.maximum(m_old, jnp.max(s, axis=0, keepdims=True))
            alpha = jnp.exp2(m_old - m_new)
            p = jnp.exp2(s - m_new)
            l_ref[h : h + 1] = alpha * l_ref[h : h + 1] + jnp.sum(p, axis=0, keepdims=True)
            m_ref[h : h + 1] = m_new
            a_ref[h : h + 1] = alpha
            p_ref[h] = p.astype(bf16)
        for h in range(heads):
            part = slice(h * hd, (h + 1) * hd)
            acc_ref[part, :] = a_ref[h : h + 1] * acc_ref[part, :] + dot(vt_ref[h, :hd, rows], p_ref[h])
        return carry

    lax.fori_loop(0, i - first_ref[i] + 1, lambda n, c: step(i - n, c), 0)
    for h in range(heads):
        part = slice(h * hd, (h + 1) * hd)
        acc_ref[part, :] = acc_ref[part, :] / l_ref[h : h + 1]
    o_ref[...] = acc_ref[...].T.astype(bf16)
    lse_ref[...] = m_ref[...] + jnp.log2(l_ref[...])


def attention_forward(first, low, high, q3, k3, vt, start_row, hd, scale, wait=(), blk=BLK):
    heads, rows, lanes = k3.shape
    base, count = low // blk, (high - low) // blk
    return pl.pallas_call(
        functools.partial(attention_forward_kernel, base=base, blk=blk, hd=hd, scale=scale),
        grid_spec=pltpu.PrefetchScalarGridSpec(
            num_scalar_prefetch=1,
            grid=(count,),
            in_specs=[
                pl.BlockSpec((heads, blk, lanes), lambda i, t: (0, i + base, 0)),
                pl.BlockSpec((heads, high, lanes), lambda i, t: (0, 0, 0), **ONE),
                pl.BlockSpec((heads, lanes, high), lambda i, t: (0, 0, 0), **ONE),
                pl.BlockSpec((1, 1, blk), lambda i, t: (i + base, 0, 0)),
            ]
            + [ANY] * len(wait),
            out_specs=[
                pl.BlockSpec((blk, heads * hd), lambda i, t: (i, 0)),
                pl.BlockSpec((heads, blk), lambda i, t: (0, i)),
            ],
            scratch_shapes=[
                pltpu.VMEM((heads * hd, blk), f32),
                pltpu.VMEM((heads, blk), f32),
                pltpu.VMEM((heads, blk), f32),
                pltpu.VMEM((heads, blk), f32),
                pltpu.VMEM((heads, blk, blk), f32),
                pltpu.VMEM((heads, blk, blk), bf16),
            ],
        ),
        out_shape=[
            jax.ShapeDtypeStruct((count * blk, heads * hd), bf16),
            jax.ShapeDtypeStruct((heads, count * blk), f32),
        ],
        compiler_params=params(56),
        cost_estimate=taking(5 * count),
        name="attention_forward",
    )(first, q3, k3, vt, start_row, *wait)


def attention_backward_kernel(
    first_ref, q_ref, k_ref, v_ref, kt_ref, start_ref, lse_ref, o_ref, do_ref, cos_ref, sin_ref, cost_ref, sint_ref, w_ref, *refs,
    base, count, blk, hd, scale, carried, waits, outs,
):
    carry_in, refs = (refs[:2], refs[2:]) if carried else ((), refs)
    refs = refs[waits:]
    g_ref, wide_ref, narrow, refs = *refs[:2], refs[2 : 2 + outs], refs[2 + outs :]
    carry_out, refs = (refs[:2], refs[2:]) if base else ((), refs)
    do3_ref, dk_ref, dv_ref, dqt_ref, d_ref, s_ref, dp_ref, p_ref, ds_ref = refs
    heads, rows, lanes = k_ref.shape
    half = hd // 2
    step_at = pl.program_id(0)
    i = base + count - 1 - step_at

    @pl.when(step_at == 0)
    def _():
        do3_ref[...] = jnp.zeros_like(do3_ref)
        if carried:
            dk_ref[...] = carry_in[0][...]
            dv_ref[...] = carry_in[1][...]
        else:
            dk_ref[...] = jnp.zeros_like(dk_ref)
            dv_ref[...] = jnp.zeros_like(dv_ref)

    for h in range(heads):
        do3_ref[h, :, :hd] = do_ref[:, h * hd : (h + 1) * hd]
    prod = do_ref[...].astype(f32) * o_ref[...].astype(f32)
    high = prod.astype(bf16)
    low = (prod - high.astype(f32)).astype(bf16)
    pad_heads = d_ref.shape[0]
    owner = lax.broadcasted_iota(jnp.int32, (pad_heads, heads * hd), 1) // hd
    pick = (owner == lax.broadcasted_iota(jnp.int32, (pad_heads, heads * hd), 0)).astype(f32).astype(bf16)
    d_ref[...] = dot(pick, high, NT) + dot(pick, low, NT)
    dqt_ref[...] = jnp.zeros_like(dqt_ref)
    c2 = scale * LOG2E

    def step(j, carry):
        mask = allowed_mask(j, i, start_ref[0], blk)
        at = pl.ds(pl.multiple_of(j * blk, blk), blk)
        for h in range(heads):
            s_ref[h] = dot(k_ref[h, at, :], q_ref[h], NT)
            dp_ref[h] = dot(v_ref[h, at, :], do3_ref[h], NT)
        for h in range(heads):
            p = jnp.where(mask, jnp.exp2(s_ref[h] * c2 - lse_ref[h : h + 1]), 0.0)
            p_ref[h] = p.astype(bf16)
            ds_ref[h] = (p * (dp_ref[h] - d_ref[h : h + 1])).astype(bf16)
        for h in range(heads):
            dv_ref[h, at, :] += dot(p_ref[h], do3_ref[h])
            dk_ref[h, at, :] += dot(ds_ref[h], q_ref[h])
            part = slice(h * hd, (h + 1) * hd)
            dqt_ref[part, :] += dot(kt_ref[h, :hd, at], ds_ref[h])
        return carry

    lax.fori_loop(first_ref[i], i + 1, step, 0)
    ct = cost_ref[...]
    st = sint_ref[...]
    for h in range(heads):
        a = dqt_ref[h * hd : h * hd + half, :] * scale
        b = dqt_ref[h * hd + half : (h + 1) * hd, :] * scale
        dqt_ref[h * hd : h * hd + half, :] = a * ct + b * st
        dqt_ref[h * hd + half : (h + 1) * hd, :] = b * ct - a * st
    g_ref[0] = dqt_ref[...].T.astype(bf16)
    at = pl.ds(pl.multiple_of(i * blk, blk), blk)
    cos, sin = cos_ref[...], sin_ref[...]
    lane = lax.broadcasted_iota(jnp.int32, (blk, lanes), 1)
    for h in range(heads):
        x = dk_ref[h, at, :] * scale
        other = jnp.where(lane < half, pltpu.roll(x, lanes - half, 1), -pltpu.roll(x, half, 1))
        g_ref[1, :, h * hd : (h + 1) * hd] = (x * cos + other * sin).astype(bf16)[:, :hd]
        g_ref[2, :, h * hd : (h + 1) * hd] = dv_ref[h, at, :].astype(bf16)[:, :hd]
    total = dot(g_ref[0], w_ref[0], NT) + dot(g_ref[1], w_ref[1], NT) + dot(g_ref[2], w_ref[2], NT)
    wide_ref[...] = total
    for n in range(outs):

        @pl.when((i - base) // (count // outs) == n)
        def _():
            narrow[n][...] = total.astype(bf16)
    if base:

        @pl.when(step_at == count - 1)
        def _():
            carry_out[0][...] = dk_ref[:, : base * blk, :]
            carry_out[1][...] = dv_ref[:, : base * blk, :]


def attention_backward(first, low, high, q3, k3, v3, kt, start_row, lse, attended, grad_att, tables, attn_in, hd, scale, carry, outs=1, wait=(), blk=BLK):
    heads, rows, lanes = k3.shape
    base, count = low // blk, (high - low) // blk
    cos, sin, cost, sint = tables
    pad_heads = max(8, heads)
    half = hd // 2
    here = lambda i: count - 1 - i
    there = lambda i: base + count - 1 - i
    carried = carry is not None
    before = jax.ShapeDtypeStruct((heads, low, lanes), f32)
    return pl.pallas_call(
        functools.partial(attention_backward_kernel, base=base, count=count, blk=blk, hd=hd, scale=scale, carried=carried, waits=len(wait), outs=outs),
        grid_spec=pltpu.PrefetchScalarGridSpec(
            num_scalar_prefetch=1,
            grid=(count,),
            in_specs=[
                pl.BlockSpec((heads, blk, lanes), lambda i, t: (0, there(i), 0)),
                pl.BlockSpec((heads, high, lanes), lambda i, t: (0, 0, 0), **ONE),
                pl.BlockSpec((heads, high, lanes), lambda i, t: (0, 0, 0), **ONE),
                pl.BlockSpec((heads, lanes, high), lambda i, t: (0, 0, 0), **ONE),
                pl.BlockSpec((1, 1, blk), lambda i, t: (there(i), 0, 0)),
                pl.BlockSpec((heads, blk), lambda i, t: (0, here(i))),
                pl.BlockSpec((blk, heads * hd), lambda i, t: (here(i), 0)),
                pl.BlockSpec((blk, heads * hd), lambda i, t: (here(i), 0)),
                pl.BlockSpec((blk, lanes), lambda i, t: (there(i), 0)),
                pl.BlockSpec((blk, lanes), lambda i, t: (there(i), 0)),
                pl.BlockSpec((half, blk), lambda i, t: (0, there(i))),
                pl.BlockSpec((half, blk), lambda i, t: (0, there(i))),
                pl.BlockSpec(attn_in.shape, lambda i, t: (0, 0, 0), **ONE),
            ]
            + [pl.BlockSpec((heads, high, lanes), lambda i, t: (0, 0, 0), **ONE)] * (2 if carried else 0)
            + [ANY] * len(wait),
            out_specs=[pl.BlockSpec((3, blk, heads * hd), lambda i, t: (0, here(i), 0))]
            + [pl.BlockSpec((blk, attn_in.shape[1]), lambda i, t: (here(i), 0))]
            + [
                pl.BlockSpec((blk, attn_in.shape[1]), lambda i, t, k=k, n=count // outs: (jnp.clip(here(i) - k * n, 0, n - 1), 0))
                for k in range(outs)
            ]
            + [pl.BlockSpec((heads, low, lanes), lambda i, t: (0, 0, 0), **ONE)] * (2 if base else 0),
            scratch_shapes=[
                pltpu.VMEM((heads, blk, lanes), bf16),
                pltpu.VMEM((heads, high, lanes), f32),
                pltpu.VMEM((heads, high, lanes), f32),
                pltpu.VMEM((heads * hd, blk), f32),
                pltpu.VMEM((pad_heads, blk), f32),
                pltpu.VMEM((heads, blk, blk), f32),
                pltpu.VMEM((heads, blk, blk), f32),
                pltpu.VMEM((heads, blk, blk), bf16),
                pltpu.VMEM((heads, blk, blk), bf16),
            ],
        ),
        out_shape=[
            jax.ShapeDtypeStruct((3, count * blk, heads * hd), bf16),
            jax.ShapeDtypeStruct((count * blk, attn_in.shape[1]), f32),
        ]
        + [jax.ShapeDtypeStruct((count * blk // outs, attn_in.shape[1]), bf16)] * outs
        + [before] * (2 if base else 0),
        compiler_params=params(60),
        cost_estimate=taking(10 * count),
        name="attention_backward",
    )(first, q3, k3, v3, kt, start_row, lse, attended, grad_att, cos, sin, cost, sint, attn_in, *(carry if carried else ()), *wait)


def mix_kernel(me_ref, own_ref, gain_ref, *refs, base, own_blocks, others, parts, pieces, per):
    other, refs = refs[:others], refs[others:]
    attended, refs = refs[: parts * pieces], refs[parts * pieces :]
    weights = refs[:parts]
    middle_ref, normed_ref = refs[-2:]
    i = pl.program_id(0)
    mine = (base + i) // own_blocks == me_ref[0]
    x = own_ref[...].astype(f32)
    if others:
        x = jnp.where(mine, x, chosen((base + i) % own_blocks, other, own_blocks // others).astype(f32))
    for n in range(parts):
        x = x + dot(chosen(i, attended[n * pieces : (n + 1) * pieces], per), weights[n][...])
    middle_ref[...] = x
    inverse = lax.rsqrt(jnp.mean(x * x, axis=-1, keepdims=True) + EPSILON)
    normed_ref[...] = (x * inverse * gain_ref[...]).astype(bf16)


def mix(me, low, bucket_rows, own_x, other_x, gain_row, attended, weights, before=None, wait=(), blk=BLK):
    own_rows, dim = own_x.shape
    own_blocks = own_rows // blk
    parts, pieces = len(attended), len(attended[0])
    per = attended[0][0].shape[0] // blk
    base, count = low // blk, pieces * per
    extra = () if before is None else tuple(before)
    at_x = lambda i, m: ((base + i) % own_blocks, 0)
    at = lambda i, m: (base + i, 0)
    return pl.pallas_call(
        functools.partial(
            mix_kernel, base=base, own_blocks=own_blocks, others=len(other_x), parts=parts, pieces=pieces, per=per
        ),
        grid_spec=pltpu.PrefetchScalarGridSpec(
            num_scalar_prefetch=1,
            grid=(count,),
            in_specs=[
                pl.BlockSpec((blk, dim), at_x),
                pl.BlockSpec((1, dim), lambda i, m: (0, 0)),
            ]
            + [
                pl.BlockSpec((blk, dim), lambda i, m, k=k, n=own_blocks // len(other_x): (jnp.clip((base + i) % own_blocks - k * n, 0, n - 1), 0))
                for k in range(len(other_x))
            ]
            + [
                pl.BlockSpec((blk, a.shape[1]), lambda i, m, k=k: (jnp.clip(i - k * per, 0, per - 1), 0))
                for part in attended
                for k, a in enumerate(part)
            ]
            + [pl.BlockSpec(w.shape, lambda i, m: (0, 0), **ONE) for w in weights]
            + [ANY] * (len(extra) + len(wait)),
            out_specs=[pl.BlockSpec((blk, dim), at)] * 2,
        ),
        out_shape=[jax.ShapeDtypeStruct((bucket_rows, dim), f32), jax.ShapeDtypeStruct((bucket_rows, dim), bf16)],
        input_output_aliases={3 + len(other_x) + parts * (pieces + 1) + n: n for n in range(len(extra))},
        compiler_params=params(48),
        name="mix",
    )(scalar(me), own_x, gain_row[None, :], *other_x, *[a for part in attended for a in part], *weights, *extra, *wait)


def ff_forward_kernel(base_ref, x_ref, wg_ref, wu_ref, *refs, rc):
    g_ref, u_ref, act_ref = refs[-3:]

    for low in range(0, x_ref.shape[0], rc):
        at = slice(low, low + rc)
        x = x_ref[at, :]
        g = dot(x, wg_ref[...])
        u = dot(x, wu_ref[...])
        g_ref[at, :] = g
        u_ref[at, :] = u
        act_ref[at, :] = (g * (1.0 / (1.0 + jnp.exp(-g))) * u).astype(bf16)


def ff_forward(x, base, rows, mlp_in, wait=(), hb=512, rc=512):
    dim = x.shape[1]
    hidden = mlp_in.shape[2]
    hb = block_of(hidden, hb)
    rc = block_of(rows, rc)
    return pl.pallas_call(
        functools.partial(ff_forward_kernel, rc=rc),
        grid_spec=pltpu.PrefetchScalarGridSpec(
            num_scalar_prefetch=1,
            grid=(hidden // hb,),
            in_specs=[
                pl.BlockSpec((rows, dim), lambda h, b: (b[0], 0), **ONE),
                pl.BlockSpec((None, dim, hb), lambda h, b: (0, 0, h)),
                pl.BlockSpec((None, dim, hb), lambda h, b: (1, 0, h)),
            ]
            + [ANY] * len(wait),
            out_specs=[pl.BlockSpec((rows, hb), lambda h, b: (0, h))] * 3,
        ),
        out_shape=[jax.ShapeDtypeStruct((rows, hidden), f32)] * 2 + [jax.ShapeDtypeStruct((rows, hidden), bf16)],
        compiler_params=params(60),
        cost_estimate=taking(19),
        name="ff_forward",
    )(scalar(base), x, mlp_in, mlp_in, *wait)


def ff_output_kernel(me_ref, act_ref, w_ref, *refs, pieces, per, whole):
    total = dot(act_ref[...], w_ref[...])
    if whole:
        total = total + refs[0][...] + chosen(pl.program_id(0), refs[1 : 1 + pieces], per).astype(f32)
    refs[-1][...] = total.astype(bf16)


def ff_output(me, act, low, high, mlp_out, middle=None, got=(), wait=(), blk=BLK):
    hidden, dim = mlp_out.shape
    base, count = low // blk, (high - low) // blk
    whole = middle is not None
    per = got[0].shape[0] // blk if got else 1
    return pl.pallas_call(
        functools.partial(ff_output_kernel, pieces=len(got), per=per, whole=whole),
        grid_spec=pltpu.PrefetchScalarGridSpec(
            num_scalar_prefetch=1,
            grid=(count,),
            in_specs=[pl.BlockSpec((blk, hidden), lambda i, m: (base + i, 0)), pl.BlockSpec((hidden, dim), lambda i, m: (0, 0), **ONE)]
            + [pl.BlockSpec((blk, dim), lambda i, m: (m[0] * count + i, 0))] * (1 if whole else 0)
            + in_turn(len(got), per, blk, dim)
            + [ANY] * len(wait),
            out_specs=pl.BlockSpec((blk, dim), lambda i, m: (i, 0)),
        ),
        out_shape=jax.ShapeDtypeStruct((high - low, dim), bf16),
        compiler_params=params(48),
        cost_estimate=taking(1.8 * count),
        name="ff_output",
    )(scalar(me), act, mlp_out, *((middle,) if whole else ()), *got, *wait)


def ff_backward_kernel(*refs, rc, pieces, outs):
    og, refs = refs[:pieces], refs[pieces:]
    g_ref, u_ref, wg_ref, wu_ref, wo_ref = refs[:5]
    gn, (gg_ref, gu_ref, acc_ref) = refs[-3 - outs : -3], refs[-3:]
    rows = acc_ref.shape[0]

    @pl.when(pl.program_id(0) == 0)
    def _():
        acc_ref[...] = jnp.zeros_like(acc_ref)

    def by_rows(og_ref, low, r):
        here = slice(r * rc, (r + 1) * rc)
        at = slice(low + r * rc, low + (r + 1) * rc)
        ga = dot(og_ref[here, :], wo_ref[...], NT)
        g = g_ref[at, :]
        s = 1.0 / (1.0 + jnp.exp(-g))
        silu = g * s
        gg = (ga * u_ref[at, :] * (s * (1.0 + g * (1.0 - s)))).astype(bf16)
        gu = (ga * silu).astype(bf16)
        gg_ref[at, :] = gg
        gu_ref[at, :] = gu
        acc_ref[at, :] += dot(gg, wg_ref[...], NT) + dot(gu, wu_ref[...], NT)

    low = 0
    for og_ref in og:
        count = og_ref.shape[0] // rc
        for r in range(count):
            by_rows(og_ref, low, r)
        low += og_ref.shape[0]

    @pl.when(pl.program_id(0) == pl.num_programs(0) - 1)
    def _():
        for n, out in enumerate(gn):
            out[...] = acc_ref[n * out.shape[0] : (n + 1) * out.shape[0], :].astype(out.dtype)


def ff_backward(og, g, u, mlp_in, mlp_out, dtype, outs=1, wait=(), hb=512, rc=512):
    rows, hidden = g.shape
    dim = mlp_out.shape[1]
    hb = block_of(hidden, hb)
    rc = block_of(og[0].shape[0], rc)
    return pl.pallas_call(
        functools.partial(ff_backward_kernel, rc=rc, pieces=len(og), outs=outs),
        grid=(hidden // hb,),
        in_specs=[pl.BlockSpec(a.shape, lambda h: (0, 0), **ONE) for a in og]
        + [
            pl.BlockSpec((rows, hb), lambda h: (0, h)),
            pl.BlockSpec((rows, hb), lambda h: (0, h)),
            pl.BlockSpec((None, dim, hb), lambda h: (0, 0, h)),
            pl.BlockSpec((None, dim, hb), lambda h: (1, 0, h)),
            pl.BlockSpec((hb, dim), lambda h: (h, 0)),
        ]
        + [ANY] * len(wait),
        out_specs=[pl.BlockSpec((rows // outs, dim), lambda h: (0, 0), **ONE)] * outs + [pl.BlockSpec((rows, hb), lambda h: (0, h))] * 2,
        scratch_shapes=[pltpu.VMEM((rows, dim), f32)],
        out_shape=[jax.ShapeDtypeStruct((rows // outs, dim), dtype)] * outs + [jax.ShapeDtypeStruct((rows, hidden), bf16)] * 2,
        compiler_params=params(60),
        cost_estimate=taking(33),
        name="ff_backward",
    )(*og, g, u, mlp_in, mlp_in, mlp_out, *wait)


def store_split(total, first, share, side, keep_ref, send_ref):
    for n in range(0, total.shape[0] // share, 2):
        even = total[n * share : (n + 1) * share]
        odd = total[(n + 1) * share : (n + 2) * share]
        at = slice((first // share + n) // 2 * share, ((first // share + n) // 2 + 1) * share)
        keep_ref[at, :] = jnp.where(side == 0, even, odd).astype(bf16)
        send_ref[at, :] = jnp.where(side == 0, odd, even).astype(bf16)


def weights_kernel(base_ref, *refs, pieces, outs, share, cc):
    lhs, rhs, out = refs[:pieces], refs[pieces : 2 * pieces], refs[-outs:]
    dim = lhs[0].shape[1]

    def product(at):
        total = None
        for x_ref, r_ref in zip(lhs, rhs):
            part = dot(x_ref[:, at], r_ref[...], TN)
            total = part if total is None else total + part
        return total

    if outs == 2:
        for first in range(0, dim, cc):
            store_split(product(slice(first, first + cc)), first, share, base_ref[1], *out)
        return

    def by_columns(t, c):
        at = pl.ds(pl.multiple_of(t * cc, cc), cc)
        out[0][at, :] = product(at).astype(bf16)
        return c

    lax.fori_loop(0, dim // cc, by_columns, 0)


def weight_gradient(base, terms, side=None, share=None, wait=(), hb=512, cc=640):
    dim = terms[0][0].shape[1]
    columns = terms[0][2].shape[1]
    hb = block_of(columns, hb)
    outs = 1 if side is None else 2
    table = jnp.stack([jnp.asarray(base, jnp.int32), jnp.asarray(0 if side is None else side, jnp.int32)])
    return pl.pallas_call(
        functools.partial(weights_kernel, pieces=len(terms), outs=outs, share=share, cc=cc),
        grid_spec=pltpu.PrefetchScalarGridSpec(
            num_scalar_prefetch=1,
            grid=(columns // hb,),
            in_specs=[pl.BlockSpec((n, dim), lambda h, b, m=m: (m(b[0]), 0), **ONE) for _, m, _, _, n in terms]
            + [pl.BlockSpec((n, hb), lambda h, b, k=k: (k, h)) for _, _, _, k, n in terms]
            + [ANY] * len(wait),
            out_specs=[pl.BlockSpec((dim // outs, hb), lambda h, b: (0, h))] * outs,
        ),
        out_shape=[jax.ShapeDtypeStruct((dim // outs, columns), bf16)] * outs,
        compiler_params=params(60),
        cost_estimate=taking(20),
        name="weight_gradient",
    )(table, *[t[0] for t in terms], *[t[2] for t in terms], *wait)


def attn_weights_kernel(side_ref, n_ref, *refs, lows, outs, share, cc):
    parts, out = refs[: len(lows)], refs[-outs:]

    def product(at):
        total = None
        for low, g_ref in zip(lows, parts):
            part = dot(n_ref[low : low + g_ref.shape[0], at], g_ref[...], TN)
            total = part if total is None else total + part
        return total

    for first in range(0, n_ref.shape[1], cc):
        at = slice(first, first + cc)
        if outs == 2:
            store_split(product(at), first, share, side_ref[0], *out)
        else:
            out[0][at, :] = product(at).astype(bf16)


def attn_weight_gradient(normed_one, lows, grad_qkv, side=None, share=None, wait=(), cc=640):
    rows, dim = normed_one.shape
    cols = grad_qkv[0].shape[2]
    outs = 1 if side is None else 2
    flat = cols % LANES == 0
    spec = pl.BlockSpec((dim // outs, cols), lambda j, s: (0, j)) if flat else pl.BlockSpec((None, dim, cols), lambda j, s: (j, 0, 0))
    shape = (dim // outs, 3 * cols) if flat else (3, dim, cols)
    return pl.pallas_call(
        functools.partial(attn_weights_kernel, lows=lows, outs=outs, share=share, cc=cc),
        grid_spec=pltpu.PrefetchScalarGridSpec(
            num_scalar_prefetch=1,
            grid=(3,),
            in_specs=[pl.BlockSpec((rows, dim), lambda j, s: (0, 0), **ONE)]
            + [pl.BlockSpec((None, g.shape[1], cols), lambda j, s: (j, 0, 0)) for g in grad_qkv]
            + [ANY] * len(wait),
            out_specs=[spec] * outs,
        ),
        out_shape=[jax.ShapeDtypeStruct(shape, bf16)] * outs,
        compiler_params=params(56),
        cost_estimate=taking(18),
        name="attn_weight_gradient",
    )(scalar(0 if side is None else side), normed_one, *grad_qkv, *wait)


def norm_input_part(z, gain, e):
    inverse = lax.rsqrt(jnp.mean(z * z, axis=-1, keepdims=True) + EPSILON)
    weighted = e * gain
    inner = jnp.mean(weighted * z, axis=-1, keepdims=True)
    return weighted * inverse - z * (inverse * inverse * inverse) * inner


def middle_backward_kernel(me_ref, og_ref, z_ref, own_ref, gain_ref, *refs, pieces, per, parts):
    got, refs = refs[:pieces], refs[pieces:]
    weights, refs = refs[:parts], refs[-2 - parts :]
    i = pl.program_id(0)
    e = own_ref[...]
    if pieces:
        e = e + chosen(i, got, per).astype(f32)
    grad = og_ref[...].astype(f32) + norm_input_part(z_ref[...], gain_ref[...], e)
    refs[0][...] = grad
    branch = grad.astype(bf16)
    refs[1][...] = branch
    for w, out in zip(weights, refs[2:]):
        out[...] = dot(branch, w[...], NT).astype(bf16)


def middle_backward(me, out_grad, middle, gn_own, got_gn, gain_row, weights, wait=(), blk=BLK):
    rows, dim = out_grad.shape
    pieces = len(got_gn)
    per = got_gn[0].shape[0] // blk if pieces else 1
    own_blocks = rows // blk
    at = lambda i, m: (i, 0)
    return pl.pallas_call(
        functools.partial(middle_backward_kernel, pieces=pieces, per=per, parts=len(weights)),
        grid_spec=pltpu.PrefetchScalarGridSpec(
            num_scalar_prefetch=1,
            grid=(own_blocks,),
            in_specs=[
                pl.BlockSpec((blk, dim), at),
                pl.BlockSpec((blk, dim), lambda i, m: (m[0] * own_blocks + i, 0)),
                pl.BlockSpec((blk, dim), at),
                pl.BlockSpec((1, dim), lambda i, m: (0, 0)),
            ]
            + in_turn(pieces, per, blk, dim)
            + [pl.BlockSpec(w.shape, lambda i, m: (0, 0), **ONE) for w in weights]
            + [ANY] * len(wait),
            out_specs=[pl.BlockSpec((blk, dim), at)] * 2 + [pl.BlockSpec((blk, w.shape[0]), at) for w in weights],
        ),
        out_shape=[jax.ShapeDtypeStruct((rows, dim), f32), jax.ShapeDtypeStruct((rows, dim), bf16)]
        + [jax.ShapeDtypeStruct((rows, w.shape[0]), bf16) for w in weights],
        compiler_params=params(48),
        cost_estimate=taking(12),
        name="middle_backward",
    )(scalar(me), out_grad, middle, gn_own, gain_row[None, :], *got_gn, *weights, *wait)


def tokens_backward_kernel(me_ref, x_ref, grad_ref, gain_ref, *refs, sides):
    i = pl.program_id(0)
    out_ref, refs = refs[-1], refs[:-1]
    e = None
    for n, ((count, each), (more, every)) in enumerate(sides):
        own, got, refs = refs[:count], refs[count : count + more], refs[count + more :]
        here = chosen(i, own, each) + chosen(i, got, every).astype(f32)
        e = here if e is None else jnp.where(me_ref[0] == n, here, e)
    out_ref[...] = (grad_ref[...] + norm_input_part(x_ref[...].astype(f32), gain_ref[...], e)).astype(bf16)


def tokens_backward(me, tokens, grad_middle, gain_row, sides, wait=(), blk=BLK):
    rows, dim = tokens.shape
    at = lambda i, m: (i, 0)
    shape = tuple(tuple((len(part), part[0].shape[0] // blk) for part in side) for side in sides)
    specs = [spec for side in shape for part in side for spec in in_turn(*part, blk, dim)]
    return pl.pallas_call(
        functools.partial(tokens_backward_kernel, sides=shape),
        grid_spec=pltpu.PrefetchScalarGridSpec(
            num_scalar_prefetch=1,
            grid=(rows // blk,),
            in_specs=[pl.BlockSpec((blk, dim), at), pl.BlockSpec((blk, dim), at), pl.BlockSpec((1, dim), lambda i, m: (0, 0))] + specs
            + [ANY] * len(wait),
            out_specs=pl.BlockSpec((blk, dim), at),
        ),
        out_shape=jax.ShapeDtypeStruct((rows, dim), bf16),
        compiler_params=params(48),
        cost_estimate=taking(10),
        name="tokens_backward",
    )(scalar(me), tokens, grad_middle, gain_row[None, :], *[a for own, got in sides for a in (*own, *got)], *wait)


def contract(a, b, dims):
    return lax.dot_general(a, b, (dims, ((), ())), preferred_element_type=f32)


def after(value, *others):
    return lax.optimization_barrier((value, *others))[0]


SWAP = ((0, 1), (1, 0))


def halving_step(state, group, n_dp, behind):
    bit, send, keep = state
    got = lax.ppermute(send, "dp", [(n, n ^ (1 << bit)) for n in range(n_dp)])
    keep, behind = lax.optimization_barrier((keep, behind))
    if n_dp >> bit == 2:
        return (bit + 1, got, keep), behind
    split = lambda a: a.reshape(n_dp >> (bit + 2), 2, -1, a.shape[-1])
    side = (group >> (bit + 1)) & 1

    def pick(at):
        parts = [lax.dynamic_index_in_dim(split(a), at, 1, False).astype(f32) for a in (keep, got)]
        return (parts[0] + parts[1]).astype(bf16).reshape(-1, keep.shape[-1])

    return (bit + 1, pick(1 - side), pick(side)), behind


def halving_in_orders(got, keep, group, n_dp, orders, beside):
    partner = lambda a, bit: lax.ppermute(a, "dp", [(n, n ^ (1 << bit)) for n in range(n_dp)])
    share = keep.shape[0] * 2 // n_dp
    states, low, made = [], 0, []
    for width, bits in orders:
        states.append((keep[:, low : low + width], got[:, low : low + width], sorted(bits, reverse=True)))
        low += width
    for step in range(len(orders[0][1])):
        sent = []
        for n, (width, bits) in enumerate(orders):
            kept, came, left = states[n]
            axis = left.index(bits[step])
            view = lambda a: a.reshape((2,) * len(left) + (share, width))

            def pick(at):
                parts = [lax.dynamic_index_in_dim(view(a), at, axis, False).astype(f32) for a in (kept, came)]
                return (parts[0] + parts[1]).astype(bf16).reshape(-1, width)

            own = (group >> bits[step]) & 1
            sent.append(pick(1 - own))
            states[n] = (pick(own), partner(sent[-1], bits[step]), [b for b in left if b != bits[step]])
        if step < len(beside):
            made.append(beside[step](tuple(sent)))
            for n, (kept, came, left) in enumerate(states):
                kept, made[-1] = lax.optimization_barrier((kept, made[-1]))
                states[n] = (kept, came, left)
    return jnp.concatenate([kept.astype(f32) + came.astype(f32) for kept, came, _ in states], axis=1), made


def halving_end(state):
    _, got, keep = state
    return keep.astype(f32) + got.astype(f32)


def per_device(tokens, norm_gains, attn_in, attn_out, mlp_in, mlp_out, lengths, out_grad):
    n_mp = lax.axis_size("mp")
    n_dp = lax.axis_size("dp")
    me = lax.axis_index("mp")
    group = lax.axis_index("dp")
    rows, dim = tokens.shape
    bucket = rows * n_mp
    hd = HEAD_DIM
    cols = attn_out.shape[0]
    hidden = mlp_out.shape[0]
    share = dim // n_dp
    scale = hd**-0.5
    pair = n_mp == 2
    hb = block_of(hidden, 512)
    places, starts = layout(lengths[0], bucket)
    tables = turning(places - starts, hd)
    cos, sin = tables[:2]
    first = starts[::BLK] // BLK
    start_row = starts.reshape(bucket // BLK, 1, BLK)
    own_blocks = rows // BLK

    def mine(array, axis, size):
        return lax.dynamic_slice_in_dim(array, group * size, size, axis)

    def swap(array):
        return lax.ppermute(array, "mp", SWAP)

    def scatter(array):
        return lax.psum_scatter(array, "dp", scatter_dimension=0, tiled=True)

    chunk = rows // 2
    halves = (0, chunk)
    whole = lambda b: 0
    if pair:
        piece, lower = lax.optimization_barrier((mine(attn_out, 0, cols // n_dp), tokens[:chunk]))
        other_x = [swap(lower), swap(tokens[chunk:])]
        piece = swap(piece)
        other_attn_out = lax.all_gather(piece, "dp", axis=0, tiled=True)
        projected = project(tokens, me * own_blocks, bucket, norm_gains[0], attn_in, cos, sin, hd, wait=(piece,))
        att, lse, att_got = [], [], []
        for n, low in enumerate(range(0, bucket, chunk)):
            if n < 2:
                projected = project(
                    other_x[n], (1 - me) * own_blocks + n * own_blocks // 2, bucket, norm_gains[0], attn_in, cos, sin, hd,
                    projected, wait=tuple(att),
                )
            normed_one, q3, k3, v3, kt, vt = projected
            wait = tuple(att_got[n - 2 : n - 1]) if n > 1 else ()
            if n == 1:
                wait = (other_attn_out,)
            a, l = attention_forward(first, low, low + chunk, q3, k3, vt, start_row, hd, scale, tuple(att[-1:]) + wait)
            att.append(a)
            lse.append(l)
            att_got.append(swap(a))
        got_grad = [out_grad[low : low + chunk] for low in halves]
        *got_grad, att_got[2] = lax.optimization_barrier((*got_grad, att_got[2]))
        got_grad = [swap(a) for a in got_grad]
        mix_rows = lambda low, these, before: mix(
            me, low, bucket, tokens, other_x, norm_gains[1], (att[these], att_got[these]), (attn_out, other_attn_out), before
        )
        middle_all, normed_two = mix_rows(3 * chunk, slice(3, 4), mix_rows(0, slice(0, 3), None))
        other = 1 - me
        g_b, u_b, act_b = ff_forward(normed_two, other, rows, mlp_in)
        g_a, u_a, act_a = ff_forward(normed_two, me, rows, mlp_in, wait=(act_b, got_grad[0]))
        (gw_out,) = weight_gradient(
            0,
            [(got_grad[n], whole, act_b, n, chunk) for n in range(2)] + [(out_grad, whole, act_a, 0, rows)],
            wait=(act_a,),
        )
        sum_out = scatter(gw_out)
        *got_gn, gg_b, gu_b = ff_backward(got_grad, g_b, u_b, mlp_in, mlp_out, bf16, 2, wait=(gw_out,))
        got_gn = [swap(a) for a in got_gn]
        gn_a, gg_a, gu_a = ff_backward([out_grad], g_a, u_a, mlp_in, mlp_out, f32, wait=(gg_b,))
        side = lambda b, a: [(normed_two, lambda b: 1 - b, b, 0, rows), (normed_two, lambda b: b, a, 0, rows)]
        (gw_gate,) = weight_gradient(me, side(gg_b, gg_a), wait=(gn_a, got_gn[0]))
        sum_gate = scatter(gw_gate)
        grad_middle, branch_grad, do_own, do_send = middle_backward(
            me, out_grad, middle_all, gn_a, got_gn, norm_gains[1], (attn_out, other_attn_out), wait=(gw_gate, sum_out)
        )
    else:
        all_x = lax.all_gather(tokens, "mp", axis=0, tiled=True)
        normed_one, q3, k3, v3, kt, vt = project(all_x, 0, bucket, norm_gains[0], attn_in, cos, sin, hd)
        att_all, lse_all = attention_forward(first, 0, bucket, q3, k3, vt, start_row, hd, scale)
        every_head = lax.all_gather(att_all, "mp", axis=1, tiled=True)
        every_out = lax.all_gather(attn_out, "mp", axis=0, tiled=True)
        middle_all, normed_two = mix(0, 0, bucket, all_x, (), norm_gains[1], ((every_head,),), (every_out,))
        all_grad = lax.all_gather(out_grad, "mp", axis=0, tiled=True)
        g_b, u_b, act_b = ff_forward(normed_two, 0, bucket, mlp_in)
        gn_b, gg_b, gu_b = ff_backward([all_grad], g_b, u_b, mlp_in, mlp_out, bf16)
        sum_out = scatter(weight_gradient(0, [(all_grad, whole, act_b, 0, bucket)])[0])
        sum_gate = scatter(weight_gradient(0, [(normed_two, whole, gg_b, 0, bucket)])[0])
        sum_up = scatter(weight_gradient(0, [(normed_two, whole, gu_b, 0, bucket)])[0])
        grad_normed_two = lax.psum_scatter(gn_b, "mp", scatter_dimension=0, tiled=True).astype(f32)
        grad_middle, branch_grad = middle_backward(me, out_grad, middle_all, grad_normed_two, (), norm_gains[1], ())
        middle = lax.dynamic_slice_in_dim(middle_all, me * rows, rows, 0)
        out_b = ff_output(0, act_b, 0, bucket, mlp_out)
        output = (middle + lax.psum_scatter(out_b, "mp", scatter_dimension=0, tiled=True).astype(f32)).astype(bf16)
    if pair:
        do_got = swap(do_send)
        up_keep, up_send = weight_gradient(me, side(gu_b, gu_a), group & 1, share, wait=(do_send,))
        up = (0, up_send, up_keep)
        out_b = [ff_output(me, act_b, low, low + chunk, mlp_out, wait=(up_keep,)) for low in halves]
        att_own = jnp.where(me == 0, jnp.concatenate(att[:2]), jnp.concatenate(att[2:]))
        att_other = jnp.where(me == 0, jnp.concatenate(att_got[:2]), jnp.concatenate(att_got[2:]))
        gw_attn_out = jnp.concatenate(
            [contract(branch_grad, a, ((0,), (0,))).astype(bf16) for a in (att_own, att_other)], axis=1
        )
        up, gw_attn_out = halving_step(up, group, n_dp, gw_attn_out)
        sum_attn_out = scatter(gw_attn_out)
        got_out = [swap(a) for a in out_b]
        do_low = jnp.where(me == 0, do_own, do_got)
        do_high = jnp.where(me == 0, do_got, do_own)
        grad_att = {0: do_low[:chunk], chunk: do_low[chunk:], rows: do_high}
        lse_of = {0: lse[0], chunk: lse[1], rows: jnp.concatenate(lse[2:], axis=1)}
        att_of = {0: att[0], chunk: att[1], rows: jnp.concatenate(att[2:], axis=0)}
        carry, grad_qkv, own_part, got_part = None, {}, {}, {}
        for low, high in ((rows, bucket), (chunk, rows), (0, chunk)):
            wait = {rows: (), chunk: (sum_gate, got_out[0]), 0: (got_out[1],) + tuple(got_part.get(rows, ())[:1])}[low]
            made = attention_backward(
                first, low, high, q3, k3, v3, kt, start_row, lse_of[low], att_of[low], grad_att[low], tables, attn_in, hd, scale,
                carry, (high - low) // chunk, wait + (up[1],),
            )
            send = made[2 : 2 + (high - low) // chunk]
            own_part[low], carry = made[1], made[2 + len(send) :]
            up, grad_qkv[low] = halving_step(up, group, n_dp, made[0])
            path = ((0, 1),) if low == rows else ((1, 0),)
            got_part[low] = [lax.ppermute(a, "mp", path) for a in send]
        lows = (0, chunk, rows)
        in_keep, in_send = attn_weight_gradient(
            normed_one, lows, [grad_qkv[low] for low in lows], group & 1, share, wait=(sum_attn_out, got_part[rows][1], got_part[chunk][0], up[1])
        )
        bits = tuple(range(1, n_dp.bit_length() - 1))
        width = (3 * cols // 2 + LANES - 1) // LANES * LANES
        in_got = lax.ppermute(in_send, "dp", [(n, n ^ 1) for n in range(n_dp)])
        finish_output = lambda sent: ff_output(me, act_a, 0, rows, mlp_out, middle_all, got_out, wait=sent)
        finish_tokens = lambda sent: tokens_backward(
            me,
            tokens,
            grad_middle,
            norm_gains[0],
            (([own_part[0], own_part[chunk]], got_part[0] + got_part[chunk]), ([own_part[rows]], got_part[rows])),
            wait=sent,
        )
        sum_attn_in, (output, grad_tokens) = halving_in_orders(
            in_got, in_keep, group, n_dp, ((width, bits), (3 * cols - width, bits[1:] + bits[:1])), (finish_output, finish_tokens)
        )
        sum_up = halving_end(up)
    else:
        all_branch = lax.all_gather(branch_grad, "mp", axis=0, tiled=True)
        grad_heads = contract(all_branch, attn_out, ((1,), (1,))).astype(bf16)
        gw_attn_out = contract(all_branch, att_all, ((0,), (0,))).astype(bf16)
        made = attention_backward(
            first, 0, bucket, q3, k3, v3, kt, start_row, lse_all, att_all, grad_heads, tables, attn_in, hd, scale, None
        )
        grad_qkv, grad_normed_one = made[0], lax.psum_scatter(made[2], "mp", scatter_dimension=0, tiled=True)
        nothing = jnp.zeros((rows, dim), f32)
        grad_tokens = tokens_backward(0, tokens, grad_middle, norm_gains[0], (((nothing,), (grad_normed_one,)),))
        (gw_attn_in,) = attn_weight_gradient(normed_one, (0,), [grad_qkv])
        if gw_attn_in.ndim == 3:
            gw_attn_in = gw_attn_in.transpose(1, 0, 2).reshape(dim, 3 * cols)
        sum_attn_in = scatter(gw_attn_in).astype(f32)
    sum_in = jnp.stack([sum_gate.astype(f32), sum_up.astype(f32)])
    sum_out = sum_out.astype(f32)
    if not pair:
        sum_attn_out = scatter(gw_attn_out)
    sum_attn_out = sum_attn_out.astype(f32)
    if pair:
        sum_attn_out = sum_attn_out[:, :cols] + swap(sum_attn_out[:, cols:].astype(bf16)).astype(f32)
    sum_attn_in = sum_attn_in.reshape(share, 3, cols).transpose(1, 0, 2)
    gain_one = jnp.sum(mine(attn_in, 1, share).astype(f32) * sum_attn_in, axis=(0, 2))
    gain_two = jnp.sum(mine(mlp_in, 1, share).astype(f32) * sum_in, axis=(0, 2))
    gains = jnp.stack([gain_one, gain_two]) / mine(norm_gains, 1, share)
    if pair:
        halves = gains.reshape(2, 2, share // 2)
        gains = lax.dynamic_index_in_dim(halves, me, 1, False) + swap(lax.dynamic_index_in_dim(halves, 1 - me, 1, False))
    else:
        gains = lax.psum_scatter(gains, "mp", scatter_dimension=1, tiled=True)
    return (output, grad_tokens, gains, sum_attn_in, sum_attn_out.T, sum_in, sum_out.T)


def solution(mesh):
    placed = (
        P(("dp", "mp"), None),
        P(),
        P(None, None, "mp"),
        P("mp", None),
        P(None, None, "mp"),
        P("mp", None),
        P("dp", None),
        P(("dp", "mp"), None),
    )
    return jax.shard_map(
        per_device,
        mesh=mesh,
        in_specs=placed,
        out_specs=(
            P(("dp", "mp"), None),
            P(("dp", "mp"), None),
            P(None, ("dp", "mp")),
            P(None, "dp", "mp"),
            P("mp", "dp"),
            P(None, "dp", "mp"),
            P("mp", "dp"),
        ),
        check_vma=False,
    )
```

```python
import functools

import jax
import jax.numpy as jnp
from jax import lax
from jax.experimental import pallas as pl
from jax.experimental.pallas import tpu as pltpu
from jax.sharding import PartitionSpec as P

BLK = 256
LANES = 128
HEAD_DIM = 80
EPSILON = 1e-06
LOG2E = 1.4426950408889634
NEG = -1e30
bf16 = jnp.bfloat16
f32 = jnp.float32
NT = (((1,), (1,)), ((), ()))
NN = (((1,), (0,)), ((), ()))
TN = (((0,), (0,)), ((), ()))
FLOPS = 2_500_000_000
ONE = dict(pipeline_mode=pl.Buffered(1))


def dot(a, b, contract=NN):
    return lax.dot_general(a, b, contract, preferred_element_type=f32)


ANY = pl.BlockSpec(memory_space=pl.ANY)


def taking(micros):
    return pl.CostEstimate(flops=int(micros * FLOPS), bytes_accessed=1 << 20, transcendentals=0)


def params(mib):
    return pltpu.CompilerParams(vmem_limit_bytes=mib << 20)


def block_of(size, most):
    return next(b for b in (most, 1024, 512, 256, 128) if b <= most and size % b == 0)


def scalar(value):
    return jnp.reshape(value, (1,)).astype(jnp.int32)


def chosen(i, refs, per):
    value = refs[0][...]
    for k in range(1, len(refs)):
        value = jnp.where(i // per == k, refs[k][...], value)
    return value


def in_turn(count, per, blk, wide):
    return [pl.BlockSpec((blk, wide), lambda i, m, k=k: (jnp.clip(i - k * per, 0, per - 1), 0)) for k in range(count)]


def layout(lengths_row, bucket_rows):
    series_ends = jnp.cumsum(lengths_row, dtype=jnp.int32)
    places = jnp.arange(bucket_rows, dtype=jnp.int32)
    before = series_ends[None, :] <= places[:, None]
    starts = jnp.sum(jnp.where(before, lengths_row[None, :], 0), axis=1, dtype=jnp.int32)
    return places, starts


def turning(position, hd):
    half = hd // 2
    frequency = 10000.0 ** (-(jnp.arange(half, dtype=f32) * 2.0 / hd))
    place = position.astype(f32)
    turned = frequency[:, None] * place[None, :]
    wide = jnp.concatenate([frequency, frequency, jnp.zeros((LANES - hd,), f32)])
    angles = place[:, None] * wide[None, :]
    return jnp.cos(angles), jnp.sin(angles), jnp.cos(turned), jnp.sin(turned)


def project_kernel(base_ref, x_ref, gain_ref, w_ref, cos_ref, sin_ref, *refs, hd):
    n_ref, q_ref, k_ref, v_ref, kt_ref, vt_ref = refs[-6:]
    heads, rows, lanes = q_ref.shape
    half = hd // 2
    x = x_ref[...].astype(f32)
    inverse = lax.rsqrt(jnp.mean(x * x, axis=-1, keepdims=True) + EPSILON)
    normed = (x * inverse * gain_ref[...]).astype(bf16)
    n_ref[...] = normed
    cos = cos_ref[...]
    lane = lax.broadcasted_iota(jnp.int32, (rows, lanes), 1)
    sin = jnp.where(lane < half, -sin_ref[...], sin_ref[...])
    pad = jnp.zeros((rows, lanes - hd), f32)
    for j, out in enumerate((q_ref, k_ref, v_ref)):
        y = dot(normed, w_ref[j])
        for h in range(heads):
            part = jnp.concatenate([y[:, h * hd : (h + 1) * hd], pad], axis=1)
            if j < 2:
                part = part * cos + jnp.where(lane < half, pltpu.roll(part, lanes - half, 1), pltpu.roll(part, half, 1)) * sin
            part = part.astype(bf16)
            out[h] = part
            if j == 1:
                kt_ref[h] = part.T
            if j == 2:
                vt_ref[h] = part.T


def project(x, base, bucket_rows, gain_row, attn_in, cos, sin, hd, before=None, wait=(), blk=BLK):
    rows, dim = x.shape
    heads = attn_in.shape[2] // hd
    at = lambda i, b: (b[0] + i, 0)
    at_heads = lambda i, b: (0, b[0] + i, 0)
    at_turned = lambda i, b: (0, 0, b[0] + i)
    extra = () if before is None else tuple(before)
    return pl.pallas_call(
        functools.partial(project_kernel, hd=hd),
        grid_spec=pltpu.PrefetchScalarGridSpec(
            num_scalar_prefetch=1,
            grid=(rows // blk,),
            in_specs=[
                pl.BlockSpec((blk, dim), lambda i, b: (i, 0)),
                pl.BlockSpec((1, dim), lambda i, b: (0, 0)),
                pl.BlockSpec(attn_in.shape, lambda i, b: (0, 0, 0), **ONE),
                pl.BlockSpec((blk, LANES), at),
                pl.BlockSpec((blk, LANES), at),
            ]
            + [ANY] * (len(extra) + len(wait)),
            out_specs=[pl.BlockSpec((blk, dim), at)]
            + [pl.BlockSpec((heads, blk, LANES), at_heads)] * 3
            + [pl.BlockSpec((heads, LANES, blk), at_turned)] * 2,
        ),
        out_shape=[jax.ShapeDtypeStruct((bucket_rows, dim), bf16)]
        + [jax.ShapeDtypeStruct((heads, bucket_rows, LANES), bf16)] * 3
        + [jax.ShapeDtypeStruct((heads, LANES, bucket_rows), bf16)] * 2,
        input_output_aliases={6 + n: n for n in range(len(extra))},
        compiler_params=params(56),
        cost_estimate=taking(20 * rows // 1024),
        name="project",
    )(scalar(base), x, gain_row[None, :], attn_in, cos, sin, *extra, *wait)


def allowed_mask(j, i, start_row, blk):
    kpos = j * blk + lax.broadcasted_iota(jnp.int32, (blk, blk), 0)
    qpos = i * blk + lax.broadcasted_iota(jnp.int32, (blk, blk), 1)
    return (kpos >= start_row) & (kpos <= qpos)


def attention_forward_kernel(first_ref, q_ref, k_ref, vt_ref, start_ref, *refs, base, blk, hd, scale):
    o_ref, lse_ref, acc_ref, m_ref, l_ref, a_ref, s_ref, p_ref = refs[-8:]
    heads = k_ref.shape[0]
    i = base + pl.program_id(0)
    acc_ref[...] = jnp.zeros_like(acc_ref)
    m_ref[...] = jnp.full_like(m_ref, NEG)
    l_ref[...] = jnp.zeros_like(l_ref)
    c2 = scale * LOG2E

    def step(j, carry):
        mask = allowed_mask(j, i, start_ref[0], blk)
        rows = pl.ds(pl.multiple_of(j * blk, blk), blk)
        for h in range(heads):
            s_ref[h] = dot(k_ref[h, rows, :], q_ref[h], NT)
        for h in range(heads):
            s = jnp.where(mask, s_ref[h] * c2, NEG)
            m_old = m_ref[h : h + 1]
            m_new = jnp.maximum(m_old, jnp.max(s, axis=0, keepdims=True))
            alpha = jnp.exp2(m_old - m_new)
            p = jnp.exp2(s - m_new)
            l_ref[h : h + 1] = alpha * l_ref[h : h + 1] + jnp.sum(p, axis=0, keepdims=True)
            m_ref[h : h + 1] = m_new
            a_ref[h : h + 1] = alpha
            p_ref[h] = p.astype(bf16)
        for h in range(heads):
            part = slice(h * hd, (h + 1) * hd)
            acc_ref[part, :] = a_ref[h : h + 1] * acc_ref[part, :] + dot(vt_ref[h, :hd, rows], p_ref[h])
        return carry

    lax.fori_loop(0, i - first_ref[i] + 1, lambda n, c: step(i - n, c), 0)
    for h in range(heads):
        part = slice(h * hd, (h + 1) * hd)
        acc_ref[part, :] = acc_ref[part, :] / l_ref[h : h + 1]
    o_ref[...] = acc_ref[...].T.astype(bf16)
    lse_ref[...] = m_ref[...] + jnp.log2(l_ref[...])


def attention_forward(first, low, high, q3, k3, vt, start_row, hd, scale, wait=(), blk=BLK):
    heads, rows, lanes = k3.shape
    base, count = low // blk, (high - low) // blk
    return pl.pallas_call(
        functools.partial(attention_forward_kernel, base=base, blk=blk, hd=hd, scale=scale),
        grid_spec=pltpu.PrefetchScalarGridSpec(
            num_scalar_prefetch=1,
            grid=(count,),
            in_specs=[
                pl.BlockSpec((heads, blk, lanes), lambda i, t: (0, i + base, 0)),
                pl.BlockSpec((heads, high, lanes), lambda i, t: (0, 0, 0), **ONE),
                pl.BlockSpec((heads, lanes, high), lambda i, t: (0, 0, 0), **ONE),
                pl.BlockSpec((1, 1, blk), lambda i, t: (i + base, 0, 0)),
            ]
            + [ANY] * len(wait),
            out_specs=[
                pl.BlockSpec((blk, heads * hd), lambda i, t: (i, 0)),
                pl.BlockSpec((heads, blk), lambda i, t: (0, i)),
            ],
            scratch_shapes=[
                pltpu.VMEM((heads * hd, blk), f32),
                pltpu.VMEM((heads, blk), f32),
                pltpu.VMEM((heads, blk), f32),
                pltpu.VMEM((heads, blk), f32),
                pltpu.VMEM((heads, blk, blk), f32),
                pltpu.VMEM((heads, blk, blk), bf16),
            ],
        ),
        out_shape=[
            jax.ShapeDtypeStruct((count * blk, heads * hd), bf16),
            jax.ShapeDtypeStruct((heads, count * blk), f32),
        ],
        compiler_params=params(56),
        cost_estimate=taking(5 * count),
        name="attention_forward",
    )(first, q3, k3, vt, start_row, *wait)


def attention_backward_kernel(
    first_ref, q_ref, k_ref, v_ref, kt_ref, start_ref, lse_ref, o_ref, do_ref, cos_ref, sin_ref, cost_ref, sint_ref, w_ref, *refs,
    base, count, blk, hd, scale, carried, waits, outs,
):
    carry_in, refs = (refs[:2], refs[2:]) if carried else ((), refs)
    refs = refs[waits:]
    g_ref, wide_ref, narrow, refs = *refs[:2], refs[2 : 2 + outs], refs[2 + outs :]
    carry_out, refs = (refs[:2], refs[2:]) if base else ((), refs)
    do3_ref, dk_ref, dv_ref, dqt_ref, d_ref, s_ref, dp_ref, p_ref, ds_ref = refs
    heads, rows, lanes = k_ref.shape
    half = hd // 2
    step_at = pl.program_id(0)
    i = base + count - 1 - step_at

    @pl.when(step_at == 0)
    def _():
        do3_ref[...] = jnp.zeros_like(do3_ref)
        if carried:
            dk_ref[...] = carry_in[0][...]
            dv_ref[...] = carry_in[1][...]
        else:
            dk_ref[...] = jnp.zeros_like(dk_ref)
            dv_ref[...] = jnp.zeros_like(dv_ref)

    for h in range(heads):
        do3_ref[h, :, :hd] = do_ref[:, h * hd : (h + 1) * hd]
    prod = do_ref[...].astype(f32) * o_ref[...].astype(f32)
    high = prod.astype(bf16)
    low = (prod - high.astype(f32)).astype(bf16)
    pad_heads = d_ref.shape[0]
    owner = lax.broadcasted_iota(jnp.int32, (pad_heads, heads * hd), 1) // hd
    pick = (owner == lax.broadcasted_iota(jnp.int32, (pad_heads, heads * hd), 0)).astype(f32).astype(bf16)
    d_ref[...] = dot(pick, high, NT) + dot(pick, low, NT)
    dqt_ref[...] = jnp.zeros_like(dqt_ref)
    c2 = scale * LOG2E

    def step(j, carry):
        mask = allowed_mask(j, i, start_ref[0], blk)
        at = pl.ds(pl.multiple_of(j * blk, blk), blk)
        for h in range(heads):
            s_ref[h] = dot(k_ref[h, at, :], q_ref[h], NT)
            dp_ref[h] = dot(v_ref[h, at, :], do3_ref[h], NT)
        for h in range(heads):
            p = jnp.where(mask, jnp.exp2(s_ref[h] * c2 - lse_ref[h : h + 1]), 0.0)
            p_ref[h] = p.astype(bf16)
            ds_ref[h] = (p * (dp_ref[h] - d_ref[h : h + 1])).astype(bf16)
        for h in range(heads):
            dv_ref[h, at, :] += dot(p_ref[h], do3_ref[h])
            dk_ref[h, at, :] += dot(ds_ref[h], q_ref[h])
            part = slice(h * hd, (h + 1) * hd)
            dqt_ref[part, :] += dot(kt_ref[h, :hd, at], ds_ref[h])
        return carry

    lax.fori_loop(first_ref[i], i + 1, step, 0)
    ct = cost_ref[...]
    st = sint_ref[...]
    for h in range(heads):
        a = dqt_ref[h * hd : h * hd + half, :] * scale
        b = dqt_ref[h * hd + half : (h + 1) * hd, :] * scale
        dqt_ref[h * hd : h * hd + half, :] = a * ct + b * st
        dqt_ref[h * hd + half : (h + 1) * hd, :] = b * ct - a * st
    g_ref[0] = dqt_ref[...].T.astype(bf16)
    at = pl.ds(pl.multiple_of(i * blk, blk), blk)
    cos, sin = cos_ref[...], sin_ref[...]
    lane = lax.broadcasted_iota(jnp.int32, (blk, lanes), 1)
    for h in range(heads):
        x = dk_ref[h, at, :] * scale
        other = jnp.where(lane < half, pltpu.roll(x, lanes - half, 1), -pltpu.roll(x, half, 1))
        g_ref[1, :, h * hd : (h + 1) * hd] = (x * cos + other * sin).astype(bf16)[:, :hd]
        g_ref[2, :, h * hd : (h + 1) * hd] = dv_ref[h, at, :].astype(bf16)[:, :hd]
    total = dot(g_ref[0], w_ref[0], NT) + dot(g_ref[1], w_ref[1], NT) + dot(g_ref[2], w_ref[2], NT)
    wide_ref[...] = total
    for n in range(outs):

        @pl.when((i - base) // (count // outs) == n)
        def _():
            narrow[n][...] = total.astype(bf16)
    if base:

        @pl.when(step_at == count - 1)
        def _():
            carry_out[0][...] = dk_ref[:, : base * blk, :]
            carry_out[1][...] = dv_ref[:, : base * blk, :]


def attention_backward(first, low, high, q3, k3, v3, kt, start_row, lse, attended, grad_att, tables, attn_in, hd, scale, carry, outs=1, wait=(), blk=BLK):
    heads, rows, lanes = k3.shape
    base, count = low // blk, (high - low) // blk
    cos, sin, cost, sint = tables
    pad_heads = max(8, heads)
    half = hd // 2
    here = lambda i: count - 1 - i
    there = lambda i: base + count - 1 - i
    carried = carry is not None
    before = jax.ShapeDtypeStruct((heads, low, lanes), f32)
    return pl.pallas_call(
        functools.partial(attention_backward_kernel, base=base, count=count, blk=blk, hd=hd, scale=scale, carried=carried, waits=len(wait), outs=outs),
        grid_spec=pltpu.PrefetchScalarGridSpec(
            num_scalar_prefetch=1,
            grid=(count,),
            in_specs=[
                pl.BlockSpec((heads, blk, lanes), lambda i, t: (0, there(i), 0)),
                pl.BlockSpec((heads, high, lanes), lambda i, t: (0, 0, 0), **ONE),
                pl.BlockSpec((heads, high, lanes), lambda i, t: (0, 0, 0), **ONE),
                pl.BlockSpec((heads, lanes, high), lambda i, t: (0, 0, 0), **ONE),
                pl.BlockSpec((1, 1, blk), lambda i, t: (there(i), 0, 0)),
                pl.BlockSpec((heads, blk), lambda i, t: (0, here(i))),
                pl.BlockSpec((blk, heads * hd), lambda i, t: (here(i), 0)),
                pl.BlockSpec((blk, heads * hd), lambda i, t: (here(i), 0)),
                pl.BlockSpec((blk, lanes), lambda i, t: (there(i), 0)),
                pl.BlockSpec((blk, lanes), lambda i, t: (there(i), 0)),
                pl.BlockSpec((half, blk), lambda i, t: (0, there(i))),
                pl.BlockSpec((half, blk), lambda i, t: (0, there(i))),
                pl.BlockSpec(attn_in.shape, lambda i, t: (0, 0, 0), **ONE),
            ]
            + [pl.BlockSpec((heads, high, lanes), lambda i, t: (0, 0, 0), **ONE)] * (2 if carried else 0)
            + [ANY] * len(wait),
            out_specs=[pl.BlockSpec((3, blk, heads * hd), lambda i, t: (0, here(i), 0))]
            + [pl.BlockSpec((blk, attn_in.shape[1]), lambda i, t: (here(i), 0))]
            + [
                pl.BlockSpec((blk, attn_in.shape[1]), lambda i, t, k=k, n=count // outs: (jnp.clip(here(i) - k * n, 0, n - 1), 0))
                for k in range(outs)
            ]
            + [pl.BlockSpec((heads, low, lanes), lambda i, t: (0, 0, 0), **ONE)] * (2 if base else 0),
            scratch_shapes=[
                pltpu.VMEM((heads, blk, lanes), bf16),
                pltpu.VMEM((heads, high, lanes), f32),
                pltpu.VMEM((heads, high, lanes), f32),
                pltpu.VMEM((heads * hd, blk), f32),
                pltpu.VMEM((pad_heads, blk), f32),
                pltpu.VMEM((heads, blk, blk), f32),
                pltpu.VMEM((heads, blk, blk), f32),
                pltpu.VMEM((heads, blk, blk), bf16),
                pltpu.VMEM((heads, blk, blk), bf16),
            ],
        ),
        out_shape=[
            jax.ShapeDtypeStruct((3, count * blk, heads * hd), bf16),
            jax.ShapeDtypeStruct((count * blk, attn_in.shape[1]), f32),
        ]
        + [jax.ShapeDtypeStruct((count * blk // outs, attn_in.shape[1]), bf16)] * outs
        + [before] * (2 if base else 0),
        compiler_params=params(60),
        cost_estimate=taking(10 * count),
        name="attention_backward",
    )(first, q3, k3, v3, kt, start_row, lse, attended, grad_att, cos, sin, cost, sint, attn_in, *(carry if carried else ()), *wait)


def mix_kernel(me_ref, own_ref, gain_ref, *refs, base, own_blocks, others, parts, pieces, per):
    other, refs = refs[:others], refs[others:]
    attended, refs = refs[: parts * pieces], refs[parts * pieces :]
    weights = refs[:parts]
    middle_ref, normed_ref = refs[-2:]
    i = pl.program_id(0)
    mine = (base + i) // own_blocks == me_ref[0]
    x = own_ref[...].astype(f32)
    if others:
        x = jnp.where(mine, x, chosen((base + i) % own_blocks, other, own_blocks // others).astype(f32))
    for n in range(parts):
        x = x + dot(chosen(i, attended[n * pieces : (n + 1) * pieces], per), weights[n][...])
    middle_ref[...] = x
    inverse = lax.rsqrt(jnp.mean(x * x, axis=-1, keepdims=True) + EPSILON)
    normed_ref[...] = (x * inverse * gain_ref[...]).astype(bf16)


def mix(me, low, bucket_rows, own_x, other_x, gain_row, attended, weights, before=None, wait=(), blk=BLK):
    own_rows, dim = own_x.shape
    own_blocks = own_rows // blk
    parts, pieces = len(attended), len(attended[0])
    per = attended[0][0].shape[0] // blk
    base, count = low // blk, pieces * per
    extra = () if before is None else tuple(before)
    at_x = lambda i, m: ((base + i) % own_blocks, 0)
    at = lambda i, m: (base + i, 0)
    return pl.pallas_call(
        functools.partial(
            mix_kernel, base=base, own_blocks=own_blocks, others=len(other_x), parts=parts, pieces=pieces, per=per
        ),
        grid_spec=pltpu.PrefetchScalarGridSpec(
            num_scalar_prefetch=1,
            grid=(count,),
            in_specs=[
                pl.BlockSpec((blk, dim), at_x),
                pl.BlockSpec((1, dim), lambda i, m: (0, 0)),
            ]
            + [
                pl.BlockSpec((blk, dim), lambda i, m, k=k, n=own_blocks // len(other_x): (jnp.clip((base + i) % own_blocks - k * n, 0, n - 1), 0))
                for k in range(len(other_x))
            ]
            + [
                pl.BlockSpec((blk, a.shape[1]), lambda i, m, k=k: (jnp.clip(i - k * per, 0, per - 1), 0))
                for part in attended
                for k, a in enumerate(part)
            ]
            + [pl.BlockSpec(w.shape, lambda i, m: (0, 0), **ONE) for w in weights]
            + [ANY] * (len(extra) + len(wait)),
            out_specs=[pl.BlockSpec((blk, dim), at)] * 2,
        ),
        out_shape=[jax.ShapeDtypeStruct((bucket_rows, dim), f32), jax.ShapeDtypeStruct((bucket_rows, dim), bf16)],
        input_output_aliases={3 + len(other_x) + parts * (pieces + 1) + n: n for n in range(len(extra))},
        compiler_params=params(48),
        name="mix",
    )(scalar(me), own_x, gain_row[None, :], *other_x, *[a for part in attended for a in part], *weights, *extra, *wait)


def ff_forward_kernel(base_ref, x_ref, wg_ref, wu_ref, *refs, rc):
    g_ref, u_ref, act_ref = refs[-3:]

    for low in range(0, x_ref.shape[0], rc):
        at = slice(low, low + rc)
        x = x_ref[at, :]
        g = dot(x, wg_ref[...])
        u = dot(x, wu_ref[...])
        g_ref[at, :] = g
        u_ref[at, :] = u
        act_ref[at, :] = (g * (1.0 / (1.0 + jnp.exp(-g))) * u).astype(bf16)


def ff_forward(x, base, rows, mlp_in, wait=(), hb=512, rc=512):
    dim = x.shape[1]
    hidden = mlp_in.shape[2]
    hb = block_of(hidden, hb)
    rc = block_of(rows, rc)
    return pl.pallas_call(
        functools.partial(ff_forward_kernel, rc=rc),
        grid_spec=pltpu.PrefetchScalarGridSpec(
            num_scalar_prefetch=1,
            grid=(hidden // hb,),
            in_specs=[
                pl.BlockSpec((rows, dim), lambda h, b: (b[0], 0), **ONE),
                pl.BlockSpec((None, dim, hb), lambda h, b: (0, 0, h)),
                pl.BlockSpec((None, dim, hb), lambda h, b: (1, 0, h)),
            ]
            + [ANY] * len(wait),
            out_specs=[pl.BlockSpec((rows, hb), lambda h, b: (0, h))] * 3,
        ),
        out_shape=[jax.ShapeDtypeStruct((rows, hidden), f32)] * 2 + [jax.ShapeDtypeStruct((rows, hidden), bf16)],
        compiler_params=params(60),
        cost_estimate=taking(19),
        name="ff_forward",
    )(scalar(base), x, mlp_in, mlp_in, *wait)


def ff_output_kernel(me_ref, act_ref, w_ref, *refs, pieces, per, whole, outs):
    i = pl.program_id(0)
    total = dot(act_ref[...], w_ref[...])
    if whole:
        total = total + refs[0][...] + chosen(i, refs[1 : 1 + pieces], per).astype(f32)
    for n in range(outs):

        @pl.when(i // (pl.num_programs(0) // outs) == n)
        def _():
            refs[n - outs][...] = total.astype(bf16)


def ff_output(me, act, low, high, mlp_out, middle=None, got=(), wait=(), outs=1, blk=BLK):
    hidden, dim = mlp_out.shape
    base, count = low // blk, (high - low) // blk
    whole = middle is not None
    per = got[0].shape[0] // blk if got else 1
    return pl.pallas_call(
        functools.partial(ff_output_kernel, pieces=len(got), per=per, whole=whole, outs=outs),
        grid_spec=pltpu.PrefetchScalarGridSpec(
            num_scalar_prefetch=1,
            grid=(count,),
            in_specs=[pl.BlockSpec((blk, hidden), lambda i, m: (base + i, 0)), pl.BlockSpec((hidden, dim), lambda i, m: (0, 0), **ONE)]
            + [pl.BlockSpec((blk, dim), lambda i, m: (m[0] * count + i, 0))] * (1 if whole else 0)
            + in_turn(len(got), per, blk, dim)
            + [ANY] * len(wait),
            out_specs=in_turn(outs, count // outs, blk, dim),
        ),
        out_shape=[jax.ShapeDtypeStruct(((high - low) // outs, dim), bf16)] * outs,
        compiler_params=params(48),
        cost_estimate=taking(1.8 * count),
        name="ff_output",
    )(scalar(me), act, mlp_out, *((middle,) if whole else ()), *got, *wait)


def ff_backward_kernel(*refs, rc, pieces, outs):
    og, refs = refs[:pieces], refs[pieces:]
    g_ref, u_ref, wg_ref, wu_ref, wo_ref = refs[:5]
    gn, (gg_ref, gu_ref, acc_ref) = refs[-3 - outs : -3], refs[-3:]
    rows = acc_ref.shape[0]

    @pl.when(pl.program_id(0) == 0)
    def _():
        acc_ref[...] = jnp.zeros_like(acc_ref)

    def by_rows(og_ref, low, r):
        here = slice(r * rc, (r + 1) * rc)
        at = slice(low + r * rc, low + (r + 1) * rc)
        ga = dot(og_ref[here, :], wo_ref[...], NT)
        g = g_ref[at, :]
        s = 1.0 / (1.0 + jnp.exp(-g))
        silu = g * s
        gg = (ga * u_ref[at, :] * (s * (1.0 + g * (1.0 - s)))).astype(bf16)
        gu = (ga * silu).astype(bf16)
        gg_ref[at, :] = gg
        gu_ref[at, :] = gu
        acc_ref[at, :] += dot(gg, wg_ref[...], NT) + dot(gu, wu_ref[...], NT)

    low = 0
    for og_ref in og:
        count = og_ref.shape[0] // rc
        for r in range(count):
            by_rows(og_ref, low, r)
        low += og_ref.shape[0]

    @pl.when(pl.program_id(0) == pl.num_programs(0) - 1)
    def _():
        for n, out in enumerate(gn):
            out[...] = acc_ref[n * out.shape[0] : (n + 1) * out.shape[0], :].astype(out.dtype)


def ff_backward(og, g, u, mlp_in, mlp_out, dtype, outs=1, wait=(), hb=512, rc=512):
    rows, hidden = g.shape
    dim = mlp_out.shape[1]
    hb = block_of(hidden, hb)
    rc = block_of(og[0].shape[0], rc)
    return pl.pallas_call(
        functools.partial(ff_backward_kernel, rc=rc, pieces=len(og), outs=outs),
        grid=(hidden // hb,),
        in_specs=[pl.BlockSpec(a.shape, lambda h: (0, 0), **ONE) for a in og]
        + [
            pl.BlockSpec((rows, hb), lambda h: (0, h)),
            pl.BlockSpec((rows, hb), lambda h: (0, h)),
            pl.BlockSpec((None, dim, hb), lambda h: (0, 0, h)),
            pl.BlockSpec((None, dim, hb), lambda h: (1, 0, h)),
            pl.BlockSpec((hb, dim), lambda h: (h, 0)),
        ]
        + [ANY] * len(wait),
        out_specs=[pl.BlockSpec((rows // outs, dim), lambda h: (0, 0), **ONE)] * outs + [pl.BlockSpec((rows, hb), lambda h: (0, h))] * 2,
        scratch_shapes=[pltpu.VMEM((rows, dim), f32)],
        out_shape=[jax.ShapeDtypeStruct((rows // outs, dim), dtype)] * outs + [jax.ShapeDtypeStruct((rows, hidden), bf16)] * 2,
        compiler_params=params(60),
        cost_estimate=taking(33),
        name="ff_backward",
    )(*og, g, u, mlp_in, mlp_in, mlp_out, *wait)


def store_split(total, first, share, side, keep_ref, send_ref):
    for n in range(0, total.shape[0] // share, 2):
        even = total[n * share : (n + 1) * share]
        odd = total[(n + 1) * share : (n + 2) * share]
        at = slice((first // share + n) // 2 * share, ((first // share + n) // 2 + 1) * share)
        keep_ref[at, :] = jnp.where(side == 0, even, odd).astype(bf16)
        send_ref[at, :] = jnp.where(side == 0, odd, even).astype(bf16)


def weights_kernel(base_ref, *refs, pieces, outs, share, cc):
    lhs, rhs, out = refs[:pieces], refs[pieces : 2 * pieces], refs[-outs:]
    dim = lhs[0].shape[1]

    def product(at):
        total = None
        for x_ref, r_ref in zip(lhs, rhs):
            part = dot(x_ref[:, at], r_ref[...], TN)
            total = part if total is None else total + part
        return total

    if outs == 2:
        for first in range(0, dim, cc):
            store_split(product(slice(first, first + cc)), first, share, base_ref[1], *out)
        return

    def by_columns(t, c):
        at = pl.ds(pl.multiple_of(t * cc, cc), cc)
        out[0][at, :] = product(at).astype(bf16)
        return c

    lax.fori_loop(0, dim // cc, by_columns, 0)


def weight_gradient(base, terms, side=None, share=None, wait=(), hb=512, cc=640):
    dim = terms[0][0].shape[1]
    columns = terms[0][2].shape[1]
    hb = block_of(columns, hb)
    outs = 1 if side is None else 2
    table = jnp.stack([jnp.asarray(base, jnp.int32), jnp.asarray(0 if side is None else side, jnp.int32)])
    return pl.pallas_call(
        functools.partial(weights_kernel, pieces=len(terms), outs=outs, share=share, cc=cc),
        grid_spec=pltpu.PrefetchScalarGridSpec(
            num_scalar_prefetch=1,
            grid=(columns // hb,),
            in_specs=[pl.BlockSpec((n, dim), lambda h, b, m=m: (m(b[0]), 0), **ONE) for _, m, _, _, n in terms]
            + [pl.BlockSpec((n, hb), lambda h, b, k=k: (k, h)) for _, _, _, k, n in terms]
            + [ANY] * len(wait),
            out_specs=[pl.BlockSpec((dim // outs, hb), lambda h, b: (0, h))] * outs,
        ),
        out_shape=[jax.ShapeDtypeStruct((dim // outs, columns), bf16)] * outs,
        compiler_params=params(60),
        cost_estimate=taking(20),
        name="weight_gradient",
    )(table, *[t[0] for t in terms], *[t[2] for t in terms], *wait)


def attn_weights_kernel(side_ref, n_ref, *refs, lows, outs, share, cc):
    parts, out = refs[: len(lows)], refs[-outs:]

    def product(at):
        total = None
        for low, g_ref in zip(lows, parts):
            part = dot(n_ref[low : low + g_ref.shape[0], at], g_ref[...], TN)
            total = part if total is None else total + part
        return total

    for first in range(0, n_ref.shape[1], cc):
        at = slice(first, first + cc)
        if outs == 2:
            store_split(product(at), first, share, side_ref[0], *out)
        else:
            out[0][at, :] = product(at).astype(bf16)


def attn_weight_gradient(normed_one, lows, grad_qkv, side=None, share=None, wait=(), cc=640):
    rows, dim = normed_one.shape
    cols = grad_qkv[0].shape[2]
    outs = 1 if side is None else 2
    flat = cols % LANES == 0
    spec = pl.BlockSpec((dim // outs, cols), lambda j, s: (0, j)) if flat else pl.BlockSpec((None, dim, cols), lambda j, s: (j, 0, 0))
    shape = (dim // outs, 3 * cols) if flat else (3, dim, cols)
    return pl.pallas_call(
        functools.partial(attn_weights_kernel, lows=lows, outs=outs, share=share, cc=cc),
        grid_spec=pltpu.PrefetchScalarGridSpec(
            num_scalar_prefetch=1,
            grid=(3,),
            in_specs=[pl.BlockSpec((rows, dim), lambda j, s: (0, 0), **ONE)]
            + [pl.BlockSpec((None, g.shape[1], cols), lambda j, s: (j, 0, 0)) for g in grad_qkv]
            + [ANY] * len(wait),
            out_specs=[spec] * outs,
        ),
        out_shape=[jax.ShapeDtypeStruct(shape, bf16)] * outs,
        compiler_params=params(56),
        cost_estimate=taking(18),
        name="attn_weight_gradient",
    )(scalar(0 if side is None else side), normed_one, *grad_qkv, *wait)


def norm_input_part(z, gain, e):
    inverse = lax.rsqrt(jnp.mean(z * z, axis=-1, keepdims=True) + EPSILON)
    weighted = e * gain
    inner = jnp.mean(weighted * z, axis=-1, keepdims=True)
    return weighted * inverse - z * (inverse * inverse * inverse) * inner


def middle_backward_kernel(me_ref, og_ref, z_ref, own_ref, gain_ref, *refs, pieces, per, parts):
    got, refs = refs[:pieces], refs[pieces:]
    weights, refs = refs[:parts], refs[-2 - parts :]
    i = pl.program_id(0)
    e = own_ref[...]
    if pieces:
        e = e + chosen(i, got, per).astype(f32)
    grad = og_ref[...].astype(f32) + norm_input_part(z_ref[...], gain_ref[...], e)
    refs[0][...] = grad
    branch = grad.astype(bf16)
    refs[1][...] = branch
    for w, out in zip(weights, refs[2:]):
        out[...] = dot(branch, w[...], NT).astype(bf16)


def middle_backward(me, out_grad, middle, gn_own, got_gn, gain_row, weights, wait=(), blk=BLK):
    rows, dim = out_grad.shape
    pieces = len(got_gn)
    per = got_gn[0].shape[0] // blk if pieces else 1
    own_blocks = rows // blk
    at = lambda i, m: (i, 0)
    return pl.pallas_call(
        functools.partial(middle_backward_kernel, pieces=pieces, per=per, parts=len(weights)),
        grid_spec=pltpu.PrefetchScalarGridSpec(
            num_scalar_prefetch=1,
            grid=(own_blocks,),
            in_specs=[
                pl.BlockSpec((blk, dim), at),
                pl.BlockSpec((blk, dim), lambda i, m: (m[0] * own_blocks + i, 0)),
                pl.BlockSpec((blk, dim), at),
                pl.BlockSpec((1, dim), lambda i, m: (0, 0)),
            ]
            + in_turn(pieces, per, blk, dim)
            + [pl.BlockSpec(w.shape, lambda i, m: (0, 0), **ONE) for w in weights]
            + [ANY] * len(wait),
            out_specs=[pl.BlockSpec((blk, dim), at)] * 2 + [pl.BlockSpec((blk, w.shape[0]), at) for w in weights],
        ),
        out_shape=[jax.ShapeDtypeStruct((rows, dim), f32), jax.ShapeDtypeStruct((rows, dim), bf16)]
        + [jax.ShapeDtypeStruct((rows, w.shape[0]), bf16) for w in weights],
        compiler_params=params(48),
        cost_estimate=taking(12),
        name="middle_backward",
    )(scalar(me), out_grad, middle, gn_own, gain_row[None, :], *got_gn, *weights, *wait)


def tokens_backward_kernel(me_ref, x_ref, grad_ref, gain_ref, *refs, sides):
    i = pl.program_id(0)
    out_ref, refs = refs[-1], refs[:-1]
    e = None
    for n, ((count, each), (more, every)) in enumerate(sides):
        own, got, refs = refs[:count], refs[count : count + more], refs[count + more :]
        here = chosen(i, own, each) + chosen(i, got, every).astype(f32)
        e = here if e is None else jnp.where(me_ref[0] == n, here, e)
    out_ref[...] = (grad_ref[...] + norm_input_part(x_ref[...].astype(f32), gain_ref[...], e)).astype(bf16)


def tokens_backward(me, tokens, grad_middle, gain_row, sides, wait=(), blk=BLK):
    rows, dim = tokens.shape
    at = lambda i, m: (i, 0)
    shape = tuple(tuple((len(part), part[0].shape[0] // blk) for part in side) for side in sides)
    specs = [spec for side in shape for part in side for spec in in_turn(*part, blk, dim)]
    return pl.pallas_call(
        functools.partial(tokens_backward_kernel, sides=shape),
        grid_spec=pltpu.PrefetchScalarGridSpec(
            num_scalar_prefetch=1,
            grid=(rows // blk,),
            in_specs=[pl.BlockSpec((blk, dim), at), pl.BlockSpec((blk, dim), at), pl.BlockSpec((1, dim), lambda i, m: (0, 0))] + specs
            + [ANY] * len(wait),
            out_specs=pl.BlockSpec((blk, dim), at),
        ),
        out_shape=jax.ShapeDtypeStruct((rows, dim), bf16),
        compiler_params=params(48),
        cost_estimate=taking(10),
        name="tokens_backward",
    )(scalar(me), tokens, grad_middle, gain_row[None, :], *[a for own, got in sides for a in (*own, *got)], *wait)


def contract(a, b, dims):
    return lax.dot_general(a, b, (dims, ((), ())), preferred_element_type=f32)


def after(value, *others):
    return lax.optimization_barrier((value, *others))[0]


SWAP = ((0, 1), (1, 0))


def halving_step(state, group, n_dp, behind):
    bit, send, keep = state
    got = lax.ppermute(send, "dp", [(n, n ^ (1 << bit)) for n in range(n_dp)])
    keep, behind = lax.optimization_barrier((keep, behind))
    if n_dp >> bit == 2:
        return (bit + 1, got, keep), behind
    split = lambda a: a.reshape(n_dp >> (bit + 2), 2, -1, a.shape[-1])
    side = (group >> (bit + 1)) & 1

    def pick(at):
        parts = [lax.dynamic_index_in_dim(split(a), at, 1, False).astype(f32) for a in (keep, got)]
        return (parts[0] + parts[1]).astype(bf16).reshape(-1, keep.shape[-1])

    return (bit + 1, pick(1 - side), pick(side)), behind


def halving_in_orders(got, keep, group, n_dp, orders, beside):
    partner = lambda a, bit: lax.ppermute(a, "dp", [(n, n ^ (1 << bit)) for n in range(n_dp)])
    share = keep.shape[0] * 2 // n_dp
    states, low, made = [], 0, []
    for width, bits in orders:
        states.append((keep[:, low : low + width], got[:, low : low + width], sorted(bits, reverse=True)))
        low += width
    for step in range(len(orders[0][1])):
        sent = []
        for n, (width, bits) in enumerate(orders):
            kept, came, left = states[n]
            axis = left.index(bits[step])
            view = lambda a: a.reshape((2,) * len(left) + (share, width))

            def pick(at):
                parts = [lax.dynamic_index_in_dim(view(a), at, axis, False).astype(f32) for a in (kept, came)]
                return (parts[0] + parts[1]).astype(bf16).reshape(-1, width)

            own = (group >> bits[step]) & 1
            sent.append(pick(1 - own))
            states[n] = (pick(own), partner(sent[-1], bits[step]), [b for b in left if b != bits[step]])
        if step < len(beside):
            made.append(beside[step](tuple(sent)))
            for n, (kept, came, left) in enumerate(states):
                kept, made[-1] = lax.optimization_barrier((kept, made[-1]))
                states[n] = (kept, came, left)
    return jnp.concatenate([kept.astype(f32) + came.astype(f32) for kept, came, _ in states], axis=1), made


def halving_end(state):
    _, got, keep = state
    return keep.astype(f32) + got.astype(f32)


def per_device(tokens, norm_gains, attn_in, attn_out, mlp_in, mlp_out, lengths, out_grad):
    n_mp = lax.axis_size("mp")
    n_dp = lax.axis_size("dp")
    me = lax.axis_index("mp")
    group = lax.axis_index("dp")
    rows, dim = tokens.shape
    bucket = rows * n_mp
    hd = HEAD_DIM
    cols = attn_out.shape[0]
    hidden = mlp_out.shape[0]
    share = dim // n_dp
    scale = hd**-0.5
    pair = n_mp == 2
    hb = block_of(hidden, 512)
    places, starts = layout(lengths[0], bucket)
    tables = turning(places - starts, hd)
    cos, sin = tables[:2]
    first = starts[::BLK] // BLK
    start_row = starts.reshape(bucket // BLK, 1, BLK)
    own_blocks = rows // BLK

    def mine(array, axis, size):
        return lax.dynamic_slice_in_dim(array, group * size, size, axis)

    def swap(array):
        return lax.ppermute(array, "mp", SWAP)

    def scatter(array):
        return lax.psum_scatter(array, "dp", scatter_dimension=0, tiled=True)

    chunk = rows // 2
    halves = (0, chunk)
    whole = lambda b: 0
    if pair:
        piece, lower = lax.optimization_barrier((mine(attn_out, 0, cols // n_dp), tokens[:chunk]))
        other_x = [swap(lower), swap(tokens[chunk:])]
        piece = swap(piece)
        other_attn_out = lax.all_gather(piece, "dp", axis=0, tiled=True)
        projected = project(tokens, me * own_blocks, bucket, norm_gains[0], attn_in, cos, sin, hd, wait=(piece,))
        att, lse, att_got = [], [], []
        for n, low in enumerate(range(0, bucket, chunk)):
            if n < 2:
                projected = project(
                    other_x[n], (1 - me) * own_blocks + n * own_blocks // 2, bucket, norm_gains[0], attn_in, cos, sin, hd,
                    projected, wait=tuple(att),
                )
            normed_one, q3, k3, v3, kt, vt = projected
            wait = tuple(att_got[n - 2 : n - 1]) if n > 1 else ()
            if n == 1:
                wait = (other_attn_out,)
            a, l = attention_forward(first, low, low + chunk, q3, k3, vt, start_row, hd, scale, tuple(att[-1:]) + wait)
            att.append(a)
            lse.append(l)
            att_got.append(swap(a))
        got_grad = [out_grad[low : low + chunk] for low in halves]
        *got_grad, att_got[2] = lax.optimization_barrier((*got_grad, att_got[2]))
        got_grad = [swap(a) for a in got_grad]
        mix_rows = lambda low, these, before: mix(
            me, low, bucket, tokens, other_x, norm_gains[1], (att[these], att_got[these]), (attn_out, other_attn_out), before
        )
        middle_all, normed_two = mix_rows(3 * chunk, slice(3, 4), mix_rows(0, slice(0, 3), None))
        other = 1 - me
        g_b, u_b, act_b = ff_forward(normed_two, other, rows, mlp_in)
        g_a, u_a, act_a = ff_forward(normed_two, me, rows, mlp_in, wait=(act_b, got_grad[0]))
        (gw_out,) = weight_gradient(
            0,
            [(got_grad[n], whole, act_b, n, chunk) for n in range(2)] + [(out_grad, whole, act_a, 0, rows)],
            wait=(act_a,),
        )
        sum_out = scatter(gw_out)
        *got_gn, gg_b, gu_b = ff_backward(got_grad, g_b, u_b, mlp_in, mlp_out, bf16, 2, wait=(gw_out,))
        got_gn = [swap(a) for a in got_gn]
        gn_a, gg_a, gu_a = ff_backward([out_grad], g_a, u_a, mlp_in, mlp_out, f32, wait=(gg_b,))
        side = lambda b, a: [(normed_two, lambda b: 1 - b, b, 0, rows), (normed_two, lambda b: b, a, 0, rows)]
        (gw_gate,) = weight_gradient(me, side(gg_b, gg_a), wait=(gn_a, got_gn[0]))
        sum_gate = scatter(gw_gate)
        grad_middle, branch_grad, do_own, do_send = middle_backward(
            me, out_grad, middle_all, gn_a, got_gn, norm_gains[1], (attn_out, other_attn_out), wait=(gw_gate, sum_out)
        )
    else:
        all_x = lax.all_gather(tokens, "mp", axis=0, tiled=True)
        normed_one, q3, k3, v3, kt, vt = project(all_x, 0, bucket, norm_gains[0], attn_in, cos, sin, hd)
        att_all, lse_all = attention_forward(first, 0, bucket, q3, k3, vt, start_row, hd, scale)
        every_head = lax.all_gather(att_all, "mp", axis=1, tiled=True)
        every_out = lax.all_gather(attn_out, "mp", axis=0, tiled=True)
        middle_all, normed_two = mix(0, 0, bucket, all_x, (), norm_gains[1], ((every_head,),), (every_out,))
        all_grad = lax.all_gather(out_grad, "mp", axis=0, tiled=True)
        g_b, u_b, act_b = ff_forward(normed_two, 0, bucket, mlp_in)
        gn_b, gg_b, gu_b = ff_backward([all_grad], g_b, u_b, mlp_in, mlp_out, bf16)
        sum_out = scatter(weight_gradient(0, [(all_grad, whole, act_b, 0, bucket)])[0])
        sum_gate = scatter(weight_gradient(0, [(normed_two, whole, gg_b, 0, bucket)])[0])
        sum_up = scatter(weight_gradient(0, [(normed_two, whole, gu_b, 0, bucket)])[0])
        grad_normed_two = lax.psum_scatter(gn_b, "mp", scatter_dimension=0, tiled=True).astype(f32)
        grad_middle, branch_grad = middle_backward(me, out_grad, middle_all, grad_normed_two, (), norm_gains[1], ())
        middle = lax.dynamic_slice_in_dim(middle_all, me * rows, rows, 0)
        (out_b,) = ff_output(0, act_b, 0, bucket, mlp_out)
        output = (middle + lax.psum_scatter(out_b, "mp", scatter_dimension=0, tiled=True).astype(f32)).astype(bf16)
    if pair:
        do_got = swap(do_send)
        up_keep, up_send = weight_gradient(me, side(gu_b, gu_a), group & 1, share, wait=(do_send,))
        up = (0, up_send, up_keep)
        out_b = ff_output(me, act_b, 0, rows, mlp_out, wait=(up_keep,), outs=2)
        att_own = jnp.where(me == 0, jnp.concatenate(att[:2]), jnp.concatenate(att[2:]))
        att_other = jnp.where(me == 0, jnp.concatenate(att_got[:2]), jnp.concatenate(att_got[2:]))
        gw_attn_out = jnp.concatenate(
            [contract(branch_grad, a, ((0,), (0,))).astype(bf16) for a in (att_own, att_other)], axis=1
        )
        up, gw_attn_out = halving_step(up, group, n_dp, gw_attn_out)
        sum_attn_out = scatter(gw_attn_out)
        got_out = [swap(a) for a in out_b]
        do_low = jnp.where(me == 0, do_own, do_got)
        do_high = jnp.where(me == 0, do_got, do_own)
        grad_att = {0: do_low[:chunk], chunk: do_low[chunk:], rows: do_high}
        lse_of = {0: lse[0], chunk: lse[1], rows: jnp.concatenate(lse[2:], axis=1)}
        att_of = {0: att[0], chunk: att[1], rows: jnp.concatenate(att[2:], axis=0)}
        carry, grad_qkv, own_part, got_part = None, {}, {}, {}
        for low, high in ((rows, bucket), (chunk, rows), (0, chunk)):
            wait = {rows: (), chunk: (sum_gate, got_out[0]), 0: (got_out[1],) + tuple(got_part.get(rows, ())[:1])}[low]
            made = attention_backward(
                first, low, high, q3, k3, v3, kt, start_row, lse_of[low], att_of[low], grad_att[low], tables, attn_in, hd, scale,
                carry, (high - low) // chunk, wait + (up[1],),
            )
            send = made[2 : 2 + (high - low) // chunk]
            own_part[low], carry = made[1], made[2 + len(send) :]
            up, grad_qkv[low] = halving_step(up, group, n_dp, made[0])
            path = ((0, 1),) if low == rows else ((1, 0),)
            got_part[low] = [lax.ppermute(a, "mp", path) for a in send]
        lows = (0, chunk, rows)
        in_keep, in_send = attn_weight_gradient(
            normed_one, lows, [grad_qkv[low] for low in lows], group & 1, share, wait=(sum_attn_out, got_part[rows][1], got_part[chunk][0], up[1])
        )
        bits = tuple(range(1, n_dp.bit_length() - 1))
        width = (3 * cols // 2 + LANES - 1) // LANES * LANES
        in_got = lax.ppermute(in_send, "dp", [(n, n ^ 1) for n in range(n_dp)])
        finish_output = lambda sent: ff_output(me, act_a, 0, rows, mlp_out, middle_all, got_out, wait=sent)[0]
        finish_tokens = lambda sent: tokens_backward(
            me,
            tokens,
            grad_middle,
            norm_gains[0],
            (([own_part[0], own_part[chunk]], got_part[0] + got_part[chunk]), ([own_part[rows]], got_part[rows])),
            wait=sent,
        )
        sum_attn_in, (output, grad_tokens) = halving_in_orders(
            in_got, in_keep, group, n_dp, ((width, bits), (3 * cols - width, bits[1:] + bits[:1])), (finish_output, finish_tokens)
        )
        sum_up = halving_end(up)
    else:
        all_branch = lax.all_gather(branch_grad, "mp", axis=0, tiled=True)
        grad_heads = contract(all_branch, attn_out, ((1,), (1,))).astype(bf16)
        gw_attn_out = contract(all_branch, att_all, ((0,), (0,))).astype(bf16)
        made = attention_backward(
            first, 0, bucket, q3, k3, v3, kt, start_row, lse_all, att_all, grad_heads, tables, attn_in, hd, scale, None
        )
        grad_qkv, grad_normed_one = made[0], lax.psum_scatter(made[2], "mp", scatter_dimension=0, tiled=True)
        nothing = jnp.zeros((rows, dim), f32)
        grad_tokens = tokens_backward(0, tokens, grad_middle, norm_gains[0], (((nothing,), (grad_normed_one,)),))
        (gw_attn_in,) = attn_weight_gradient(normed_one, (0,), [grad_qkv])
        if gw_attn_in.ndim == 3:
            gw_attn_in = gw_attn_in.transpose(1, 0, 2).reshape(dim, 3 * cols)
        sum_attn_in = scatter(gw_attn_in).astype(f32)
    sum_in = jnp.stack([sum_gate.astype(f32), sum_up.astype(f32)])
    sum_out = sum_out.astype(f32)
    if not pair:
        sum_attn_out = scatter(gw_attn_out)
    sum_attn_out = sum_attn_out.astype(f32)
    if pair:
        sum_attn_out = sum_attn_out[:, :cols] + swap(sum_attn_out[:, cols:].astype(bf16)).astype(f32)
    sum_attn_in = sum_attn_in.reshape(share, 3, cols).transpose(1, 0, 2)
    gain_one = jnp.sum(mine(attn_in, 1, share).astype(f32) * sum_attn_in, axis=(0, 2))
    gain_two = jnp.sum(mine(mlp_in, 1, share).astype(f32) * sum_in, axis=(0, 2))
    gains = jnp.stack([gain_one, gain_two]) / mine(norm_gains, 1, share)
    if pair:
        halves = gains.reshape(2, 2, share // 2)
        gains = lax.dynamic_index_in_dim(halves, me, 1, False) + swap(lax.dynamic_index_in_dim(halves, 1 - me, 1, False))
    else:
        gains = lax.psum_scatter(gains, "mp", scatter_dimension=1, tiled=True)
    return (output, grad_tokens, gains, sum_attn_in, sum_attn_out.T, sum_in, sum_out.T)


def solution(mesh):
    placed = (
        P(("dp", "mp"), None),
        P(),
        P(None, None, "mp"),
        P("mp", None),
        P(None, None, "mp"),
        P("mp", None),
        P("dp", None),
        P(("dp", "mp"), None),
    )
    return jax.shard_map(
        per_device,
        mesh=mesh,
        in_specs=placed,
        out_specs=(
            P(("dp", "mp"), None),
            P(("dp", "mp"), None),
            P(None, ("dp", "mp")),
            P(None, "dp", "mp"),
            P("mp", "dp"),
            P(None, "dp", "mp"),
            P("mp", "dp"),
        ),
        check_vma=False,
    )
```
